128 devices in a mesh: req: 16 (over x, z), tp: 8 (over y, core).
Axes of the slice: x: 4, y: 4, z: 4, core: 2. Of those that a mesh axis runs over, the one named last changes fastest.
Arguments:
- hidden: bfloat16 [8192, 2048], P('req', 'tp'), may hold values from -6 to 6
- qkv_weight: bfloat16 [2048, 3072], P('req', 'tp'), may hold values from -0.125 to 0.125
- out_weight: bfloat16 [2048, 2048], P('tp', 'req'), may hold values from -0.125 to 0.125
- kv_pages: bfloat16 [1024, 128, 1024], P('req', None, 'tp'), may hold values from -160 to 160, as said below
- cache_pages: int32 [16], replicated, may hold values from 1 to 256, 960 in all
- slot_order: int32 [1024], replicated, may hold values from 0 to 1023, each once
Outputs:
- attention_out: bfloat16 [8192, 2048], P('req', 'tp')
- pages_out: bfloat16 [1024, 128, 1024], P('req', None, 'tp')
The draws below stay inside these ranges and needn't reach their ends.
Inputs may be any that keep to these rules, and one draw needn't show every extreme that they name: `cache_pages`: each request has at least one cached page and at most 256, and one request has exactly 256; all cached pages plus 4 new pages per request fill exactly 1024 slots. `slot_order`: each global slot appears once. `kv_pages`: cached rotated keys and values.
All inputs are finite; a program needn't handle non-finite values.
Results may differ from the reference program's by a relative error of at most 0.02.
The reference program's roundings to bfloat16 on the way count: a program that leaves them out, or rounds other values in their place, can miss the bound.
Values may be sent and summed in bfloat16 or wider, within the bound.
A program may use at most 128 MiB of HBM per device.

```python
import math
import jax
import jax.numpy as jnp
import numpy as np
from jax import lax

D = 2048
HQ = 32
KVH = 8
HD = 64
GROUP = 4
SPAN = 512
PAGE = 128
MOST_PAGES = 256
SLOTS = 64
REQS = 16
TOKENS = 8192
TOTAL_SLOTS = 1024
OLD_PAGES = 960
N_TP = 8


def draw_kv_pages(key, part):
    page_shape = (TOTAL_SLOTS, PAGE, KVH * 2 * HD)
    values_drawn = jnp.clip(jax.random.normal(key, page_shape, jnp.float32), -6.0, 6.0)
    return values_drawn.astype(jnp.bfloat16)


def steps_of(own_key, shape, cuts, low, high):
    def one(dim, blocks):
        heights = jax.random.uniform(jax.random.fold_in(jax.random.fold_in(own_key, 6), dim), (blocks,), jnp.float32, low / len(cuts), high / len(cuts))
        return jnp.repeat(jnp.exp(heights), shape[dim] // blocks).reshape((-1,) + (1,) * (len(shape) - dim - 1))

    level = one(*cuts[0])
    for cut in cuts[1:]:
        level = level * one(*cut)
    return level


def length_profile(number_of, total, bound, skew):
    portions = [(1 << 20) // math.isqrt(standing ** skew) + 1 for standing in range(2, number_of + 1)]
    rest, given = total - bound - (number_of - 1), [1] * (number_of - 1)
    while rest > 0:
        free = [i for i in range(number_of - 1) if given[i] < bound]
        pool, remaining = sum([portions[i] for i in free]), rest
        for i in free:
            addition = min(bound - given[i], max(1, remaining * portions[i] // pool), rest)
            given[i] = given[i] + addition
            rest = rest - addition
    return np.array([bound] + given)


def ragged_sizes(stream_key, number_of, total, reach, lean):
    if number_of == 2:
        one = jax.random.randint(stream_key, (), max(1, total - reach), min(reach, total - 1) + 1)
        return jnp.stack([one, total - one])
    lengths = jnp.asarray(length_profile(number_of, total, reach, lean), jnp.int32)
    pairs = (number_of - 1) // 2
    giver, sink = lengths[1:1 + 2 * pairs:2], lengths[2:2 + 2 * pairs:2]
    margin = jnp.minimum(giver - 1, reach - sink)
    passed = jax.random.randint(jax.random.fold_in(stream_key, 1), (pairs,), 0, 1 << 20) % (margin + 1)
    lengths = lengths.at[1:1 + 2 * pairs:2].set(giver - passed).at[2:2 + 2 * pairs:2].set(sink + passed)
    return lengths[jax.random.permutation(jax.random.fold_in(stream_key, 2), number_of)]


def noise(rng, dims, width, most, shards=(), kind=jnp.bfloat16):
    values = width * jax.random.normal(rng, dims, jnp.float32)
    if shards:
        values = values * steps_of(rng, dims, shards, -0.22, 0.18)
    return jnp.clip(values, -most, most).astype(kind)


def setup_inputs(seed: int = 0) -> dict:
    key_of = jax.random.split(jax.random.key(seed), 7)
    hidden = noise(key_of[0], (TOKENS, D), 1.0, 6.0, ((0, 16), (1, 8)))
    qkv_weight = noise(key_of[1], (D, KVH * (GROUP + 2) * HD), D ** -0.5, 0.125, ((0, 16), (1, 8)))
    out_weight = noise(key_of[2], (HQ * HD, D), (HQ * HD) ** -0.5, 0.125, ((0, 8), (1, 16)))
    kv_pages = draw_kv_pages(jax.random.fold_in(key_of[6], 71), 0)
    cache_pages = ragged_sizes(key_of[4], REQS, OLD_PAGES, MOST_PAGES, 2).astype(jnp.int32)
    slot_order = jax.random.permutation(key_of[5], TOTAL_SLOTS).astype(jnp.int32)
    return dict(hidden=hidden, qkv_weight=qkv_weight, out_weight=out_weight, kv_pages=kv_pages, cache_pages=cache_pages, slot_order=slot_order)


THETA = 1000000.0
NEG_BIG = -1e+30

def rotary(values, positions):
    head_width = values.shape[-1]
    half_width = head_width // 2
    inv_freq = jnp.power(THETA, -(jnp.arange(half_width, dtype=jnp.float32) * 2.0 / head_width))
    angles = positions.astype(jnp.float32)[..., None] * inv_freq
    cosines = jnp.cos(angles)
    sines = jnp.sin(angles)
    lower_half = values[..., :half_width]
    upper_half = values[..., half_width:]
    return jnp.concatenate([lower_half * cosines - upper_half * sines, upper_half * cosines + lower_half * sines], axis=-1)

def to_columns(stat):
    return jnp.moveaxis(stat, -1, -3)[..., None]

def locate(slot_ids, cache_pages, slot_order, new_pages):
    requests = cache_pages.shape[0]
    slot_count = slot_order.shape[0]
    counts = cache_pages + new_pages
    page_ends = jnp.cumsum(counts).astype(jnp.int32)
    starts = page_ends - counts
    ranking = lax.optimization_barrier(jnp.sum(jnp.where(slot_order[None, :] == slot_ids[:, None], jnp.arange(slot_count, dtype=jnp.int32)[None, :], 0), axis=1)).astype(jnp.int32)
    holder = (lax.optimization_barrier(jnp.sum((starts[None, :] <= ranking[:, None]).astype(jnp.int32), axis=1)) - 1).astype(jnp.int32)
    onehot = jnp.arange(requests, dtype=jnp.int32)[None, :] == holder[:, None]
    first_page = lax.optimization_barrier(jnp.sum(jnp.where(onehot, starts[None, :], 0), axis=1)).astype(jnp.int32)
    cached = lax.optimization_barrier(jnp.sum(jnp.where(onehot, cache_pages[None, :], 0), axis=1)).astype(jnp.int32)
    return (holder, (ranking - first_page).astype(jnp.int32), cached)

def write_pages(kv_pages, fresh, slot_req, page_index, cached, new_pages):
    page_rows = kv_pages.shape[1]
    lane_width = kv_pages.shape[2]
    fresh_pages = fresh.reshape(-1, page_rows, lane_width)
    pick = (slot_req * new_pages + jnp.clip(page_index - cached, 0, new_pages - 1)).astype(jnp.int32)
    return jnp.where((page_index >= cached)[:, None, None], fresh_pages[pick], kv_pages)

def block_terms(queries, query_start, page_block, slot_req, key_start, is_live):
    block_slots = page_block.shape[0]
    page_rows = page_block.shape[1]
    kv_heads = queries.shape[2]
    head_width = queries.shape[4]
    span_rows = queries.shape[1]
    kv_pairs = page_block.reshape(block_slots, page_rows, kv_heads, 2, head_width)
    key_rows = kv_pairs[:, :, :, 0, :].astype(jnp.float32)
    value_rows = kv_pairs[:, :, :, 1, :].astype(jnp.float32)
    chosen = queries[slot_req].astype(jnp.float32)
    scores = jnp.einsum('bckgd,bpkd->bkgcp', chosen, key_rows) * (1.0 / math.sqrt(head_width))
    query_pos = query_start[slot_req][:, None] + jnp.arange(span_rows, dtype=jnp.int32)[None, :]
    key_pos = key_start[:, None] + jnp.arange(page_rows, dtype=jnp.int32)[None, :]
    visible = (key_pos[:, None, :] <= query_pos[:, :, None]) & is_live[:, None, None]
    visible = visible[:, None, None, :, :]
    masked = jnp.where(visible, scores, NEG_BIG)
    block_max = lax.optimization_barrier(jnp.max(masked, axis=-1))
    exp_terms = jnp.where(visible, jnp.exp(masked - block_max[..., None]), 0.0)
    block_sum = lax.optimization_barrier(jnp.sum(exp_terms, axis=-1))
    weights = lax.optimization_barrier(exp_terms.astype(jnp.bfloat16)).astype(jnp.float32)
    block_out = jnp.einsum('bkgcp,bpkd->bckgd', weights, value_rows)
    return (block_out, block_max, block_sum)

def fold(running, terms, slot_req):
    acc_out, acc_max, acc_sum = running
    block_out, block_max, block_sum = terms
    for j in range(block_out.shape[0]):
        target = slot_req[j]
        old_max = lax.dynamic_index_in_dim(acc_max, target, 0, keepdims=False)
        new_max = jnp.maximum(old_max, block_max[j])
        keep_old = jnp.exp(old_max - new_max)
        take_new = jnp.exp(block_max[j] - new_max)
        old_out = lax.dynamic_index_in_dim(acc_out, target, 0, keepdims=False)
        old_sum = lax.dynamic_index_in_dim(acc_sum, target, 0, keepdims=False)
        acc_out = lax.dynamic_update_index_in_dim(acc_out, old_out * to_columns(keep_old) + block_out[j] * to_columns(take_new), target, 0)
        acc_sum = lax.dynamic_update_index_in_dim(acc_sum, old_sum * keep_old + block_sum[j] * take_new, target, 0)
        acc_max = lax.dynamic_update_index_in_dim(acc_max, new_max, target, 0)
    return (acc_out, acc_max, acc_sum)

def init_state(requests, span_rows, kv_heads, group_size, head_width):
    return (jnp.zeros((requests, span_rows, kv_heads, group_size, head_width), jnp.float32), jnp.full((requests, kv_heads, group_size, span_rows), NEG_BIG, jnp.float32), jnp.zeros((requests, kv_heads, group_size, span_rows), jnp.float32))

def reference(hidden, qkv_weight, out_weight, kv_pages, cache_pages, slot_order):
    new_pages = SPAN // PAGE
    projected = jnp.dot(hidden, qkv_weight, preferred_element_type=jnp.float32).reshape(REQS, SPAN, KVH, GROUP + 2, HD)
    query_start = (cache_pages * PAGE).astype(jnp.int32)
    positions = (query_start[:, None] + jnp.arange(SPAN, dtype=jnp.int32)[None, :])[:, :, None, None]
    queries = rotary(projected[:, :, :, :GROUP, :], positions).astype(jnp.bfloat16)
    key_new = rotary(projected[:, :, :, GROUP:GROUP + 1, :], positions).astype(jnp.bfloat16)
    value_new = projected[:, :, :, GROUP + 1:, :].astype(jnp.bfloat16)
    fresh = jnp.concatenate([key_new, value_new], axis=3).reshape(REQS, SPAN, KVH * 2 * HD)
    slot_ids = jnp.arange(TOTAL_SLOTS, dtype=jnp.int32)
    slot_req, page_index, cached = locate(slot_ids, cache_pages, slot_order, new_pages)
    pages_out = write_pages(kv_pages, fresh, slot_req, page_index, cached, new_pages)
    block_slots = math.gcd(SLOTS, max(1, 512 // PAGE))

    def advance(j, running):
        low_slot = j * block_slots
        page_block = lax.dynamic_slice_in_dim(pages_out, low_slot, block_slots, 0)
        block_req = lax.dynamic_slice_in_dim(slot_req, low_slot, block_slots, 0)
        key_start = lax.dynamic_slice_in_dim(page_index, low_slot, block_slots, 0) * PAGE
        is_live = jnp.ones((block_slots,), dtype=jnp.bool_)
        terms = block_terms(queries, query_start, page_block, block_req, key_start, is_live)
        return fold(running, terms, block_req)
    acc_out, acc_max, acc_sum = lax.fori_loop(0, TOTAL_SLOTS // block_slots, advance, init_state(REQS, SPAN, KVH, GROUP, HD))
    attention = (acc_out / to_columns(acc_sum)).astype(jnp.bfloat16).reshape(TOKENS, HQ * HD)
    head_block = HQ * HD // N_TP
    summed = jnp.zeros((TOKENS, D), jnp.float32)
    for t in range(N_TP):
        part_sum = jnp.dot(attention[:, t * head_block:(t + 1) * head_block], out_weight[t * head_block:(t + 1) * head_block], preferred_element_type=jnp.float32)
        summed = summed + lax.optimization_barrier(part_sum.astype(jnp.bfloat16)).astype(jnp.float32)
    return (summed.astype(jnp.bfloat16), pages_out)
```

```python
import math

import jax
import jax.numpy as jnp
from jax import lax
from jax.experimental import pallas as pl
from jax.experimental.pallas import tpu as pltpu
from jax.sharding import PartitionSpec as P

HD = 64
GROUP = 4
SPAN = 512


THETA = 1000000.0
NEG_BIG = -1e30


def rotary(values, positions):
    head_width = values.shape[-1]
    half_width = head_width // 2
    inv_freq = jnp.power(THETA, -(jnp.arange(half_width, dtype=jnp.float32) * 2.0 / head_width))
    angles = positions.astype(jnp.float32)[..., None] * inv_freq
    cosines = jnp.cos(angles)
    sines = jnp.sin(angles)
    lower_half = values[..., :half_width]
    upper_half = values[..., half_width:]
    return jnp.concatenate(
        [lower_half * cosines - upper_half * sines, upper_half * cosines + lower_half * sines],
        axis=-1,
    )


def locate(slot_ids, cache_pages, slot_order, new_pages):
    requests = cache_pages.shape[0]
    slot_count = slot_order.shape[0]
    counts = cache_pages + new_pages
    page_ends = jnp.cumsum(counts)
    starts = page_ends - counts
    ranking = jnp.sum(
        jnp.where(
            slot_order[None, :] == slot_ids[:, None],
            jnp.arange(slot_count, dtype=jnp.int32)[None, :],
            0,
        ),
        axis=1,
    )
    holder = jnp.sum((starts[None, :] <= ranking[:, None]).astype(jnp.int32), axis=1) - 1
    onehot = jnp.arange(requests, dtype=jnp.int32)[None, :] == holder[:, None]
    first_page = jnp.sum(jnp.where(onehot, starts[None, :], 0), axis=1)
    cached = jnp.sum(jnp.where(onehot, cache_pages[None, :], 0), axis=1)
    return (holder, ranking - first_page, cached)


def write_pages(kv_pages, fresh, slot_req, page_index, cached, new_pages):
    page_rows = kv_pages.shape[1]
    lane_width = kv_pages.shape[2]
    fresh_pages = fresh.reshape(-1, page_rows, lane_width)
    pick = slot_req * new_pages + jnp.clip(page_index - cached, 0, new_pages - 1)
    return jnp.where((page_index >= cached)[:, None, None], fresh_pages[pick], kv_pages)


def slot_attention(sreq, perm, kstart, qstart, packed, pages):
    reqs, span_rows, _ = packed.shape
    slots, page_rows, _ = pages.shape
    qw = GROUP * HD

    def kernel(sreq_ref, perm_ref, kstart_ref, qstart_ref, q_ref, page_ref, o_ref, st_ref, m_sc, l_sc, acc_sc):
        i = pl.program_id(0)
        n = pl.num_programs(0)
        req = sreq_ref[i]
        prev = sreq_ref[jnp.maximum(i - 1, 0)]
        nxt = sreq_ref[jnp.minimum(i + 1, n - 1)]
        first = jnp.logical_or(i == 0, prev != req)
        last = jnp.logical_or(i == n - 1, nxt != req)

        @pl.when(first)
        def _():
            m_sc[...] = jnp.full(m_sc.shape, NEG_BIG, jnp.float32)
            l_sc[...] = jnp.zeros(l_sc.shape, jnp.float32)
            acc_sc[...] = jnp.zeros(acc_sc.shape, jnp.float32)

        kst = kstart_ref[i]
        qst = qstart_ref[req]
        page = page_ref[0]
        keys = page[:, :HD]
        vals = page[:, HD:]
        q_all = q_ref[0]
        row = lax.broadcasted_iota(jnp.int32, (span_rows, page_rows), 0) + qst
        col = lax.broadcasted_iota(jnp.int32, (span_rows, page_rows), 1) + kst
        vis = col <= row
        for g in range(GROUP):
            qg = q_all[:, g * HD:(g + 1) * HD]
            s = lax.dot_general(qg, keys, (((1,), (1,)), ((), ())), preferred_element_type=jnp.float32)
            s = jnp.where(vis, s, NEG_BIG)
            m_prev = m_sc[g]
            m_next = jnp.maximum(m_prev, jnp.max(s, axis=1, keepdims=True))
            alpha = jnp.exp(m_prev - m_next)
            p = jnp.where(vis, jnp.exp(s - m_next), 0.0)
            l_sc[g] = alpha * l_sc[g] + jnp.sum(p, axis=1, keepdims=True)
            m_sc[g] = m_next
            pv = jnp.dot(p.astype(jnp.bfloat16), vals, preferred_element_type=jnp.float32)
            acc_sc[g] = acc_sc[g] * alpha[:, :HD] + pv

        @pl.when(last)
        def _():
            lane = lax.broadcasted_iota(jnp.int32, (span_rows, page_rows), 1)
            st = jnp.zeros((span_rows, page_rows), jnp.float32)
            for g in range(GROUP):
                l_g = l_sc[g]
                safe = jnp.where(l_g > 0.0, l_g, 1.0)
                o_ref[0, :, g * HD:(g + 1) * HD] = (acc_sc[g] / safe[:, :HD]).astype(o_ref.dtype)
                st = jnp.where(lane == g, m_sc[g], st)
                st = jnp.where(lane == GROUP + g, l_g, st)
            st_ref[0] = st[:, :2 * GROUP]

    grid_spec = pltpu.PrefetchScalarGridSpec(
        num_scalar_prefetch=4,
        grid=(slots,),
        in_specs=[
            pl.BlockSpec((1, span_rows, qw), lambda i, sr, pm, ks, qs: (sr[i], 0, 0)),
            pl.BlockSpec((1, page_rows, 2 * HD), lambda i, sr, pm, ks, qs: (pm[i], 0, 0)),
        ],
        out_specs=[
            pl.BlockSpec((1, span_rows, qw), lambda i, sr, pm, ks, qs: (sr[i], 0, 0)),
            pl.BlockSpec((1, span_rows, 2 * GROUP), lambda i, sr, pm, ks, qs: (sr[i], 0, 0)),
        ],
        scratch_shapes=[
            pltpu.VMEM((GROUP, span_rows, page_rows), jnp.float32),
            pltpu.VMEM((GROUP, span_rows, page_rows), jnp.float32),
            pltpu.VMEM((GROUP, span_rows, HD), jnp.float32),
        ],
    )
    return pl.pallas_call(
        kernel,
        grid_spec=grid_spec,
        out_shape=[
            jax.ShapeDtypeStruct((reqs, span_rows, qw), jnp.bfloat16),
            jax.ShapeDtypeStruct((reqs, span_rows, 2 * GROUP), jnp.float32),
        ],
        compiler_params=pltpu.CompilerParams(dimension_semantics=("arbitrary",)),
    )(sreq, perm, kstart, qstart, packed, pages)


def body(hidden, qkv_weight, out_weight, kv_pages, cache_pages, slot_order):
    whole = lax.all_gather(hidden, "tp", axis=1, tiled=True)
    tok_rows = whole.shape[0]
    projected = jnp.dot(
        whole,
        lax.all_gather(qkv_weight, "req", axis=0, tiled=True),
        preferred_element_type=jnp.float32,
    )
    local_slots = kv_pages.shape[0]
    page_rows = kv_pages.shape[1]
    lane_width = kv_pages.shape[2]
    kv_heads = lane_width // (2 * HD)
    assert kv_heads == 1 and tok_rows == SPAN
    new_pages = SPAN // page_rows
    requests = cache_pages.shape[0]
    my_index = lax.axis_index("req")
    query_start = cache_pages * page_rows
    home_start = lax.dynamic_slice_in_dim(query_start, my_index, 1, 0)
    projected = projected.reshape(SPAN, GROUP + 2, HD)
    positions = (home_start + jnp.arange(SPAN, dtype=jnp.int32))[:, None]
    rotated = rotary(projected[:, : GROUP + 1, :], positions)
    scale = jnp.concatenate(
        [jnp.full((GROUP, 1), 1.0 / math.sqrt(HD), jnp.float32), jnp.ones((1, 1), jnp.float32)], axis=0
    )
    rotated = (rotated * scale).astype(jnp.bfloat16)
    value_new = projected[:, GROUP + 1 :, :].astype(jnp.bfloat16)
    packed = jnp.concatenate([rotated, value_new], axis=1).reshape(1, SPAN, (GROUP + 2) * HD)
    packed_all = lax.all_gather(packed, "req", axis=0, tiled=True)
    fresh_all = packed_all[:, :, GROUP * HD :]

    my_slots = my_index * local_slots + jnp.arange(local_slots, dtype=jnp.int32)
    slot_req, page_index, cached = locate(my_slots, cache_pages, slot_order, new_pages)
    pages_out = write_pages(kv_pages, fresh_all, slot_req, page_index, cached, new_pages)

    perm = jnp.argsort(slot_req, stable=True).astype(jnp.int32)
    sreq = slot_req[perm].astype(jnp.int32)
    kstart = (page_index[perm] * page_rows).astype(jnp.int32)
    part_o, part_st = slot_attention(sreq, perm, kstart, query_start.astype(jnp.int32), packed_all, pages_out)

    got_o = lax.all_to_all(part_o, "req", 0, 0, tiled=True)
    got_st = lax.all_to_all(part_st, "req", 0, 0, tiled=True)

    all_slots = jnp.arange(slot_order.shape[0], dtype=jnp.int32)
    all_req, unused_index, unused_cached = locate(all_slots, cache_pages, slot_order, new_pages)
    holds = (all_req.reshape(-1, local_slots) == my_index).any(axis=1)
    valid = holds[:, None, None]
    m_parts = jnp.where(valid, got_st[:, :, :GROUP], NEG_BIG)
    l_parts = jnp.where(valid, got_st[:, :, GROUP:], 0.0)
    top = jnp.max(m_parts, axis=0)
    w = l_parts * jnp.exp(m_parts - top[None])
    den = jnp.sum(w, axis=0)
    o_parts = jnp.where(valid[..., None], got_o.reshape(requests, SPAN, GROUP, HD).astype(jnp.float32), 0.0)
    num = jnp.sum(o_parts * w[..., None], axis=0)
    attention_flat = (num / den[..., None]).astype(jnp.bfloat16).reshape(SPAN, GROUP * HD)

    head_terms = jnp.dot(
        attention_flat,
        lax.all_gather(out_weight, "req", axis=1, tiled=True),
        preferred_element_type=jnp.float32,
    )
    attention_out = lax.psum_scatter(
        head_terms.astype(jnp.bfloat16), "tp", scatter_dimension=1, tiled=True
    )
    return (attention_out, pages_out)


def solution(mesh):
    return jax.shard_map(
        body,
        mesh=mesh,
        in_specs=(P("req", "tp"), P("req", "tp"), P("tp", "req"), P("req", None, "tp"), P(), P()),
        out_specs=(P("req", "tp"), P("req", None, "tp")),
        check_vma=False,
    )
```

```python
import math

import jax
import jax.numpy as jnp
from jax import lax
from jax.experimental import pallas as pl
from jax.experimental.pallas import tpu as pltpu
from jax.sharding import PartitionSpec as P

HD = 64
GROUP = 4
SPAN = 512


THETA = 1000000.0
NEG_BIG = -1e30


def rotary(values, positions):
    head_width = values.shape[-1]
    half_width = head_width // 2
    inv_freq = jnp.power(THETA, -(jnp.arange(half_width, dtype=jnp.float32) * 2.0 / head_width))
    angles = positions.astype(jnp.float32)[..., None] * inv_freq
    cosines = jnp.cos(angles)
    sines = jnp.sin(angles)
    lower_half = values[..., :half_width]
    upper_half = values[..., half_width:]
    return jnp.concatenate(
        [lower_half * cosines - upper_half * sines, upper_half * cosines + lower_half * sines],
        axis=-1,
    )


def locate(slot_ids, cache_pages, slot_order, new_pages):
    requests = cache_pages.shape[0]
    slot_count = slot_order.shape[0]
    counts = cache_pages + new_pages
    page_ends = jnp.cumsum(counts)
    starts = page_ends - counts
    ranking = jnp.sum(
        jnp.where(
            slot_order[None, :] == slot_ids[:, None],
            jnp.arange(slot_count, dtype=jnp.int32)[None, :],
            0,
        ),
        axis=1,
    )
    holder = jnp.sum((starts[None, :] <= ranking[:, None]).astype(jnp.int32), axis=1) - 1
    onehot = jnp.arange(requests, dtype=jnp.int32)[None, :] == holder[:, None]
    first_page = jnp.sum(jnp.where(onehot, starts[None, :], 0), axis=1)
    cached = jnp.sum(jnp.where(onehot, cache_pages[None, :], 0), axis=1)
    return (holder, ranking - first_page, cached)


def write_pages(kv_pages, fresh, slot_req, page_index, cached, new_pages):
    page_rows = kv_pages.shape[1]
    lane_width = kv_pages.shape[2]
    fresh_pages = fresh.reshape(-1, page_rows, lane_width)
    pick = slot_req * new_pages + jnp.clip(page_index - cached, 0, new_pages - 1)
    return jnp.where((page_index >= cached)[:, None, None], fresh_pages[pick], kv_pages)


def slot_attention(sreq, perm, kstart, qstart, packed, pages):
    reqs, span_rows, _ = packed.shape
    slots, page_rows, _ = pages.shape
    qw = GROUP * HD

    def kernel(sreq_ref, perm_ref, kstart_ref, qstart_ref, q_ref, page_ref, o_ref, st_ref, m_sc, l_sc, acc_sc):
        i = pl.program_id(0)
        n = pl.num_programs(0)
        req = sreq_ref[i]
        prev = sreq_ref[jnp.maximum(i - 1, 0)]
        nxt = sreq_ref[jnp.minimum(i + 1, n - 1)]
        first = jnp.logical_or(i == 0, prev != req)
        last = jnp.logical_or(i == n - 1, nxt != req)

        @pl.when(first)
        def _():
            m_sc[...] = jnp.full(m_sc.shape, NEG_BIG, jnp.float32)
            l_sc[...] = jnp.zeros(l_sc.shape, jnp.float32)
            acc_sc[...] = jnp.zeros(acc_sc.shape, jnp.float32)

        kst = kstart_ref[i]
        qst = qstart_ref[req]
        page = page_ref[0]
        keys = page[:, :HD]
        vals = page[:, HD:]
        q_all = q_ref[0]

        def update(masked):
            if masked:
                row = lax.broadcasted_iota(jnp.int32, (span_rows, page_rows), 0) + qst
                col = lax.broadcasted_iota(jnp.int32, (span_rows, page_rows), 1) + kst
                vis = col <= row
            for g in range(GROUP):
                qg = q_all[:, g * HD:(g + 1) * HD]
                s = lax.dot_general(qg, keys, (((1,), (1,)), ((), ())), preferred_element_type=jnp.float32)
                if masked:
                    s = jnp.where(vis, s, NEG_BIG)
                m_prev = m_sc[g]
                m_next = jnp.maximum(m_prev, jnp.max(s, axis=1, keepdims=True))
                alpha = jnp.exp(m_prev - m_next)
                p = jnp.exp(s - m_next)
                if masked:
                    p = jnp.where(vis, p, 0.0)
                l_sc[g] = alpha * l_sc[g] + jnp.sum(p, axis=1, keepdims=True)
                m_sc[g] = m_next
                pv = jnp.dot(p.astype(jnp.bfloat16), vals, preferred_element_type=jnp.float32)
                acc_sc[g] = acc_sc[g] * alpha[:, :HD] + pv

        partial = kst + (page_rows - 1) > qst

        @pl.when(partial)
        def _():
            update(True)

        @pl.when(jnp.logical_not(partial))
        def _():
            update(False)

        @pl.when(last)
        def _():
            lane = lax.broadcasted_iota(jnp.int32, (span_rows, page_rows), 1)
            st = jnp.zeros((span_rows, page_rows), jnp.float32)
            for g in range(GROUP):
                l_g = l_sc[g]
                safe = jnp.where(l_g > 0.0, l_g, 1.0)
                o_ref[0, :, g * HD:(g + 1) * HD] = (acc_sc[g] / safe[:, :HD]).astype(o_ref.dtype)
                st = jnp.where(lane == g, m_sc[g], st)
                st = jnp.where(lane == GROUP + g, l_g, st)
            st_ref[0] = st[:, :2 * GROUP]

    grid_spec = pltpu.PrefetchScalarGridSpec(
        num_scalar_prefetch=4,
        grid=(slots,),
        in_specs=[
            pl.BlockSpec((1, span_rows, qw), lambda i, sr, pm, ks, qs: (sr[i], 0, 0)),
            pl.BlockSpec((1, page_rows, 2 * HD), lambda i, sr, pm, ks, qs: (pm[i], 0, 0)),
        ],
        out_specs=[
            pl.BlockSpec((1, span_rows, qw), lambda i, sr, pm, ks, qs: (sr[i], 0, 0)),
            pl.BlockSpec((1, span_rows, 2 * GROUP), lambda i, sr, pm, ks, qs: (sr[i], 0, 0)),
        ],
        scratch_shapes=[
            pltpu.VMEM((GROUP, span_rows, page_rows), jnp.float32),
            pltpu.VMEM((GROUP, span_rows, page_rows), jnp.float32),
            pltpu.VMEM((GROUP, span_rows, HD), jnp.float32),
        ],
    )
    return pl.pallas_call(
        kernel,
        grid_spec=grid_spec,
        out_shape=[
            jax.ShapeDtypeStruct((reqs, span_rows, qw), jnp.bfloat16),
            jax.ShapeDtypeStruct((reqs, span_rows, 2 * GROUP), jnp.float32),
        ],
        compiler_params=pltpu.CompilerParams(dimension_semantics=("arbitrary",)),
    )(sreq, perm, kstart, qstart, packed, pages)


def body(hidden, qkv_weight, out_weight, kv_pages, cache_pages, slot_order):
    whole = lax.all_gather(hidden, "tp", axis=1, tiled=True)
    tok_rows = whole.shape[0]
    n_req = lax.axis_size("req")
    qkv_size = qkv_weight.size
    both = jnp.concatenate([qkv_weight.reshape(1, -1), out_weight.reshape(1, -1)], axis=1)
    both = lax.all_gather(both, "req", axis=0, tiled=True)
    qkv_full = both[:, :qkv_size].reshape(n_req * qkv_weight.shape[0], qkv_weight.shape[1])
    out_full = jnp.moveaxis(
        both[:, qkv_size:].reshape(n_req, out_weight.shape[0], out_weight.shape[1]), 0, 1
    ).reshape(out_weight.shape[0], n_req * out_weight.shape[1])
    projected = jnp.dot(whole, qkv_full, preferred_element_type=jnp.float32)
    local_slots = kv_pages.shape[0]
    page_rows = kv_pages.shape[1]
    lane_width = kv_pages.shape[2]
    kv_heads = lane_width // (2 * HD)
    assert kv_heads == 1 and tok_rows == SPAN
    new_pages = SPAN // page_rows
    requests = cache_pages.shape[0]
    my_index = lax.axis_index("req")
    query_start = cache_pages * page_rows
    home_start = lax.dynamic_slice_in_dim(query_start, my_index, 1, 0)
    projected = projected.reshape(SPAN, GROUP + 2, HD)
    positions = (home_start + jnp.arange(SPAN, dtype=jnp.int32))[:, None]
    rotated = rotary(projected[:, : GROUP + 1, :], positions)
    scale = jnp.concatenate(
        [jnp.full((GROUP, 1), 1.0 / math.sqrt(HD), jnp.float32), jnp.ones((1, 1), jnp.float32)], axis=0
    )
    rotated = (rotated * scale).astype(jnp.bfloat16)
    value_new = projected[:, GROUP + 1 :, :].astype(jnp.bfloat16)
    packed = jnp.concatenate([rotated, value_new], axis=1).reshape(1, SPAN, (GROUP + 2) * HD)
    packed_all = lax.all_gather(packed, "req", axis=0, tiled=True)
    fresh_all = packed_all[:, :, GROUP * HD :]

    my_slots = my_index * local_slots + jnp.arange(local_slots, dtype=jnp.int32)
    slot_req, page_index, cached = locate(my_slots, cache_pages, slot_order, new_pages)
    pages_out = write_pages(kv_pages, fresh_all, slot_req, page_index, cached, new_pages)

    perm = jnp.argsort(slot_req, stable=True).astype(jnp.int32)
    sreq = slot_req[perm].astype(jnp.int32)
    kstart = (page_index[perm] * page_rows).astype(jnp.int32)
    part_o, part_st = slot_attention(sreq, perm, kstart, query_start.astype(jnp.int32), packed_all, pages_out)

    hi = lax.reduce_precision(part_st, exponent_bits=8, mantissa_bits=7)
    rest = part_st - hi
    mid = lax.reduce_precision(rest, exponent_bits=8, mantissa_bits=7)
    lo = rest - mid
    hi, mid, lo = (t.astype(jnp.bfloat16) for t in (hi, mid, lo))
    st_rows = (SPAN * 3 * 2 * GROUP) // (GROUP * HD)
    st_bits = jnp.concatenate([hi, mid, lo], axis=2).reshape(requests, st_rows, GROUP * HD)
    sent = jnp.concatenate([part_o, st_bits], axis=1)
    got = lax.all_to_all(sent, "req", 0, 0, tiled=True)
    got_o = got[:, :SPAN]
    got_bits = got[:, SPAN:].reshape(requests, SPAN, 3, 2 * GROUP).astype(jnp.float32)
    got_st = (got_bits[:, :, 0] + got_bits[:, :, 1]) + got_bits[:, :, 2]

    all_slots = jnp.arange(slot_order.shape[0], dtype=jnp.int32)
    all_req, unused_index, unused_cached = locate(all_slots, cache_pages, slot_order, new_pages)
    holds = (all_req.reshape(-1, local_slots) == my_index).any(axis=1)
    valid = holds[:, None, None]
    m_parts = jnp.where(valid, got_st[:, :, :GROUP], NEG_BIG)
    l_parts = jnp.where(valid, got_st[:, :, GROUP:], 0.0)
    top = jnp.max(m_parts, axis=0)
    w = l_parts * jnp.exp(m_parts - top[None])
    den = jnp.sum(w, axis=0)
    o_parts = jnp.where(valid[..., None], got_o.reshape(requests, SPAN, GROUP, HD).astype(jnp.float32), 0.0)
    num = jnp.sum(o_parts * w[..., None], axis=0)
    attention_flat = (num / den[..., None]).astype(jnp.bfloat16).reshape(SPAN, GROUP * HD)

    head_terms = jnp.dot(attention_flat, out_full, preferred_element_type=jnp.float32)
    attention_out = lax.psum_scatter(
        head_terms.astype(jnp.bfloat16), "tp", scatter_dimension=1, tiled=True
    )
    return (attention_out, pages_out)


def solution(mesh):
    return jax.shard_map(
        body,
        mesh=mesh,
        in_specs=(P("req", "tp"), P("req", "tp"), P("tp", "req"), P("req", None, "tp"), P(), P()),
        out_specs=(P("req", "tp"), P("req", None, "tp")),
        check_vma=False,
    )
```

```python
import math

import jax
import jax.numpy as jnp
from jax import lax
from jax.experimental import pallas as pl
from jax.experimental.pallas import tpu as pltpu
from jax.sharding import PartitionSpec as P

HD = 64
GROUP = 4
SPAN = 512


THETA = 1000000.0
NEG_BIG = -1e30


def rotary(values, positions):
    head_width = values.shape[-1]
    half_width = head_width // 2
    inv_freq = jnp.power(THETA, -(jnp.arange(half_width, dtype=jnp.float32) * 2.0 / head_width))
    angles = positions.astype(jnp.float32)[..., None] * inv_freq
    cosines = jnp.cos(angles)
    sines = jnp.sin(angles)
    lower_half = values[..., :half_width]
    upper_half = values[..., half_width:]
    return jnp.concatenate(
        [lower_half * cosines - upper_half * sines, upper_half * cosines + lower_half * sines],
        axis=-1,
    )


def locate(slot_ids, cache_pages, slot_order, new_pages):
    requests = cache_pages.shape[0]
    slot_count = slot_order.shape[0]
    counts = cache_pages + new_pages
    page_ends = jnp.cumsum(counts)
    starts = page_ends - counts
    ranking = jnp.sum(
        jnp.where(
            slot_order[None, :] == slot_ids[:, None],
            jnp.arange(slot_count, dtype=jnp.int32)[None, :],
            0,
        ),
        axis=1,
    )
    holder = jnp.sum((starts[None, :] <= ranking[:, None]).astype(jnp.int32), axis=1) - 1
    onehot = jnp.arange(requests, dtype=jnp.int32)[None, :] == holder[:, None]
    first_page = jnp.sum(jnp.where(onehot, starts[None, :], 0), axis=1)
    cached = jnp.sum(jnp.where(onehot, cache_pages[None, :], 0), axis=1)
    return (holder, ranking - first_page, cached)


def write_pages(kv_pages, fresh, slot_req, page_index, cached, new_pages):
    page_rows = kv_pages.shape[1]
    lane_width = kv_pages.shape[2]
    fresh_pages = fresh.reshape(-1, page_rows, lane_width)
    pick = slot_req * new_pages + jnp.clip(page_index - cached, 0, new_pages - 1)
    return jnp.where((page_index >= cached)[:, None, None], fresh_pages[pick], kv_pages)


def slot_attention(sreq, perm, kstart, qstart, packed, pages):
    reqs, _, span_rows = packed.shape
    slots, page_rows, _ = pages.shape
    qw = GROUP * HD

    def kernel(sreq_ref, perm_ref, kstart_ref, qstart_ref, q_ref, page_ref, o_ref, st_ref, m_sc, l_sc, acc_sc):
        i = pl.program_id(0)
        n = pl.num_programs(0)
        req = sreq_ref[i]
        prev = sreq_ref[jnp.maximum(i - 1, 0)]
        nxt = sreq_ref[jnp.minimum(i + 1, n - 1)]
        first = jnp.logical_or(i == 0, prev != req)
        last = jnp.logical_or(i == n - 1, nxt != req)

        @pl.when(first)
        def _():
            m_sc[...] = jnp.full(m_sc.shape, NEG_BIG, jnp.float32)
            l_sc[...] = jnp.zeros(l_sc.shape, jnp.float32)
            acc_sc[...] = jnp.zeros(acc_sc.shape, jnp.float32)

        kst = kstart_ref[i]
        qst = qstart_ref[req]
        page = page_ref[0]
        keys = page[:, :HD]
        vals = page[:, HD:]

        def update(masked):
            if masked:
                key_pos = lax.broadcasted_iota(jnp.int32, (page_rows, span_rows), 0) + kst
                query_pos = lax.broadcasted_iota(jnp.int32, (page_rows, span_rows), 1) + qst
                vis = key_pos <= query_pos
            for g in range(GROUP):
                q_g = q_ref[0, g * HD:(g + 1) * HD, :]
                s = jnp.dot(keys, q_g, preferred_element_type=jnp.float32)
                if masked:
                    s = jnp.where(vis, s, NEG_BIG)
                m_prev = m_sc[g]
                m_next = jnp.maximum(m_prev, jnp.max(s, axis=0, keepdims=True))
                alpha = jnp.exp(m_prev - m_next)
                p = jnp.exp(s - m_next)
                if masked:
                    p = jnp.where(vis, p, 0.0)
                l_sc[g] = alpha * l_sc[g] + jnp.sum(p, axis=0, keepdims=True)
                m_sc[g] = m_next
                pv = lax.dot_general(
                    vals, p.astype(jnp.bfloat16), (((0,), (0,)), ((), ())),
                    preferred_element_type=jnp.float32,
                )
                acc_sc[g] = acc_sc[g] * alpha + pv

        partial = kst + (page_rows - 1) > qst

        @pl.when(partial)
        def _():
            update(True)

        @pl.when(jnp.logical_not(partial))
        def _():
            update(False)

        @pl.when(last)
        def _():
            for g in range(GROUP):
                l_g = l_sc[g]
                safe = jnp.where(l_g > 0.0, l_g, 1.0)
                o_ref[0, g * HD:(g + 1) * HD, :] = (acc_sc[g] / safe).astype(o_ref.dtype)
                st_ref[0, g:g + 1, :] = m_sc[g]
                st_ref[0, GROUP + g:GROUP + g + 1, :] = l_g

    grid_spec = pltpu.PrefetchScalarGridSpec(
        num_scalar_prefetch=4,
        grid=(slots,),
        in_specs=[
            pl.BlockSpec((1, qw, span_rows), lambda i, sr, pm, ks, qs: (sr[i], 0, 0)),
            pl.BlockSpec((1, page_rows, 2 * HD), lambda i, sr, pm, ks, qs: (pm[i], 0, 0)),
        ],
        out_specs=[
            pl.BlockSpec((1, qw, span_rows), lambda i, sr, pm, ks, qs: (sr[i], 0, 0)),
            pl.BlockSpec((1, 2 * GROUP, span_rows), lambda i, sr, pm, ks, qs: (sr[i], 0, 0)),
        ],
        scratch_shapes=[
            pltpu.VMEM((GROUP, 1, span_rows), jnp.float32),
            pltpu.VMEM((GROUP, 1, span_rows), jnp.float32),
            pltpu.VMEM((GROUP, HD, span_rows), jnp.float32),
        ],
    )
    return pl.pallas_call(
        kernel,
        grid_spec=grid_spec,
        out_shape=[
            jax.ShapeDtypeStruct((reqs, qw, span_rows), jnp.bfloat16),
            jax.ShapeDtypeStruct((reqs, 2 * GROUP, span_rows), jnp.float32),
        ],
        compiler_params=pltpu.CompilerParams(dimension_semantics=("arbitrary",)),
    )(sreq, perm, kstart, qstart, packed, pages)


def body(hidden, qkv_weight, out_weight, kv_pages, cache_pages, slot_order):
    whole = lax.all_gather(hidden, "tp", axis=1, tiled=True)
    tok_rows = whole.shape[0]
    n_req = lax.axis_size("req")
    qkv_size = qkv_weight.size
    both = jnp.concatenate([qkv_weight.reshape(1, -1), out_weight.reshape(1, -1)], axis=1)
    both = lax.all_gather(both, "req", axis=0, tiled=True)
    qkv_full = both[:, :qkv_size].reshape(n_req * qkv_weight.shape[0], qkv_weight.shape[1])
    out_full = jnp.moveaxis(
        both[:, qkv_size:].reshape(n_req, out_weight.shape[0], out_weight.shape[1]), 0, 1
    ).reshape(out_weight.shape[0], n_req * out_weight.shape[1])
    projected = jnp.dot(whole, qkv_full, preferred_element_type=jnp.float32)
    local_slots = kv_pages.shape[0]
    page_rows = kv_pages.shape[1]
    lane_width = kv_pages.shape[2]
    kv_heads = lane_width // (2 * HD)
    assert kv_heads == 1 and tok_rows == SPAN
    new_pages = SPAN // page_rows
    requests = cache_pages.shape[0]
    my_index = lax.axis_index("req")
    query_start = cache_pages * page_rows
    home_start = lax.dynamic_slice_in_dim(query_start, my_index, 1, 0)
    projected = projected.reshape(SPAN, GROUP + 2, HD)
    positions = (home_start + jnp.arange(SPAN, dtype=jnp.int32))[:, None]
    rotated = rotary(projected[:, : GROUP + 1, :], positions)
    scale = jnp.concatenate(
        [jnp.full((GROUP, 1), 1.0 / math.sqrt(HD), jnp.float32), jnp.ones((1, 1), jnp.float32)], axis=0
    )
    rotated = (rotated * scale).astype(jnp.bfloat16)
    value_new = projected[:, GROUP + 1 :, :].astype(jnp.bfloat16)
    q_t = jnp.transpose(rotated[:, :GROUP, :], (1, 2, 0)).reshape(GROUP * HD, SPAN)
    fresh = jnp.concatenate([rotated[:, GROUP:, :], value_new], axis=1).reshape(2 * HD, SPAN)
    packed = jnp.concatenate([q_t, fresh], axis=0)[None]
    packed_all = lax.all_gather(packed, "req", axis=0, tiled=True)
    fresh_all = packed_all[:, GROUP * HD :, :].reshape(requests, SPAN, 2 * HD)

    my_slots = my_index * local_slots + jnp.arange(local_slots, dtype=jnp.int32)
    slot_req, page_index, cached = locate(my_slots, cache_pages, slot_order, new_pages)
    pages_out = write_pages(kv_pages, fresh_all, slot_req, page_index, cached, new_pages)

    perm = jnp.argsort(slot_req, stable=True).astype(jnp.int32)
    sreq = slot_req[perm].astype(jnp.int32)
    kstart = (page_index[perm] * page_rows).astype(jnp.int32)
    part_o, part_st = slot_attention(sreq, perm, kstart, query_start.astype(jnp.int32), packed_all, pages_out)

    hi = lax.reduce_precision(part_st, exponent_bits=8, mantissa_bits=7)
    rest = part_st - hi
    mid = lax.reduce_precision(rest, exponent_bits=8, mantissa_bits=7)
    lo = rest - mid
    sent = jnp.concatenate([part_o] + [t.astype(jnp.bfloat16) for t in (hi, mid, lo)], axis=1)
    got = lax.all_to_all(sent, "req", 0, 0, tiled=True)
    qw = GROUP * HD
    got_o = got[:, :qw].reshape(requests, GROUP, HD, SPAN)
    got_bits = got[:, qw:].reshape(requests, 3, 2 * GROUP, SPAN).astype(jnp.float32)
    got_st = (got_bits[:, 0] + got_bits[:, 1]) + got_bits[:, 2]

    all_slots = jnp.arange(slot_order.shape[0], dtype=jnp.int32)
    all_req, unused_index, unused_cached = locate(all_slots, cache_pages, slot_order, new_pages)
    holds = (all_req.reshape(-1, local_slots) == my_index).any(axis=1)
    valid = holds[:, None, None]
    m_parts = jnp.where(valid, got_st[:, :GROUP], NEG_BIG)
    l_parts = jnp.where(valid, got_st[:, GROUP:], 0.0)
    top = jnp.max(m_parts, axis=0)
    w = l_parts * jnp.exp(m_parts - top[None])
    den = jnp.sum(w, axis=0)
    o_parts = jnp.where(valid[..., None], got_o.astype(jnp.float32), 0.0)
    num = jnp.sum(o_parts * w[:, :, None, :], axis=0)
    attention_t = (num / den[:, None, :]).astype(jnp.bfloat16)
    attention_flat = jnp.transpose(attention_t, (2, 0, 1)).reshape(SPAN, GROUP * HD)

    head_terms = jnp.dot(attention_flat, out_full, preferred_element_type=jnp.float32)
    attention_out = lax.psum_scatter(
        head_terms.astype(jnp.bfloat16), "tp", scatter_dimension=1, tiled=True
    )
    return (attention_out, pages_out)


def solution(mesh):
    return jax.shard_map(
        body,
        mesh=mesh,
        in_specs=(P("req", "tp"), P("req", "tp"), P("tp", "req"), P("req", None, "tp"), P(), P()),
        out_specs=(P("req", "tp"), P("req", None, "tp")),
        check_vma=False,
    )
```

```python
import math

import jax
import jax.numpy as jnp
from jax import lax
from jax.experimental import pallas as pl
from jax.experimental.pallas import tpu as pltpu
from jax.sharding import PartitionSpec as P

HD = 64
GROUP = 4
SPAN = 512


THETA = 1000000.0
NEG_BIG = -1e30


def rotary(values, positions):
    head_width = values.shape[-1]
    half_width = head_width // 2
    inv_freq = jnp.power(THETA, -(jnp.arange(half_width, dtype=jnp.float32) * 2.0 / head_width))
    angles = positions.astype(jnp.float32)[..., None] * inv_freq
    cosines = jnp.cos(angles)
    sines = jnp.sin(angles)
    lower_half = values[..., :half_width]
    upper_half = values[..., half_width:]
    return jnp.concatenate(
        [lower_half * cosines - upper_half * sines, upper_half * cosines + lower_half * sines],
        axis=-1,
    )


def locate(slot_ids, cache_pages, slot_order, new_pages):
    requests = cache_pages.shape[0]
    slot_count = slot_order.shape[0]
    counts = cache_pages + new_pages
    page_ends = jnp.cumsum(counts)
    starts = page_ends - counts
    ranking = jnp.sum(
        jnp.where(
            slot_order[None, :] == slot_ids[:, None],
            jnp.arange(slot_count, dtype=jnp.int32)[None, :],
            0,
        ),
        axis=1,
    )
    holder = jnp.sum((starts[None, :] <= ranking[:, None]).astype(jnp.int32), axis=1) - 1
    onehot = jnp.arange(requests, dtype=jnp.int32)[None, :] == holder[:, None]
    first_page = jnp.sum(jnp.where(onehot, starts[None, :], 0), axis=1)
    cached = jnp.sum(jnp.where(onehot, cache_pages[None, :], 0), axis=1)
    return (holder, ranking - first_page, cached)


def write_pages(kv_pages, fresh, slot_req, page_index, cached, new_pages):
    page_rows = kv_pages.shape[1]
    lane_width = kv_pages.shape[2]
    fresh_pages = fresh.reshape(-1, page_rows, lane_width)
    pick = slot_req * new_pages + jnp.clip(page_index - cached, 0, new_pages - 1)
    return jnp.where((page_index >= cached)[:, None, None], fresh_pages[pick], kv_pages)


def slot_attention(sreq, perm, kstart, qstart, packed, pages):
    reqs, _, span_rows = packed.shape
    slots, page_rows, _ = pages.shape
    qw = GROUP * HD

    def kernel(sreq_ref, perm_ref, kstart_ref, qstart_ref, q_ref, page_ref, o_ref, st_ref, m_sc, l_sc, acc_sc):
        i = pl.program_id(0)
        n = pl.num_programs(0)
        req = sreq_ref[i]
        prev = sreq_ref[jnp.maximum(i - 1, 0)]
        nxt = sreq_ref[jnp.minimum(i + 1, n - 1)]
        first = jnp.logical_or(i == 0, prev != req)
        last = jnp.logical_or(i == n - 1, nxt != req)

        @pl.when(first)
        def _():
            m_sc[...] = jnp.full(m_sc.shape, NEG_BIG, jnp.float32)
            l_sc[...] = jnp.zeros(l_sc.shape, jnp.float32)
            acc_sc[...] = jnp.zeros(acc_sc.shape, jnp.float32)

        kst = kstart_ref[i]
        qst = qstart_ref[req]
        page = page_ref[0]
        keys = page[:, :HD]
        vals = page[:, HD:]

        def update(masked):
            if masked:
                key_pos = lax.broadcasted_iota(jnp.int32, (page_rows, span_rows), 0) + kst
                query_pos = lax.broadcasted_iota(jnp.int32, (page_rows, span_rows), 1) + qst
                vis = key_pos <= query_pos
            for g in range(GROUP):
                q_g = q_ref[0, g * HD:(g + 1) * HD, :]
                s = jnp.dot(keys, q_g, preferred_element_type=jnp.float32)
                if masked:
                    s = jnp.where(vis, s, NEG_BIG)
                m_prev = m_sc[g]
                m_next = jnp.maximum(m_prev, jnp.max(s, axis=0, keepdims=True))
                alpha = jnp.exp(m_prev - m_next)
                p = jnp.exp(s - m_next)
                if masked:
                    p = jnp.where(vis, p, 0.0)
                l_sc[g] = alpha * l_sc[g] + jnp.sum(p, axis=0, keepdims=True)
                m_sc[g] = m_next
                pv = lax.dot_general(
                    vals, p.astype(jnp.bfloat16), (((0,), (0,)), ((), ())),
                    preferred_element_type=jnp.float32,
                )
                acc_sc[g] = acc_sc[g] * alpha + pv

        partial = kst + (page_rows - 1) > qst

        @pl.when(partial)
        def _():
            update(True)

        @pl.when(jnp.logical_not(partial))
        def _():
            update(False)

        @pl.when(last)
        def _():
            for g in range(GROUP):
                l_g = l_sc[g]
                safe = jnp.where(l_g > 0.0, l_g, 1.0)
                o_ref[0, g * HD:(g + 1) * HD, :] = (acc_sc[g] / safe).astype(o_ref.dtype)
                st_ref[0, g:g + 1, :] = m_sc[g]
                st_ref[0, GROUP + g:GROUP + g + 1, :] = l_g

    grid_spec = pltpu.PrefetchScalarGridSpec(
        num_scalar_prefetch=4,
        grid=(slots,),
        in_specs=[
            pl.BlockSpec((1, qw, span_rows), lambda i, sr, pm, ks, qs: (sr[i], 0, 0)),
            pl.BlockSpec((1, page_rows, 2 * HD), lambda i, sr, pm, ks, qs: (pm[i], 0, 0)),
        ],
        out_specs=[
            pl.BlockSpec((1, qw, span_rows), lambda i, sr, pm, ks, qs: (sr[i], 0, 0)),
            pl.BlockSpec((1, 2 * GROUP, span_rows), lambda i, sr, pm, ks, qs: (sr[i], 0, 0)),
        ],
        scratch_shapes=[
            pltpu.VMEM((GROUP, 1, span_rows), jnp.float32),
            pltpu.VMEM((GROUP, 1, span_rows), jnp.float32),
            pltpu.VMEM((GROUP, HD, span_rows), jnp.float32),
        ],
    )
    return pl.pallas_call(
        kernel,
        grid_spec=grid_spec,
        out_shape=[
            jax.ShapeDtypeStruct((reqs, qw, span_rows), jnp.bfloat16),
            jax.ShapeDtypeStruct((reqs, 2 * GROUP, span_rows), jnp.float32),
        ],
        compiler_params=pltpu.CompilerParams(dimension_semantics=("arbitrary",)),
    )(sreq, perm, kstart, qstart, packed, pages)


def body(hidden, qkv_weight, out_weight, kv_pages, cache_pages, slot_order):
    whole = lax.all_gather(hidden, "tp", axis=1, tiled=True)
    tok_rows = whole.shape[0]
    n_req = lax.axis_size("req")
    qkv_size = qkv_weight.size
    both = jnp.concatenate([qkv_weight.reshape(1, -1), out_weight.reshape(1, -1)], axis=1)
    both = lax.all_gather(both, "req", axis=0, tiled=True)
    qkv_full = both[:, :qkv_size].reshape(n_req * qkv_weight.shape[0], qkv_weight.shape[1])
    out_full = jnp.moveaxis(
        both[:, qkv_size:].reshape(n_req, out_weight.shape[0], out_weight.shape[1]), 0, 1
    ).reshape(out_weight.shape[0], n_req * out_weight.shape[1])
    projected = jnp.dot(whole, qkv_full, preferred_element_type=jnp.float32)
    local_slots = kv_pages.shape[0]
    page_rows = kv_pages.shape[1]
    lane_width = kv_pages.shape[2]
    kv_heads = lane_width // (2 * HD)
    assert kv_heads == 1 and tok_rows == SPAN
    new_pages = SPAN // page_rows
    requests = cache_pages.shape[0]
    my_index = lax.axis_index("req")
    query_start = cache_pages * page_rows
    home_start = lax.dynamic_slice_in_dim(query_start, my_index, 1, 0)
    projected = projected.reshape(SPAN, GROUP + 2, HD)
    positions = (home_start + jnp.arange(SPAN, dtype=jnp.int32))[:, None]
    rotated = rotary(projected[:, : GROUP + 1, :], positions)
    scale = jnp.concatenate(
        [jnp.full((GROUP, 1), 1.0 / math.sqrt(HD), jnp.float32), jnp.ones((1, 1), jnp.float32)], axis=0
    )
    rotated = (rotated * scale).astype(jnp.bfloat16)
    value_new = projected[:, GROUP + 1 :, :].astype(jnp.bfloat16)
    q_t = jnp.transpose(rotated[:, :GROUP, :], (1, 2, 0)).reshape(GROUP * HD, SPAN)
    fresh = jnp.concatenate([rotated[:, GROUP:, :], value_new], axis=1)
    halves = 2
    sub = SPAN // halves
    qw = GROUP * HD
    gathered = []
    for h in range(halves):
        piece = q_t[:, h * sub:(h + 1) * sub]
        if h == 0:
            piece = jnp.concatenate([piece, fresh.reshape(-1, sub)], axis=0)
        gathered.append(lax.all_gather(piece[None], "req", axis=0, tiled=True))
    fresh_all = gathered[0][:, qw:, :].reshape(requests, SPAN, 2 * HD)

    my_slots = my_index * local_slots + jnp.arange(local_slots, dtype=jnp.int32)
    slot_req, page_index, cached = locate(my_slots, cache_pages, slot_order, new_pages)
    pages_out = write_pages(kv_pages, fresh_all, slot_req, page_index, cached, new_pages)

    perm = jnp.argsort(slot_req, stable=True).astype(jnp.int32)
    sreq = slot_req[perm].astype(jnp.int32)
    kstart = (page_index[perm] * page_rows).astype(jnp.int32)

    all_slots = jnp.arange(slot_order.shape[0], dtype=jnp.int32)
    all_req, unused_index, unused_cached = locate(all_slots, cache_pages, slot_order, new_pages)
    holds = (all_req.reshape(-1, local_slots) == my_index).any(axis=1)
    valid = holds[:, None, None]

    outs = []
    for h in range(halves):
        q_start = (query_start + h * sub).astype(jnp.int32)
        part_o, part_st = slot_attention(sreq, perm, kstart, q_start, gathered[h], pages_out)
        hi = lax.reduce_precision(part_st, exponent_bits=8, mantissa_bits=7)
        rest = part_st - hi
        mid = lax.reduce_precision(rest, exponent_bits=8, mantissa_bits=7)
        lo = rest - mid
        sent = jnp.concatenate([part_o] + [t.astype(jnp.bfloat16) for t in (hi, mid, lo)], axis=1)
        got = lax.all_to_all(sent, "req", 0, 0, tiled=True)
        got_o = got[:, :qw].reshape(requests, GROUP, HD, sub)
        got_bits = got[:, qw:].reshape(requests, 3, 2 * GROUP, sub).astype(jnp.float32)
        got_st = (got_bits[:, 0] + got_bits[:, 1]) + got_bits[:, 2]

        m_parts = jnp.where(valid, got_st[:, :GROUP], NEG_BIG)
        l_parts = jnp.where(valid, got_st[:, GROUP:], 0.0)
        top = jnp.max(m_parts, axis=0)
        w = l_parts * jnp.exp(m_parts - top[None])
        den = jnp.sum(w, axis=0)
        o_parts = jnp.where(valid[..., None], got_o.astype(jnp.float32), 0.0)
        num = jnp.sum(o_parts * w[:, :, None, :], axis=0)
        attention_t = (num / den[:, None, :]).astype(jnp.bfloat16)
        attention_flat = jnp.transpose(attention_t, (2, 0, 1)).reshape(sub, qw)

        head_terms = jnp.dot(attention_flat, out_full, preferred_element_type=jnp.float32)
        outs.append(
            lax.psum_scatter(head_terms.astype(jnp.bfloat16), "tp", scatter_dimension=1, tiled=True)
        )
    attention_out = jnp.concatenate(outs, axis=0)
    return (attention_out, pages_out)


def solution(mesh):
    return jax.shard_map(
        body,
        mesh=mesh,
        in_specs=(P("req", "tp"), P("req", "tp"), P("tp", "req"), P("req", None, "tp"), P(), P()),
        out_specs=(P("req", "tp"), P("req", None, "tp")),
        check_vma=False,
    )
```

```python
import math

import jax
import jax.numpy as jnp
from jax import lax
from jax.experimental import pallas as pl
from jax.experimental.pallas import tpu as pltpu
from jax.sharding import PartitionSpec as P

HD = 64
GROUP = 4
SPAN = 512


THETA = 1000000.0
NEG_BIG = -1e30


def rotary(values, positions):
    head_width = values.shape[-1]
    half_width = head_width // 2
    inv_freq = jnp.power(THETA, -(jnp.arange(half_width, dtype=jnp.float32) * 2.0 / head_width))
    angles = positions.astype(jnp.float32)[..., None] * inv_freq
    cosines = jnp.cos(angles)
    sines = jnp.sin(angles)
    lower_half = values[..., :half_width]
    upper_half = values[..., half_width:]
    return jnp.concatenate(
        [lower_half * cosines - upper_half * sines, upper_half * cosines + lower_half * sines],
        axis=-1,
    )


def locate(slot_ids, cache_pages, slot_order, new_pages):
    requests = cache_pages.shape[0]
    slot_count = slot_order.shape[0]
    counts = cache_pages + new_pages
    page_ends = jnp.cumsum(counts)
    starts = page_ends - counts
    ranking = jnp.sum(
        jnp.where(
            slot_order[None, :] == slot_ids[:, None],
            jnp.arange(slot_count, dtype=jnp.int32)[None, :],
            0,
        ),
        axis=1,
    )
    holder = jnp.sum((starts[None, :] <= ranking[:, None]).astype(jnp.int32), axis=1) - 1
    onehot = jnp.arange(requests, dtype=jnp.int32)[None, :] == holder[:, None]
    first_page = jnp.sum(jnp.where(onehot, starts[None, :], 0), axis=1)
    cached = jnp.sum(jnp.where(onehot, cache_pages[None, :], 0), axis=1)
    return (holder, ranking - first_page, cached)


def write_pages(kv_pages, fresh, slot_req, page_index, cached, new_pages):
    page_rows = kv_pages.shape[1]
    lane_width = kv_pages.shape[2]
    fresh_pages = fresh.reshape(-1, page_rows, lane_width)
    pick = slot_req * new_pages + jnp.clip(page_index - cached, 0, new_pages - 1)
    return jnp.where((page_index >= cached)[:, None, None], fresh_pages[pick], kv_pages)


def slot_attention(sreq, perm, kstart, qstart, packed, pages):
    reqs, _, span_rows = packed.shape
    slots, page_rows, _ = pages.shape
    qw = GROUP * HD

    def kernel(sreq_ref, perm_ref, kstart_ref, qstart_ref, q_ref, page_ref, o_ref, st_ref, m_sc, l_sc, acc_sc):
        i = pl.program_id(0)
        n = pl.num_programs(0)
        req = sreq_ref[i]
        prev = sreq_ref[jnp.maximum(i - 1, 0)]
        nxt = sreq_ref[jnp.minimum(i + 1, n - 1)]
        first = jnp.logical_or(i == 0, prev != req)
        last = jnp.logical_or(i == n - 1, nxt != req)

        @pl.when(first)
        def _():
            m_sc[...] = jnp.full(m_sc.shape, NEG_BIG, jnp.float32)
            l_sc[...] = jnp.zeros(l_sc.shape, jnp.float32)
            acc_sc[...] = jnp.zeros(acc_sc.shape, jnp.float32)

        kst = kstart_ref[i]
        qst = qstart_ref[req]
        page = page_ref[perm_ref[i]]
        keys = page[:, :HD]
        vals = page[:, HD:]

        def update(masked):
            if masked:
                key_pos = lax.broadcasted_iota(jnp.int32, (page_rows, span_rows), 0) + kst
                query_pos = lax.broadcasted_iota(jnp.int32, (page_rows, span_rows), 1) + qst
                vis = key_pos <= query_pos
            for g in range(GROUP):
                q_g = q_ref[req, g * HD:(g + 1) * HD, :]
                s = jnp.dot(keys, q_g, preferred_element_type=jnp.float32)
                if masked:
                    s = jnp.where(vis, s, NEG_BIG)
                m_prev = m_sc[g]
                m_next = jnp.maximum(m_prev, jnp.max(s, axis=0, keepdims=True))
                alpha = jnp.exp(m_prev - m_next)
                p = jnp.exp(s - m_next)
                if masked:
                    p = jnp.where(vis, p, 0.0)
                l_sc[g] = alpha * l_sc[g] + jnp.sum(p, axis=0, keepdims=True)
                m_sc[g] = m_next
                pv = lax.dot_general(
                    vals, p.astype(jnp.bfloat16), (((0,), (0,)), ((), ())),
                    preferred_element_type=jnp.float32,
                )
                acc_sc[g] = acc_sc[g] * alpha + pv

        partial = kst + (page_rows - 1) > qst

        @pl.when(partial)
        def _():
            update(True)

        @pl.when(jnp.logical_not(partial))
        def _():
            update(False)

        @pl.when(last)
        def _():
            for g in range(GROUP):
                l_g = l_sc[g]
                safe = jnp.where(l_g > 0.0, l_g, 1.0)
                o_ref[req, g * HD:(g + 1) * HD, :] = (acc_sc[g] / safe).astype(o_ref.dtype)
                st_ref[req, g:g + 1, :] = m_sc[g]
                st_ref[req, GROUP + g:GROUP + g + 1, :] = l_g

    grid_spec = pltpu.PrefetchScalarGridSpec(
        num_scalar_prefetch=4,
        grid=(slots,),
        in_specs=[
            pl.BlockSpec((reqs, qw, span_rows), lambda i, sr, pm, ks, qs: (0, 0, 0)),
            pl.BlockSpec((slots, page_rows, 2 * HD), lambda i, sr, pm, ks, qs: (0, 0, 0)),
        ],
        out_specs=[
            pl.BlockSpec((reqs, qw, span_rows), lambda i, sr, pm, ks, qs: (0, 0, 0)),
            pl.BlockSpec((reqs, 2 * GROUP, span_rows), lambda i, sr, pm, ks, qs: (0, 0, 0)),
        ],
        scratch_shapes=[
            pltpu.VMEM((GROUP, 1, span_rows), jnp.float32),
            pltpu.VMEM((GROUP, 1, span_rows), jnp.float32),
            pltpu.VMEM((GROUP, HD, span_rows), jnp.float32),
        ],
    )
    return pl.pallas_call(
        kernel,
        grid_spec=grid_spec,
        out_shape=[
            jax.ShapeDtypeStruct((reqs, qw, span_rows), jnp.bfloat16),
            jax.ShapeDtypeStruct((reqs, 2 * GROUP, span_rows), jnp.float32),
        ],
        compiler_params=pltpu.CompilerParams(
            dimension_semantics=("arbitrary",), vmem_limit_bytes=48 * 1024 * 1024
        ),
    )(sreq, perm, kstart, qstart, packed, pages)


def body(hidden, qkv_weight, out_weight, kv_pages, cache_pages, slot_order):
    whole = lax.all_gather(hidden, "tp", axis=1, tiled=True)
    tok_rows = whole.shape[0]
    n_req = lax.axis_size("req")
    qkv_size = qkv_weight.size
    both = jnp.concatenate([qkv_weight.reshape(1, -1), out_weight.reshape(1, -1)], axis=1)
    both = lax.all_gather(both, "req", axis=0, tiled=True)
    qkv_full = both[:, :qkv_size].reshape(n_req * qkv_weight.shape[0], qkv_weight.shape[1])
    out_full = jnp.moveaxis(
        both[:, qkv_size:].reshape(n_req, out_weight.shape[0], out_weight.shape[1]), 0, 1
    ).reshape(out_weight.shape[0], n_req * out_weight.shape[1])
    projected = jnp.dot(whole, qkv_full, preferred_element_type=jnp.float32)
    local_slots = kv_pages.shape[0]
    page_rows = kv_pages.shape[1]
    lane_width = kv_pages.shape[2]
    kv_heads = lane_width // (2 * HD)
    assert kv_heads == 1 and tok_rows == SPAN
    new_pages = SPAN // page_rows
    requests = cache_pages.shape[0]
    my_index = lax.axis_index("req")
    query_start = cache_pages * page_rows
    home_start = lax.dynamic_slice_in_dim(query_start, my_index, 1, 0)
    projected = projected.reshape(SPAN, GROUP + 2, HD)
    positions = (home_start + jnp.arange(SPAN, dtype=jnp.int32))[:, None]
    rotated = rotary(projected[:, : GROUP + 1, :], positions)
    scale = jnp.concatenate(
        [jnp.full((GROUP, 1), 1.0 / math.sqrt(HD), jnp.float32), jnp.ones((1, 1), jnp.float32)], axis=0
    )
    rotated = (rotated * scale).astype(jnp.bfloat16)
    value_new = projected[:, GROUP + 1 :, :].astype(jnp.bfloat16)
    q_t = jnp.transpose(rotated[:, :GROUP, :], (1, 2, 0)).reshape(GROUP * HD, SPAN)
    fresh = jnp.concatenate([rotated[:, GROUP:, :], value_new], axis=1)
    halves = 2
    sub = SPAN // halves
    qw = GROUP * HD
    gathered = []
    for h in range(halves):
        piece = q_t[:, h * sub:(h + 1) * sub]
        if h == 0:
            piece = jnp.concatenate([piece, fresh.reshape(-1, sub)], axis=0)
        gathered.append(lax.all_gather(piece[None], "req", axis=0, tiled=True))
    fresh_all = gathered[0][:, qw:, :].reshape(requests, SPAN, 2 * HD)

    my_slots = my_index * local_slots + jnp.arange(local_slots, dtype=jnp.int32)
    slot_req, page_index, cached = locate(my_slots, cache_pages, slot_order, new_pages)
    pages_out = write_pages(kv_pages, fresh_all, slot_req, page_index, cached, new_pages)

    perm = jnp.argsort(slot_req, stable=True).astype(jnp.int32)
    sreq = slot_req[perm].astype(jnp.int32)
    kstart = (page_index[perm] * page_rows).astype(jnp.int32)

    all_slots = jnp.arange(slot_order.shape[0], dtype=jnp.int32)
    all_req, unused_index, unused_cached = locate(all_slots, cache_pages, slot_order, new_pages)
    holds = (all_req.reshape(-1, local_slots) == my_index).any(axis=1)
    valid = holds[:, None, None]

    outs = []
    for h in range(halves):
        q_start = (query_start + h * sub).astype(jnp.int32)
        part_o, part_st = slot_attention(sreq, perm, kstart, q_start, gathered[h], pages_out)
        hi = lax.reduce_precision(part_st, exponent_bits=8, mantissa_bits=7)
        rest = part_st - hi
        mid = lax.reduce_precision(rest, exponent_bits=8, mantissa_bits=7)
        lo = rest - mid
        sent = jnp.concatenate([part_o] + [t.astype(jnp.bfloat16) for t in (hi, mid, lo)], axis=1)
        got = lax.all_to_all(sent, "req", 0, 0, tiled=True)
        got_o = got[:, :qw].reshape(requests, GROUP, HD, sub)
        got_bits = got[:, qw:].reshape(requests, 3, 2 * GROUP, sub).astype(jnp.float32)
        got_st = (got_bits[:, 0] + got_bits[:, 1]) + got_bits[:, 2]

        m_parts = jnp.where(valid, got_st[:, :GROUP], NEG_BIG)
        l_parts = jnp.where(valid, got_st[:, GROUP:], 0.0)
        top = jnp.max(m_parts, axis=0)
        w = l_parts * jnp.exp(m_parts - top[None])
        den = jnp.sum(w, axis=0)
        o_parts = jnp.where(valid[..., None], got_o.astype(jnp.float32), 0.0)
        num = jnp.sum(o_parts * w[:, :, None, :], axis=0)
        attention_t = (num / den[:, None, :]).astype(jnp.bfloat16)
        attention_flat = jnp.transpose(attention_t, (2, 0, 1)).reshape(sub, qw)

        head_terms = jnp.dot(attention_flat, out_full, preferred_element_type=jnp.float32)
        outs.append(head_terms.astype(jnp.bfloat16))
    attention_out = lax.psum_scatter(
        jnp.concatenate(outs, axis=0), "tp", scatter_dimension=1, tiled=True
    )
    return (attention_out, pages_out)


def solution(mesh):
    return jax.shard_map(
        body,
        mesh=mesh,
        in_specs=(P("req", "tp"), P("req", "tp"), P("tp", "req"), P("req", None, "tp"), P(), P()),
        out_specs=(P("req", "tp"), P("req", None, "tp")),
        check_vma=False,
    )
```

```python
import math

import jax
import jax.numpy as jnp
from jax import lax
from jax.experimental import pallas as pl
from jax.experimental.pallas import tpu as pltpu
from jax.sharding import PartitionSpec as P

HD = 64
GROUP = 4
SPAN = 512


THETA = 1000000.0
NEG_BIG = -1e30


def rotary(values, positions):
    head_width = values.shape[-1]
    half_width = head_width // 2
    inv_freq = jnp.power(THETA, -(jnp.arange(half_width, dtype=jnp.float32) * 2.0 / head_width))
    angles = positions.astype(jnp.float32)[..., None] * inv_freq
    cosines = jnp.cos(angles)
    sines = jnp.sin(angles)
    lower_half = values[..., :half_width]
    upper_half = values[..., half_width:]
    return jnp.concatenate(
        [lower_half * cosines - upper_half * sines, upper_half * cosines + lower_half * sines],
        axis=-1,
    )


def locate(slot_ids, cache_pages, slot_order, new_pages):
    requests = cache_pages.shape[0]
    slot_count = slot_order.shape[0]
    counts = cache_pages + new_pages
    page_ends = jnp.cumsum(counts)
    starts = page_ends - counts
    ranking = jnp.sum(
        jnp.where(
            slot_order[None, :] == slot_ids[:, None],
            jnp.arange(slot_count, dtype=jnp.int32)[None, :],
            0,
        ),
        axis=1,
    )
    holder = jnp.sum((starts[None, :] <= ranking[:, None]).astype(jnp.int32), axis=1) - 1
    onehot = jnp.arange(requests, dtype=jnp.int32)[None, :] == holder[:, None]
    first_page = jnp.sum(jnp.where(onehot, starts[None, :], 0), axis=1)
    cached = jnp.sum(jnp.where(onehot, cache_pages[None, :], 0), axis=1)
    return (holder, ranking - first_page, cached)


def write_pages(kv_pages, fresh, slot_req, page_index, cached, new_pages):
    page_rows = kv_pages.shape[1]
    lane_width = kv_pages.shape[2]
    fresh_pages = fresh.reshape(-1, page_rows, lane_width)
    pick = slot_req * new_pages + jnp.clip(page_index - cached, 0, new_pages - 1)
    return jnp.where((page_index >= cached)[:, None, None], fresh_pages[pick], kv_pages)


def slot_attention(sreq, perm, kstart, qstart, packed, pages, sub):
    reqs, _, width = packed.shape
    slots, page_rows, _ = pages.shape
    assert width == GROUP * sub and sub & (sub - 1) == 0

    def kernel(sreq_ref, perm_ref, kstart_ref, qstart_ref, q_ref, page_ref, o_ref, st_ref, m_sc, l_sc, acc_sc):
        i = pl.program_id(0)
        n = pl.num_programs(0)
        req = sreq_ref[i]
        prev = sreq_ref[jnp.maximum(i - 1, 0)]
        nxt = sreq_ref[jnp.minimum(i + 1, n - 1)]
        first = jnp.logical_or(i == 0, prev != req)
        last = jnp.logical_or(i == n - 1, nxt != req)

        @pl.when(first)
        def _():
            m_sc[...] = jnp.full(m_sc.shape, NEG_BIG, jnp.float32)
            l_sc[...] = jnp.zeros(l_sc.shape, jnp.float32)
            acc_sc[...] = jnp.zeros(acc_sc.shape, jnp.float32)

        kst = kstart_ref[i]
        qst = qstart_ref[req]
        page = page_ref[perm_ref[i]]
        keys = page[:, :HD]
        vals = page[:, HD:]
        q = q_ref[req]

        def update(masked):
            s = jnp.dot(keys, q, preferred_element_type=jnp.float32)
            if masked:
                key_pos = lax.broadcasted_iota(jnp.int32, (page_rows, width), 0) + kst
                token = jnp.bitwise_and(lax.broadcasted_iota(jnp.int32, (page_rows, width), 1), sub - 1)
                vis = key_pos <= token + qst
                s = jnp.where(vis, s, NEG_BIG)
            m_prev = m_sc[...]
            m_next = jnp.maximum(m_prev, jnp.max(s, axis=0, keepdims=True))
            alpha = jnp.exp(m_prev - m_next)
            p = jnp.exp(s - m_next)
            if masked:
                p = jnp.where(vis, p, 0.0)
            l_sc[...] = alpha * l_sc[...] + jnp.sum(p, axis=0, keepdims=True)
            m_sc[...] = m_next
            pv = lax.dot_general(
                vals, p.astype(jnp.bfloat16), (((0,), (0,)), ((), ())),
                preferred_element_type=jnp.float32,
            )
            acc_sc[...] = acc_sc[...] * alpha + pv

        partial = kst + (page_rows - 1) > qst

        @pl.when(partial)
        def _():
            update(True)

        @pl.when(jnp.logical_not(partial))
        def _():
            update(False)

        @pl.when(last)
        def _():
            l_all = l_sc[...]
            safe = jnp.where(l_all > 0.0, l_all, 1.0)
            o_ref[req] = (acc_sc[...] / safe).astype(o_ref.dtype)
            st_ref[req, 0:1, :] = m_sc[...]
            st_ref[req, 1:2, :] = l_all

    grid_spec = pltpu.PrefetchScalarGridSpec(
        num_scalar_prefetch=4,
        grid=(slots,),
        in_specs=[
            pl.BlockSpec((reqs, HD, width), lambda i, sr, pm, ks, qs: (0, 0, 0)),
            pl.BlockSpec((slots, page_rows, 2 * HD), lambda i, sr, pm, ks, qs: (0, 0, 0)),
        ],
        out_specs=[
            pl.BlockSpec((reqs, HD, width), lambda i, sr, pm, ks, qs: (0, 0, 0)),
            pl.BlockSpec((reqs, 2, width), lambda i, sr, pm, ks, qs: (0, 0, 0)),
        ],
        scratch_shapes=[
            pltpu.VMEM((1, width), jnp.float32),
            pltpu.VMEM((1, width), jnp.float32),
            pltpu.VMEM((HD, width), jnp.float32),
        ],
    )
    return pl.pallas_call(
        kernel,
        grid_spec=grid_spec,
        out_shape=[
            jax.ShapeDtypeStruct((reqs, HD, width), jnp.bfloat16),
            jax.ShapeDtypeStruct((reqs, 2, width), jnp.float32),
        ],
        compiler_params=pltpu.CompilerParams(
            dimension_semantics=("arbitrary",), vmem_limit_bytes=48 * 1024 * 1024
        ),
    )(sreq, perm, kstart, qstart, packed, pages)


def body(hidden, qkv_weight, out_weight, kv_pages, cache_pages, slot_order):
    whole = lax.all_gather(hidden, "tp", axis=1, tiled=True)
    tok_rows = whole.shape[0]
    n_req = lax.axis_size("req")
    qkv_size = qkv_weight.size
    both = jnp.concatenate([qkv_weight.reshape(1, -1), out_weight.reshape(1, -1)], axis=1)
    both = lax.all_gather(both, "req", axis=0, tiled=True)
    qkv_full = both[:, :qkv_size].reshape(n_req * qkv_weight.shape[0], qkv_weight.shape[1])
    out_full = jnp.moveaxis(
        both[:, qkv_size:].reshape(n_req, out_weight.shape[0], out_weight.shape[1]), 0, 1
    ).reshape(out_weight.shape[0], n_req * out_weight.shape[1])
    projected = jnp.dot(whole, qkv_full, preferred_element_type=jnp.float32)
    local_slots = kv_pages.shape[0]
    page_rows = kv_pages.shape[1]
    lane_width = kv_pages.shape[2]
    kv_heads = lane_width // (2 * HD)
    assert kv_heads == 1 and tok_rows == SPAN
    new_pages = SPAN // page_rows
    requests = cache_pages.shape[0]
    my_index = lax.axis_index("req")
    query_start = cache_pages * page_rows
    home_start = lax.dynamic_slice_in_dim(query_start, my_index, 1, 0)
    projected = projected.reshape(SPAN, GROUP + 2, HD)
    positions = (home_start + jnp.arange(SPAN, dtype=jnp.int32))[:, None]
    rotated = rotary(projected[:, : GROUP + 1, :], positions)
    scale = jnp.concatenate(
        [jnp.full((GROUP, 1), 1.0 / math.sqrt(HD), jnp.float32), jnp.ones((1, 1), jnp.float32)], axis=0
    )
    rotated = (rotated * scale).astype(jnp.bfloat16)
    value_new = projected[:, GROUP + 1 :, :].astype(jnp.bfloat16)
    fresh = jnp.concatenate([rotated[:, GROUP:, :], value_new], axis=1)
    halves = 2
    sub = SPAN // halves
    width = GROUP * sub
    gathered = []
    for h in range(halves):
        piece = jnp.transpose(rotated[h * sub:(h + 1) * sub, :GROUP, :], (2, 1, 0)).reshape(HD, width)
        if h == 0:
            piece = jnp.concatenate([piece, fresh.reshape(-1, width)], axis=0)
        gathered.append(lax.all_gather(piece[None], "req", axis=0, tiled=True))
    fresh_all = gathered[0][:, HD:, :].reshape(requests, SPAN, 2 * HD)

    my_slots = my_index * local_slots + jnp.arange(local_slots, dtype=jnp.int32)
    slot_req, page_index, cached = locate(my_slots, cache_pages, slot_order, new_pages)
    pages_out = write_pages(kv_pages, fresh_all, slot_req, page_index, cached, new_pages)

    perm = jnp.argsort(slot_req, stable=True).astype(jnp.int32)
    sreq = slot_req[perm].astype(jnp.int32)
    kstart = (page_index[perm] * page_rows).astype(jnp.int32)

    all_slots = jnp.arange(slot_order.shape[0], dtype=jnp.int32)
    all_req, unused_index, unused_cached = locate(all_slots, cache_pages, slot_order, new_pages)
    holds = (all_req.reshape(-1, local_slots) == my_index).any(axis=1)
    valid = holds[:, None, None]

    outs = []
    for h in range(halves):
        q_start = (query_start + h * sub).astype(jnp.int32)
        part_o, part_st = slot_attention(sreq, perm, kstart, q_start, gathered[h], pages_out, sub)
        hi = lax.reduce_precision(part_st, exponent_bits=8, mantissa_bits=7)
        rest = part_st - hi
        mid = lax.reduce_precision(rest, exponent_bits=8, mantissa_bits=7)
        lo = rest - mid
        sent = jnp.concatenate([part_o] + [t.astype(jnp.bfloat16) for t in (hi, mid, lo)], axis=1)
        got = lax.all_to_all(sent, "req", 0, 0, tiled=True)
        got_o = got[:, :HD].reshape(requests, HD, GROUP, sub)
        got_bits = got[:, HD:].reshape(requests, 3, 2, GROUP, sub).astype(jnp.float32)
        got_st = (got_bits[:, 0] + got_bits[:, 1]) + got_bits[:, 2]

        m_parts = jnp.where(valid, got_st[:, 0], NEG_BIG)
        l_parts = jnp.where(valid, got_st[:, 1], 0.0)
        top = jnp.max(m_parts, axis=0)
        w = l_parts * jnp.exp(m_parts - top[None])
        den = jnp.sum(w, axis=0)
        o_parts = jnp.where(valid[..., None], got_o.astype(jnp.float32), 0.0)
        num = jnp.sum(o_parts * w[:, None, :, :], axis=0)
        attention_t = (num / den[None]).astype(jnp.bfloat16)
        attention_flat = jnp.transpose(attention_t, (2, 1, 0)).reshape(sub, GROUP * HD)

        head_terms = jnp.dot(attention_flat, out_full, preferred_element_type=jnp.float32)
        outs.append(head_terms.astype(jnp.bfloat16))
    attention_out = lax.psum_scatter(
        jnp.concatenate(outs, axis=0), "tp", scatter_dimension=1, tiled=True
    )
    return (attention_out, pages_out)


def solution(mesh):
    return jax.shard_map(
        body,
        mesh=mesh,
        in_specs=(P("req", "tp"), P("req", "tp"), P("tp", "req"), P("req", None, "tp"), P(), P()),
        out_specs=(P("req", "tp"), P("req", None, "tp")),
        check_vma=False,
    )
```

```python
import math

import jax
import jax.numpy as jnp
from jax import lax
from jax.experimental import pallas as pl
from jax.experimental.pallas import tpu as pltpu
from jax.sharding import PartitionSpec as P

HD = 64
GROUP = 4
SPAN = 512


THETA = 1000000.0
NEG_BIG = -1e30


def rotary(values, positions):
    head_width = values.shape[-1]
    half_width = head_width // 2
    inv_freq = jnp.power(THETA, -(jnp.arange(half_width, dtype=jnp.float32) * 2.0 / head_width))
    angles = positions.astype(jnp.float32)[..., None] * inv_freq
    cosines = jnp.cos(angles)
    sines = jnp.sin(angles)
    lower_half = values[..., :half_width]
    upper_half = values[..., half_width:]
    return jnp.concatenate(
        [lower_half * cosines - upper_half * sines, upper_half * cosines + lower_half * sines],
        axis=-1,
    )


def locate(slot_ids, cache_pages, slot_order, new_pages):
    requests = cache_pages.shape[0]
    slot_count = slot_order.shape[0]
    counts = cache_pages + new_pages
    page_ends = jnp.cumsum(counts)
    starts = page_ends - counts
    ranking = jnp.sum(
        jnp.where(
            slot_order[None, :] == slot_ids[:, None],
            jnp.arange(slot_count, dtype=jnp.int32)[None, :],
            0,
        ),
        axis=1,
    )
    holder = jnp.sum((starts[None, :] <= ranking[:, None]).astype(jnp.int32), axis=1) - 1
    onehot = jnp.arange(requests, dtype=jnp.int32)[None, :] == holder[:, None]
    first_page = jnp.sum(jnp.where(onehot, starts[None, :], 0), axis=1)
    cached = jnp.sum(jnp.where(onehot, cache_pages[None, :], 0), axis=1)
    return (holder, ranking - first_page, cached)


def write_pages(kv_pages, fresh, slot_req, page_index, cached, new_pages):
    page_rows = kv_pages.shape[1]
    lane_width = kv_pages.shape[2]
    fresh_pages = fresh.reshape(-1, page_rows, lane_width)
    pick = slot_req * new_pages + jnp.clip(page_index - cached, 0, new_pages - 1)
    return jnp.where((page_index >= cached)[:, None, None], fresh_pages[pick], kv_pages)


def slot_attention(sreq, perm, kstart, qstart, packed, pages, sub):
    reqs, _, width = packed.shape
    slots, page_rows, _ = pages.shape
    assert width == GROUP * sub and sub & (sub - 1) == 0

    def kernel(sreq_ref, perm_ref, kstart_ref, qstart_ref, q_ref, page_ref, o_ref, st_ref, m_sc, l_sc, acc_sc):
        i = pl.program_id(0)
        n = pl.num_programs(0)
        req = sreq_ref[i]
        prev = sreq_ref[jnp.maximum(i - 1, 0)]
        nxt = sreq_ref[jnp.minimum(i + 1, n - 1)]
        first = jnp.logical_or(i == 0, prev != req)
        last = jnp.logical_or(i == n - 1, nxt != req)

        @pl.when(first)
        def _():
            m_sc[...] = jnp.full(m_sc.shape, NEG_BIG, jnp.float32)
            l_sc[...] = jnp.zeros(l_sc.shape, jnp.float32)
            acc_sc[...] = jnp.zeros(acc_sc.shape, jnp.float32)

        kst = kstart_ref[i]
        qst = qstart_ref[req]
        page = page_ref[perm_ref[i]]
        keys = page[:, :HD]
        vals = page[:, HD:]
        q = q_ref[req]

        def update(masked):
            s = jnp.dot(keys, q, preferred_element_type=jnp.float32)
            if masked:
                key_pos = lax.broadcasted_iota(jnp.int32, (page_rows, width), 0) + kst
                token = jnp.bitwise_and(lax.broadcasted_iota(jnp.int32, (page_rows, width), 1), sub - 1)
                vis = key_pos <= token + qst
                s = jnp.where(vis, s, NEG_BIG)
            m_prev = m_sc[...]
            m_next = jnp.maximum(m_prev, jnp.max(s, axis=0, keepdims=True))
            alpha = jnp.exp(m_prev - m_next)
            p = jnp.exp(s - m_next)
            if masked:
                p = jnp.where(vis, p, 0.0)
            l_sc[...] = alpha * l_sc[...] + jnp.sum(p, axis=0, keepdims=True)
            m_sc[...] = m_next
            pv = lax.dot_general(
                vals, p.astype(jnp.bfloat16), (((0,), (0,)), ((), ())),
                preferred_element_type=jnp.float32,
            )
            acc_sc[...] = acc_sc[...] * alpha + pv

        partial = kst + (page_rows - 1) > qst

        @pl.when(partial)
        def _():
            update(True)

        @pl.when(jnp.logical_not(partial))
        def _():
            update(False)

        @pl.when(last)
        def _():
            l_all = l_sc[...]
            safe = jnp.where(l_all > 0.0, l_all, 1.0)
            o_ref[req] = (acc_sc[...] / safe).astype(o_ref.dtype)
            st_ref[req, 0:1, :] = m_sc[...]
            st_ref[req, 1:2, :] = l_all

    grid_spec = pltpu.PrefetchScalarGridSpec(
        num_scalar_prefetch=4,
        grid=(slots,),
        in_specs=[
            pl.BlockSpec((reqs, HD, width), lambda i, sr, pm, ks, qs: (0, 0, 0)),
            pl.BlockSpec((slots, page_rows, 2 * HD), lambda i, sr, pm, ks, qs: (0, 0, 0)),
        ],
        out_specs=[
            pl.BlockSpec((reqs, HD, width), lambda i, sr, pm, ks, qs: (0, 0, 0)),
            pl.BlockSpec((reqs, 2, width), lambda i, sr, pm, ks, qs: (0, 0, 0)),
        ],
        scratch_shapes=[
            pltpu.VMEM((1, width), jnp.float32),
            pltpu.VMEM((1, width), jnp.float32),
            pltpu.VMEM((HD, width), jnp.float32),
        ],
    )
    return pl.pallas_call(
        kernel,
        grid_spec=grid_spec,
        out_shape=[
            jax.ShapeDtypeStruct((reqs, HD, width), jnp.bfloat16),
            jax.ShapeDtypeStruct((reqs, 2, width), jnp.float32),
        ],
        compiler_params=pltpu.CompilerParams(
            dimension_semantics=("arbitrary",), vmem_limit_bytes=48 * 1024 * 1024
        ),
    )(sreq, perm, kstart, qstart, packed, pages)


def body(hidden, qkv_weight, out_weight, kv_pages, cache_pages, slot_order):
    n_tp = lax.axis_size("tp")
    copies = jnp.broadcast_to(hidden[None], (n_tp,) + hidden.shape)
    whole = lax.all_to_all(copies, "tp", 0, 0, tiled=True)
    whole = jnp.moveaxis(whole, 0, 1).reshape(hidden.shape[0], n_tp * hidden.shape[1])
    tok_rows = whole.shape[0]
    n_req = lax.axis_size("req")
    lanes = out_weight.shape[1]
    qkv_rows = qkv_weight.size // lanes
    both = jnp.concatenate([qkv_weight.reshape(qkv_rows, lanes), out_weight], axis=0)
    both = lax.all_gather(both[None], "req", axis=0, tiled=True)
    qkv_full = both[:, :qkv_rows].reshape(n_req * qkv_weight.shape[0], qkv_weight.shape[1])
    out_full = jnp.moveaxis(both[:, qkv_rows:], 0, 1).reshape(out_weight.shape[0], n_req * lanes)
    projected = jnp.dot(whole, qkv_full, preferred_element_type=jnp.float32)
    local_slots = kv_pages.shape[0]
    page_rows = kv_pages.shape[1]
    lane_width = kv_pages.shape[2]
    kv_heads = lane_width // (2 * HD)
    assert kv_heads == 1 and tok_rows == SPAN
    new_pages = SPAN // page_rows
    requests = cache_pages.shape[0]
    my_index = lax.axis_index("req")
    query_start = cache_pages * page_rows
    home_start = lax.dynamic_slice_in_dim(query_start, my_index, 1, 0)
    projected = projected.reshape(SPAN, GROUP + 2, HD)
    positions = (home_start + jnp.arange(SPAN, dtype=jnp.int32))[:, None]
    rotated = rotary(projected[:, : GROUP + 1, :], positions)
    scale = jnp.concatenate(
        [jnp.full((GROUP, 1), 1.0 / math.sqrt(HD), jnp.float32), jnp.ones((1, 1), jnp.float32)], axis=0
    )
    rotated = (rotated * scale).astype(jnp.bfloat16)
    value_new = projected[:, GROUP + 1 :, :].astype(jnp.bfloat16)
    fresh = jnp.concatenate([rotated[:, GROUP:, :], value_new], axis=1)
    halves = 2
    sub = SPAN // halves
    width = GROUP * sub
    gathered = []
    for h in range(halves):
        piece = jnp.transpose(rotated[h * sub:(h + 1) * sub, :GROUP, :], (2, 1, 0)).reshape(HD, width)
        if h == 0:
            piece = jnp.concatenate([piece, fresh.reshape(-1, width)], axis=0)
        gathered.append(lax.all_gather(piece[None], "req", axis=0, tiled=True))
    fresh_all = gathered[0][:, HD:, :].reshape(requests, SPAN, 2 * HD)

    my_slots = my_index * local_slots + jnp.arange(local_slots, dtype=jnp.int32)
    slot_req, page_index, cached = locate(my_slots, cache_pages, slot_order, new_pages)
    pages_out = write_pages(kv_pages, fresh_all, slot_req, page_index, cached, new_pages)

    perm = jnp.argsort(slot_req, stable=True).astype(jnp.int32)
    sreq = slot_req[perm].astype(jnp.int32)
    kstart = (page_index[perm] * page_rows).astype(jnp.int32)

    all_slots = jnp.arange(slot_order.shape[0], dtype=jnp.int32)
    all_req, unused_index, unused_cached = locate(all_slots, cache_pages, slot_order, new_pages)
    holds = (all_req.reshape(-1, local_slots) == my_index).any(axis=1)
    valid = holds[:, None, None]

    outs = []
    for h in range(halves):
        q_start = (query_start + h * sub).astype(jnp.int32)
        part_o, part_st = slot_attention(sreq, perm, kstart, q_start, gathered[h], pages_out, sub)
        hi = lax.reduce_precision(part_st, exponent_bits=8, mantissa_bits=7)
        rest = part_st - hi
        mid = lax.reduce_precision(rest, exponent_bits=8, mantissa_bits=7)
        lo = rest - mid
        sent = jnp.concatenate([part_o] + [t.astype(jnp.bfloat16) for t in (hi, mid, lo)], axis=1)
        got = lax.all_to_all(sent, "req", 0, 0, tiled=True)
        got_o = got[:, :HD].reshape(requests, HD, GROUP, sub)
        got_bits = got[:, HD:].reshape(requests, 3, 2, GROUP, sub).astype(jnp.float32)
        got_st = (got_bits[:, 0] + got_bits[:, 1]) + got_bits[:, 2]

        m_parts = jnp.where(valid, got_st[:, 0], NEG_BIG)
        l_parts = jnp.where(valid, got_st[:, 1], 0.0)
        top = jnp.max(m_parts, axis=0)
        w = l_parts * jnp.exp(m_parts - top[None])
        den = jnp.sum(w, axis=0)
        o_parts = jnp.where(valid[..., None], got_o.astype(jnp.float32), 0.0)
        num = jnp.sum(o_parts * w[:, None, :, :], axis=0)
        attention_t = (num / den[None]).astype(jnp.bfloat16)
        attention_flat = jnp.transpose(attention_t, (2, 1, 0)).reshape(sub, GROUP * HD)

        head_terms = jnp.dot(attention_flat, out_full, preferred_element_type=jnp.float32)
        outs.append(head_terms.astype(jnp.bfloat16))
    attention_out = lax.psum_scatter(
        jnp.concatenate(outs, axis=0), "tp", scatter_dimension=1, tiled=True
    )
    return (attention_out, pages_out)


def solution(mesh):
    return jax.shard_map(
        body,
        mesh=mesh,
        in_specs=(P("req", "tp"), P("req", "tp"), P("tp", "req"), P("req", None, "tp"), P(), P()),
        out_specs=(P("req", "tp"), P("req", None, "tp")),
        check_vma=False,
    )
```

```python
import math

import jax
import jax.numpy as jnp
from jax import lax
from jax.experimental import pallas as pl
from jax.experimental.pallas import tpu as pltpu
from jax.sharding import PartitionSpec as P

HD = 64
GROUP = 4
SPAN = 512


THETA = 1000000.0
NEG_BIG = -1e30


def rotary(values, positions):
    head_width = values.shape[-1]
    half_width = head_width // 2
    inv_freq = jnp.power(THETA, -(jnp.arange(half_width, dtype=jnp.float32) * 2.0 / head_width))
    angles = positions.astype(jnp.float32)[..., None] * inv_freq
    cosines = jnp.cos(angles)
    sines = jnp.sin(angles)
    lower_half = values[..., :half_width]
    upper_half = values[..., half_width:]
    return jnp.concatenate(
        [lower_half * cosines - upper_half * sines, upper_half * cosines + lower_half * sines],
        axis=-1,
    )


def locate(slot_ids, cache_pages, slot_order, new_pages):
    requests = cache_pages.shape[0]
    slot_count = slot_order.shape[0]
    counts = cache_pages + new_pages
    page_ends = jnp.cumsum(counts)
    starts = page_ends - counts
    ranking = jnp.sum(
        jnp.where(
            slot_order[None, :] == slot_ids[:, None],
            jnp.arange(slot_count, dtype=jnp.int32)[None, :],
            0,
        ),
        axis=1,
    )
    holder = jnp.sum((starts[None, :] <= ranking[:, None]).astype(jnp.int32), axis=1) - 1
    onehot = jnp.arange(requests, dtype=jnp.int32)[None, :] == holder[:, None]
    first_page = jnp.sum(jnp.where(onehot, starts[None, :], 0), axis=1)
    cached = jnp.sum(jnp.where(onehot, cache_pages[None, :], 0), axis=1)
    return (holder, ranking - first_page, cached)


def write_pages(kv_pages, fresh, slot_req, page_index, cached, new_pages):
    page_rows = kv_pages.shape[1]
    lane_width = kv_pages.shape[2]
    fresh_pages = fresh.reshape(-1, page_rows, lane_width)
    pick = slot_req * new_pages + jnp.clip(page_index - cached, 0, new_pages - 1)
    return jnp.where((page_index >= cached)[:, None, None], fresh_pages[pick], kv_pages)


def slot_attention(sreq, perm, kstart, qstart, packed, pages, sub):
    reqs, _, width = packed.shape
    slots, page_rows, _ = pages.shape
    assert width == GROUP * sub and sub & (sub - 1) == 0

    def kernel(sreq_ref, perm_ref, kstart_ref, qstart_ref, q_ref, page_ref, o_ref, st_ref, m_sc, l_sc, acc_sc):
        i = pl.program_id(0)
        n = pl.num_programs(0)
        req = sreq_ref[i]
        prev = sreq_ref[jnp.maximum(i - 1, 0)]
        nxt = sreq_ref[jnp.minimum(i + 1, n - 1)]
        first = jnp.logical_or(i == 0, prev != req)
        last = jnp.logical_or(i == n - 1, nxt != req)

        @pl.when(first)
        def _():
            m_sc[...] = jnp.full(m_sc.shape, NEG_BIG, jnp.float32)
            l_sc[...] = jnp.zeros(l_sc.shape, jnp.float32)
            acc_sc[...] = jnp.zeros(acc_sc.shape, jnp.float32)

        kst = kstart_ref[i]
        qst = qstart_ref[req]
        page = page_ref[perm_ref[i]]
        keys = page[:, :HD]
        vals = page[:, HD:]
        q = q_ref[req]

        def update(masked):
            s = jnp.dot(keys, q, preferred_element_type=jnp.float32)
            if masked:
                key_pos = lax.broadcasted_iota(jnp.int32, (page_rows, width), 0) + kst
                token = jnp.bitwise_and(lax.broadcasted_iota(jnp.int32, (page_rows, width), 1), sub - 1)
                vis = key_pos <= token + qst
                s = jnp.where(vis, s, NEG_BIG)
            m_prev = m_sc[...]
            m_next = jnp.maximum(m_prev, jnp.max(s, axis=0, keepdims=True))
            alpha = jnp.exp(m_prev - m_next)
            p = jnp.exp(s - m_next)
            if masked:
                p = jnp.where(vis, p, 0.0)
            l_sc[...] = alpha * l_sc[...] + jnp.sum(p, axis=0, keepdims=True)
            m_sc[...] = m_next
            pv = lax.dot_general(
                vals, p.astype(jnp.bfloat16), (((0,), (0,)), ((), ())),
                preferred_element_type=jnp.float32,
            )
            acc_sc[...] = acc_sc[...] * alpha + pv

        partial = kst + (page_rows - 1) > qst

        @pl.when(partial)
        def _():
            update(True)

        @pl.when(jnp.logical_not(partial))
        def _():
            update(False)

        @pl.when(last)
        def _():
            l_all = l_sc[...]
            safe = jnp.where(l_all > 0.0, l_all, 1.0)
            o_ref[req] = (acc_sc[...] / safe).astype(o_ref.dtype)
            st_ref[req, 0:1, :] = m_sc[...]
            st_ref[req, 1:2, :] = l_all

    grid_spec = pltpu.PrefetchScalarGridSpec(
        num_scalar_prefetch=4,
        grid=(slots,),
        in_specs=[
            pl.BlockSpec((reqs, HD, width), lambda i, sr, pm, ks, qs: (0, 0, 0)),
            pl.BlockSpec((slots, page_rows, 2 * HD), lambda i, sr, pm, ks, qs: (0, 0, 0)),
        ],
        out_specs=[
            pl.BlockSpec((reqs, HD, width), lambda i, sr, pm, ks, qs: (0, 0, 0)),
            pl.BlockSpec((reqs, 2, width), lambda i, sr, pm, ks, qs: (0, 0, 0)),
        ],
        scratch_shapes=[
            pltpu.VMEM((1, width), jnp.float32),
            pltpu.VMEM((1, width), jnp.float32),
            pltpu.VMEM((HD, width), jnp.float32),
        ],
    )
    return pl.pallas_call(
        kernel,
        grid_spec=grid_spec,
        out_shape=[
            jax.ShapeDtypeStruct((reqs, HD, width), jnp.bfloat16),
            jax.ShapeDtypeStruct((reqs, 2, width), jnp.float32),
        ],
        compiler_params=pltpu.CompilerParams(
            dimension_semantics=("arbitrary",), vmem_limit_bytes=48 * 1024 * 1024
        ),
    )(sreq, perm, kstart, qstart, packed, pages)


def body(hidden, qkv_weight, out_weight, kv_pages, cache_pages, slot_order):
    n_tp = lax.axis_size("tp")
    copies = jnp.broadcast_to(hidden[None], (n_tp,) + hidden.shape)
    whole = lax.all_to_all(copies, "tp", 0, 0, tiled=True)
    whole = jnp.moveaxis(whole, 0, 1).reshape(hidden.shape[0], n_tp * hidden.shape[1])
    tok_rows = whole.shape[0]
    n_req = lax.axis_size("req")
    lanes = out_weight.shape[1]
    qkv_rows = qkv_weight.size // lanes
    both = jnp.concatenate([qkv_weight.reshape(qkv_rows, lanes), out_weight], axis=0)
    both = lax.all_gather(both[None], "req", axis=0, tiled=True)
    qkv_full = both[:, :qkv_rows].reshape(n_req * qkv_weight.shape[0], qkv_weight.shape[1])
    out_full = jnp.moveaxis(both[:, qkv_rows:], 0, 1).reshape(out_weight.shape[0], n_req * lanes)
    projected = jnp.dot(whole, qkv_full, preferred_element_type=jnp.float32)
    local_slots = kv_pages.shape[0]
    page_rows = kv_pages.shape[1]
    lane_width = kv_pages.shape[2]
    kv_heads = lane_width // (2 * HD)
    assert kv_heads == 1 and tok_rows == SPAN
    new_pages = SPAN // page_rows
    requests = cache_pages.shape[0]
    my_index = lax.axis_index("req")
    query_start = cache_pages * page_rows
    home_start = lax.dynamic_slice_in_dim(query_start, my_index, 1, 0)
    projected = projected.reshape(SPAN, GROUP + 2, HD)
    positions = (home_start + jnp.arange(SPAN, dtype=jnp.int32))[:, None]
    rotated = rotary(projected[:, : GROUP + 1, :], positions)
    scale = jnp.concatenate(
        [jnp.full((GROUP, 1), 1.0 / math.sqrt(HD), jnp.float32), jnp.ones((1, 1), jnp.float32)], axis=0
    )
    rotated = (rotated * scale).astype(jnp.bfloat16)
    value_new = projected[:, GROUP + 1 :, :].astype(jnp.bfloat16)
    fresh = jnp.concatenate([rotated[:, GROUP:, :], value_new], axis=1)
    halves = 2
    sub = SPAN // halves
    width = GROUP * sub
    gathered = []
    for h in range(halves):
        piece = jnp.transpose(rotated[h * sub:(h + 1) * sub, :GROUP, :], (2, 1, 0)).reshape(HD, width)
        gathered.append(lax.all_gather(piece[None], "req", axis=0, tiled=True))
    fresh_copies = jnp.broadcast_to(fresh.reshape(1, -1, width), (n_req, fresh.size // width, width))
    fresh_all = lax.all_to_all(fresh_copies, "req", 0, 0, tiled=True).reshape(requests, SPAN, 2 * HD)

    my_slots = my_index * local_slots + jnp.arange(local_slots, dtype=jnp.int32)
    slot_req, page_index, cached = locate(my_slots, cache_pages, slot_order, new_pages)
    pages_out = write_pages(kv_pages, fresh_all, slot_req, page_index, cached, new_pages)

    perm = jnp.argsort(slot_req, stable=True).astype(jnp.int32)
    sreq = slot_req[perm].astype(jnp.int32)
    kstart = (page_index[perm] * page_rows).astype(jnp.int32)

    all_slots = jnp.arange(slot_order.shape[0], dtype=jnp.int32)
    all_req, unused_index, unused_cached = locate(all_slots, cache_pages, slot_order, new_pages)
    holds = (all_req.reshape(-1, local_slots) == my_index).any(axis=1)
    valid = holds[:, None, None]

    outs = []
    for h in range(halves):
        q_start = (query_start + h * sub).astype(jnp.int32)
        part_o, part_st = slot_attention(sreq, perm, kstart, q_start, gathered[h], pages_out, sub)
        hi = lax.reduce_precision(part_st, exponent_bits=8, mantissa_bits=7)
        rest = part_st - hi
        mid = lax.reduce_precision(rest, exponent_bits=8, mantissa_bits=7)
        lo = rest - mid
        sent = jnp.concatenate([part_o] + [t.astype(jnp.bfloat16) for t in (hi, mid, lo)], axis=1)
        got = lax.all_to_all(sent, "req", 0, 0, tiled=True)
        got_o = got[:, :HD].reshape(requests, HD, GROUP, sub)
        got_bits = got[:, HD:].reshape(requests, 3, 2, GROUP, sub).astype(jnp.float32)
        got_st = (got_bits[:, 0] + got_bits[:, 1]) + got_bits[:, 2]

        m_parts = jnp.where(valid, got_st[:, 0], NEG_BIG)
        l_parts = jnp.where(valid, got_st[:, 1], 0.0)
        top = jnp.max(m_parts, axis=0)
        w = l_parts * jnp.exp(m_parts - top[None])
        den = jnp.sum(w, axis=0)
        o_parts = jnp.where(valid[..., None], got_o.astype(jnp.float32), 0.0)
        num = jnp.sum(o_parts * w[:, None, :, :], axis=0)
        attention_t = (num / den[None]).astype(jnp.bfloat16)
        attention_flat = jnp.transpose(attention_t, (2, 1, 0)).reshape(sub, GROUP * HD)

        head_terms = jnp.dot(attention_flat, out_full, preferred_element_type=jnp.float32)
        outs.append(head_terms.astype(jnp.bfloat16))
    attention_out = lax.psum_scatter(
        jnp.concatenate(outs, axis=0), "tp", scatter_dimension=1, tiled=True
    )
    return (attention_out, pages_out)


def solution(mesh):
    return jax.shard_map(
        body,
        mesh=mesh,
        in_specs=(P("req", "tp"), P("req", "tp"), P("tp", "req"), P("req", None, "tp"), P(), P()),
        out_specs=(P("req", "tp"), P("req", None, "tp")),
        check_vma=False,
    )
```

```python
import math

import jax
import jax.numpy as jnp
from jax import lax
from jax.experimental import pallas as pl
from jax.experimental.pallas import tpu as pltpu
from jax.sharding import PartitionSpec as P

HD = 64
GROUP = 4
SPAN = 512


THETA = 1000000.0
NEG_BIG = -1e30


def rotary(values, positions):
    head_width = values.shape[-1]
    half_width = head_width // 2
    inv_freq = jnp.power(THETA, -(jnp.arange(half_width, dtype=jnp.float32) * 2.0 / head_width))
    angles = positions.astype(jnp.float32)[..., None] * inv_freq
    cosines = jnp.cos(angles)
    sines = jnp.sin(angles)
    lower_half = values[..., :half_width]
    upper_half = values[..., half_width:]
    return jnp.concatenate(
        [lower_half * cosines - upper_half * sines, upper_half * cosines + lower_half * sines],
        axis=-1,
    )


def locate(slot_ids, cache_pages, slot_order, new_pages):
    requests = cache_pages.shape[0]
    slot_count = slot_order.shape[0]
    counts = cache_pages + new_pages
    page_ends = jnp.cumsum(counts)
    starts = page_ends - counts
    ranking = jnp.sum(
        jnp.where(
            slot_order[None, :] == slot_ids[:, None],
            jnp.arange(slot_count, dtype=jnp.int32)[None, :],
            0,
        ),
        axis=1,
    )
    holder = jnp.sum((starts[None, :] <= ranking[:, None]).astype(jnp.int32), axis=1) - 1
    onehot = jnp.arange(requests, dtype=jnp.int32)[None, :] == holder[:, None]
    first_page = jnp.sum(jnp.where(onehot, starts[None, :], 0), axis=1)
    cached = jnp.sum(jnp.where(onehot, cache_pages[None, :], 0), axis=1)
    return (holder, ranking - first_page, cached)


def write_pages(kv_pages, fresh, slot_req, page_index, cached, new_pages):
    page_rows = kv_pages.shape[1]
    lane_width = kv_pages.shape[2]
    fresh_pages = fresh.reshape(-1, page_rows, lane_width)
    pick = slot_req * new_pages + jnp.clip(page_index - cached, 0, new_pages - 1)
    return jnp.where((page_index >= cached)[:, None, None], fresh_pages[pick], kv_pages)


def slot_attention(sreq, perm, kstart, qstart, packed, pages, sub):
    reqs, _, width = packed.shape
    slots, page_rows, _ = pages.shape
    assert width == GROUP * sub and sub & (sub - 1) == 0

    def kernel(sreq_ref, perm_ref, kstart_ref, qstart_ref, q_ref, page_ref, o_ref, st_ref, m_sc, l_sc, acc_sc):
        i = pl.program_id(0)
        n = pl.num_programs(0)
        req = sreq_ref[i]
        prev = sreq_ref[jnp.maximum(i - 1, 0)]
        nxt = sreq_ref[jnp.minimum(i + 1, n - 1)]
        first = jnp.logical_or(i == 0, prev != req)
        last = jnp.logical_or(i == n - 1, nxt != req)

        @pl.when(first)
        def _():
            m_sc[...] = jnp.full(m_sc.shape, NEG_BIG, jnp.float32)
            l_sc[...] = jnp.zeros(l_sc.shape, jnp.float32)
            acc_sc[...] = jnp.zeros(acc_sc.shape, jnp.float32)

        kst = kstart_ref[i]
        qst = qstart_ref[req]
        page = page_ref[perm_ref[i]]
        keys = page[:, :HD]
        vals = page[:, HD:]
        q = q_ref[req]

        def update(masked):
            s = jnp.dot(keys, q, preferred_element_type=jnp.float32)
            if masked:
                key_pos = lax.broadcasted_iota(jnp.int32, (page_rows, width), 0) + kst
                token = jnp.bitwise_and(lax.broadcasted_iota(jnp.int32, (page_rows, width), 1), sub - 1)
                vis = key_pos <= token + qst
                s = jnp.where(vis, s, NEG_BIG)
            m_prev = m_sc[...]
            m_next = jnp.maximum(m_prev, jnp.max(s, axis=0, keepdims=True))
            alpha = jnp.exp(m_prev - m_next)
            p = jnp.exp(s - m_next)
            if masked:
                p = jnp.where(vis, p, 0.0)
            l_sc[...] = alpha * l_sc[...] + jnp.sum(p, axis=0, keepdims=True)
            m_sc[...] = m_next
            pv = lax.dot_general(
                vals, p.astype(jnp.bfloat16), (((0,), (0,)), ((), ())),
                preferred_element_type=jnp.float32,
            )
            acc_sc[...] = acc_sc[...] * alpha + pv

        partial = kst + (page_rows - 1) > qst

        @pl.when(partial)
        def _():
            update(True)

        @pl.when(jnp.logical_not(partial))
        def _():
            update(False)

        @pl.when(last)
        def _():
            l_all = l_sc[...]
            safe = jnp.where(l_all > 0.0, l_all, 1.0)
            o_ref[req] = (acc_sc[...] / safe).astype(o_ref.dtype)
            st_ref[req, 0:1, :] = m_sc[...]
            st_ref[req, 1:2, :] = l_all

    grid_spec = pltpu.PrefetchScalarGridSpec(
        num_scalar_prefetch=4,
        grid=(slots,),
        in_specs=[
            pl.BlockSpec((reqs, HD, width), lambda i, sr, pm, ks, qs: (0, 0, 0)),
            pl.BlockSpec((slots, page_rows, 2 * HD), lambda i, sr, pm, ks, qs: (0, 0, 0)),
        ],
        out_specs=[
            pl.BlockSpec((reqs, HD, width), lambda i, sr, pm, ks, qs: (0, 0, 0)),
            pl.BlockSpec((reqs, 2, width), lambda i, sr, pm, ks, qs: (0, 0, 0)),
        ],
        scratch_shapes=[
            pltpu.VMEM((1, width), jnp.float32),
            pltpu.VMEM((1, width), jnp.float32),
            pltpu.VMEM((HD, width), jnp.float32),
        ],
    )
    return pl.pallas_call(
        kernel,
        grid_spec=grid_spec,
        out_shape=[
            jax.ShapeDtypeStruct((reqs, HD, width), jnp.bfloat16),
            jax.ShapeDtypeStruct((reqs, 2, width), jnp.float32),
        ],
        compiler_params=pltpu.CompilerParams(
            dimension_semantics=("arbitrary",), vmem_limit_bytes=48 * 1024 * 1024
        ),
    )(sreq, perm, kstart, qstart, packed, pages)


def body(hidden, qkv_weight, out_weight, kv_pages, cache_pages, slot_order):
    n_tp = lax.axis_size("tp")
    copies = jnp.broadcast_to(hidden[None], (n_tp,) + hidden.shape)
    whole = lax.all_to_all(copies, "tp", 0, 0, tiled=True)
    whole = jnp.moveaxis(whole, 0, 1).reshape(hidden.shape[0], n_tp * hidden.shape[1])
    tok_rows = whole.shape[0]
    n_req = lax.axis_size("req")
    lanes = out_weight.shape[1]
    qkv_rows = qkv_weight.size // lanes
    both = jnp.concatenate([qkv_weight.reshape(qkv_rows, lanes), out_weight], axis=0)
    both = lax.all_gather(both[None], "req", axis=0, tiled=True)
    qkv_full = both[:, :qkv_rows].reshape(n_req * qkv_weight.shape[0], qkv_weight.shape[1])
    out_full = jnp.moveaxis(both[:, qkv_rows:], 0, 1).reshape(out_weight.shape[0], n_req * lanes)
    projected = jnp.dot(whole, qkv_full, preferred_element_type=jnp.float32)
    local_slots = kv_pages.shape[0]
    page_rows = kv_pages.shape[1]
    lane_width = kv_pages.shape[2]
    kv_heads = lane_width // (2 * HD)
    assert kv_heads == 1 and tok_rows == SPAN
    new_pages = SPAN // page_rows
    requests = cache_pages.shape[0]
    my_index = lax.axis_index("req")
    query_start = cache_pages * page_rows
    home_start = lax.dynamic_slice_in_dim(query_start, my_index, 1, 0)
    projected = projected.reshape(SPAN, GROUP + 2, HD)
    positions = (home_start + jnp.arange(SPAN, dtype=jnp.int32))[:, None]
    rotated = rotary(projected[:, : GROUP + 1, :], positions)
    scale = jnp.concatenate(
        [jnp.full((GROUP, 1), 1.0 / math.sqrt(HD), jnp.float32), jnp.ones((1, 1), jnp.float32)], axis=0
    )
    rotated = (rotated * scale).astype(jnp.bfloat16)
    value_new = projected[:, GROUP + 1 :, :].astype(jnp.bfloat16)
    fresh = jnp.concatenate([rotated[:, GROUP:, :], value_new], axis=1)
    halves = 2
    sub = SPAN // halves
    width = GROUP * sub
    gathered = []
    for h in range(halves):
        piece = jnp.transpose(rotated[h * sub:(h + 1) * sub, :GROUP, :], (2, 1, 0)).reshape(HD, width)
        if h == 0:
            piece = jnp.concatenate([piece, fresh.reshape(-1, width)], axis=0)
        gathered.append(lax.all_gather(piece[None], "req", axis=0, tiled=True))
    fresh_all = gathered[0][:, HD:, :].reshape(requests, SPAN, 2 * HD)

    my_slots = my_index * local_slots + jnp.arange(local_slots, dtype=jnp.int32)
    slot_req, page_index, cached = locate(my_slots, cache_pages, slot_order, new_pages)
    pages_out = write_pages(kv_pages, fresh_all, slot_req, page_index, cached, new_pages)

    perm = jnp.argsort(slot_req, stable=True).astype(jnp.int32)
    sreq = slot_req[perm].astype(jnp.int32)
    kstart = (page_index[perm] * page_rows).astype(jnp.int32)

    all_slots = jnp.arange(slot_order.shape[0], dtype=jnp.int32)
    all_req, unused_index, unused_cached = locate(all_slots, cache_pages, slot_order, new_pages)
    holds = (all_req.reshape(-1, local_slots) == my_index).any(axis=1)
    valid = holds[:, None, None]

    outs = []
    for h in range(halves):
        q_start = (query_start + h * sub).astype(jnp.int32)
        part_o, part_st = slot_attention(sreq, perm, kstart, q_start, gathered[h], pages_out, sub)
        hi = lax.reduce_precision(part_st, exponent_bits=8, mantissa_bits=7)
        rest = part_st - hi
        mid = lax.reduce_precision(rest, exponent_bits=8, mantissa_bits=7)
        lo = rest - mid
        sent = jnp.concatenate([part_o] + [t.astype(jnp.bfloat16) for t in (hi, mid, lo)], axis=1)
        got = lax.all_to_all(sent, "req", 0, 0, tiled=True)
        got_o = got[:, :HD].reshape(requests, HD, GROUP, sub)
        got_bits = got[:, HD:].reshape(requests, 3, 2, GROUP, sub).astype(jnp.float32)
        got_st = (got_bits[:, 0] + got_bits[:, 1]) + got_bits[:, 2]

        m_parts = jnp.where(valid, got_st[:, 0], NEG_BIG)
        l_parts = jnp.where(valid, got_st[:, 1], 0.0)
        top = jnp.max(m_parts, axis=0)
        w = l_parts * jnp.exp(m_parts - top[None])
        den = jnp.sum(w, axis=0)
        o_parts = jnp.where(valid[..., None], got_o.astype(jnp.float32), 0.0)
        num = jnp.sum(o_parts * w[:, None, :, :], axis=0)
        attention_t = (num / den[None]).astype(jnp.bfloat16)
        attention_flat = jnp.transpose(attention_t, (2, 1, 0)).reshape(sub, GROUP * HD)

        head_terms = jnp.dot(attention_flat, out_full, preferred_element_type=jnp.float32)
        outs.append(head_terms.astype(jnp.bfloat16))
    partial_t = jnp.concatenate(outs, axis=0)
    cols = partial_t.shape[1] // n_tp
    partial_t = jnp.moveaxis(partial_t.reshape(partial_t.shape[0], n_tp, cols), 1, 0)
    got_t = lax.all_to_all(partial_t, "tp", 0, 0, tiled=True)
    attention_out = jnp.sum(got_t.astype(jnp.float32), axis=0).astype(jnp.bfloat16)
    return (attention_out, pages_out)


def solution(mesh):
    return jax.shard_map(
        body,
        mesh=mesh,
        in_specs=(P("req", "tp"), P("req", "tp"), P("tp", "req"), P("req", None, "tp"), P(), P()),
        out_specs=(P("req", "tp"), P("req", None, "tp")),
        check_vma=False,
    )
```

```python
import math

import jax
import jax.numpy as jnp
from jax import lax
from jax.experimental import pallas as pl
from jax.experimental.pallas import tpu as pltpu
from jax.sharding import PartitionSpec as P

HD = 64
GROUP = 4
SPAN = 512


THETA = 1000000.0
NEG_BIG = -1e30


def rotary(values, positions):
    head_width = values.shape[-1]
    half_width = head_width // 2
    inv_freq = jnp.power(THETA, -(jnp.arange(half_width, dtype=jnp.float32) * 2.0 / head_width))
    angles = positions.astype(jnp.float32)[..., None] * inv_freq
    cosines = jnp.cos(angles)
    sines = jnp.sin(angles)
    lower_half = values[..., :half_width]
    upper_half = values[..., half_width:]
    return jnp.concatenate(
        [lower_half * cosines - upper_half * sines, upper_half * cosines + lower_half * sines],
        axis=-1,
    )


def locate(slot_ids, cache_pages, slot_order, new_pages):
    requests = cache_pages.shape[0]
    slot_count = slot_order.shape[0]
    counts = cache_pages + new_pages
    page_ends = jnp.cumsum(counts)
    starts = page_ends - counts
    ranking = jnp.sum(
        jnp.where(
            slot_order[None, :] == slot_ids[:, None],
            jnp.arange(slot_count, dtype=jnp.int32)[None, :],
            0,
        ),
        axis=1,
    )
    holder = jnp.sum((starts[None, :] <= ranking[:, None]).astype(jnp.int32), axis=1) - 1
    onehot = jnp.arange(requests, dtype=jnp.int32)[None, :] == holder[:, None]
    first_page = jnp.sum(jnp.where(onehot, starts[None, :], 0), axis=1)
    cached = jnp.sum(jnp.where(onehot, cache_pages[None, :], 0), axis=1)
    return (holder, ranking - first_page, cached)


def write_pages(kv_pages, fresh, slot_req, page_index, cached, new_pages):
    page_rows = kv_pages.shape[1]
    lane_width = kv_pages.shape[2]
    fresh_pages = fresh.reshape(-1, page_rows, lane_width)
    pick = slot_req * new_pages + jnp.clip(page_index - cached, 0, new_pages - 1)
    return jnp.where((page_index >= cached)[:, None, None], fresh_pages[pick], kv_pages)


def slot_attention(sreq, perm, kstart, qstart, packed, pages, sub):
    reqs, _, width = packed.shape
    slots, page_rows, _ = pages.shape
    assert width == GROUP * sub and sub & (sub - 1) == 0

    def kernel(sreq_ref, perm_ref, kstart_ref, qstart_ref, q_ref, page_ref, o_ref, st_ref, m_sc, l_sc, acc_sc):
        i = pl.program_id(0)
        n = pl.num_programs(0)
        req = sreq_ref[i]
        prev = sreq_ref[jnp.maximum(i - 1, 0)]
        nxt = sreq_ref[jnp.minimum(i + 1, n - 1)]
        first = jnp.logical_or(i == 0, prev != req)
        last = jnp.logical_or(i == n - 1, nxt != req)

        @pl.when(first)
        def _():
            m_sc[...] = jnp.full(m_sc.shape, NEG_BIG, jnp.float32)
            l_sc[...] = jnp.zeros(l_sc.shape, jnp.float32)
            acc_sc[...] = jnp.zeros(acc_sc.shape, jnp.float32)

        kst = kstart_ref[i]
        qst = qstart_ref[req]
        page = page_ref[perm_ref[i]]
        keys = page[:, :HD]
        vals = page[:, HD:]
        q = q_ref[req]

        def update(masked):
            s = jnp.dot(keys, q, preferred_element_type=jnp.float32)
            if masked:
                key_pos = lax.broadcasted_iota(jnp.int32, (page_rows, width), 0) + kst
                token = jnp.bitwise_and(lax.broadcasted_iota(jnp.int32, (page_rows, width), 1), sub - 1)
                vis = key_pos <= token + qst
                s = jnp.where(vis, s, NEG_BIG)
            m_prev = m_sc[...]
            m_next = jnp.maximum(m_prev, jnp.max(s, axis=0, keepdims=True))
            alpha = jnp.exp(m_prev - m_next)
            p = jnp.exp(s - m_next)
            if masked:
                p = jnp.where(vis, p, 0.0)
            l_sc[...] = alpha * l_sc[...] + jnp.sum(p, axis=0, keepdims=True)
            m_sc[...] = m_next
            pv = lax.dot_general(
                vals, p.astype(jnp.bfloat16), (((0,), (0,)), ((), ())),
                preferred_element_type=jnp.float32,
            )
            acc_sc[...] = acc_sc[...] * alpha + pv

        partial = kst + (page_rows - 1) > qst

        @pl.when(partial)
        def _():
            update(True)

        @pl.when(jnp.logical_not(partial))
        def _():
            update(False)

        @pl.when(last)
        def _():
            l_all = l_sc[...]
            safe = jnp.where(l_all > 0.0, l_all, 1.0)
            o_ref[req] = (acc_sc[...] / safe).astype(o_ref.dtype)
            st_ref[req, 0:1, :] = m_sc[...]
            st_ref[req, 1:2, :] = l_all

    grid_spec = pltpu.PrefetchScalarGridSpec(
        num_scalar_prefetch=4,
        grid=(slots,),
        in_specs=[
            pl.BlockSpec((reqs, HD, width), lambda i, sr, pm, ks, qs: (0, 0, 0)),
            pl.BlockSpec((slots, page_rows, 2 * HD), lambda i, sr, pm, ks, qs: (0, 0, 0)),
        ],
        out_specs=[
            pl.BlockSpec((reqs, HD, width), lambda i, sr, pm, ks, qs: (0, 0, 0)),
            pl.BlockSpec((reqs, 2, width), lambda i, sr, pm, ks, qs: (0, 0, 0)),
        ],
        scratch_shapes=[
            pltpu.VMEM((1, width), jnp.float32),
            pltpu.VMEM((1, width), jnp.float32),
            pltpu.VMEM((HD, width), jnp.float32),
        ],
    )
    return pl.pallas_call(
        kernel,
        grid_spec=grid_spec,
        out_shape=[
            jax.ShapeDtypeStruct((reqs, HD, width), jnp.bfloat16),
            jax.ShapeDtypeStruct((reqs, 2, width), jnp.float32),
        ],
        compiler_params=pltpu.CompilerParams(
            dimension_semantics=("arbitrary",), vmem_limit_bytes=48 * 1024 * 1024
        ),
    )(sreq, perm, kstart, qstart, packed, pages)


def body(hidden, qkv_weight, out_weight, kv_pages, cache_pages, slot_order):
    n_tp = lax.axis_size("tp")
    copies = jnp.broadcast_to(hidden[None], (n_tp,) + hidden.shape)
    whole = lax.all_to_all(copies, "tp", 0, 0, tiled=True)
    whole = jnp.moveaxis(whole, 0, 1).reshape(hidden.shape[0], n_tp * hidden.shape[1])
    tok_rows = whole.shape[0]
    n_req = lax.axis_size("req")
    lanes = out_weight.shape[1]
    qkv_rows = qkv_weight.size // lanes
    both = jnp.concatenate([qkv_weight.reshape(qkv_rows, lanes), out_weight], axis=0)
    both = lax.all_gather(both[None], "req", axis=0, tiled=True)
    qkv_full = both[:, :qkv_rows].reshape(n_req * qkv_weight.shape[0], qkv_weight.shape[1])
    out_full = jnp.moveaxis(both[:, qkv_rows:], 0, 1).reshape(out_weight.shape[0], n_req * lanes)
    projected = jnp.dot(whole, qkv_full, preferred_element_type=jnp.float32)
    local_slots = kv_pages.shape[0]
    page_rows = kv_pages.shape[1]
    lane_width = kv_pages.shape[2]
    kv_heads = lane_width // (2 * HD)
    assert kv_heads == 1 and tok_rows == SPAN
    new_pages = SPAN // page_rows
    requests = cache_pages.shape[0]
    my_index = lax.axis_index("req")
    query_start = cache_pages * page_rows
    home_start = lax.dynamic_slice_in_dim(query_start, my_index, 1, 0)
    projected = projected.reshape(SPAN, GROUP + 2, HD)
    positions = (home_start + jnp.arange(SPAN, dtype=jnp.int32))[:, None]
    rotated = rotary(projected[:, : GROUP + 1, :], positions)
    scale = jnp.concatenate(
        [jnp.full((GROUP, 1), 1.0 / math.sqrt(HD), jnp.float32), jnp.ones((1, 1), jnp.float32)], axis=0
    )
    rotated = (rotated * scale).astype(jnp.bfloat16)
    value_new = projected[:, GROUP + 1 :, :].astype(jnp.bfloat16)
    fresh = jnp.concatenate([rotated[:, GROUP:, :], value_new], axis=1)
    halves = 2
    sub = SPAN // halves
    width = GROUP * sub
    gathered = []
    for h in range(halves):
        piece = jnp.transpose(rotated[h * sub:(h + 1) * sub, :GROUP, :], (2, 1, 0)).reshape(HD, width)
        if h == 0:
            piece = jnp.concatenate([piece, fresh.reshape(-1, width)], axis=0)
        gathered.append(lax.all_gather(piece[None], "req", axis=0, tiled=True))
    fresh_all = gathered[0][:, HD:, :].reshape(requests, SPAN, 2 * HD)

    my_slots = my_index * local_slots + jnp.arange(local_slots, dtype=jnp.int32)
    slot_req, page_index, cached = locate(my_slots, cache_pages, slot_order, new_pages)
    pages_out = write_pages(kv_pages, fresh_all, slot_req, page_index, cached, new_pages)

    perm = jnp.argsort(slot_req, stable=True).astype(jnp.int32)
    sreq = slot_req[perm].astype(jnp.int32)
    kstart = (page_index[perm] * page_rows).astype(jnp.int32)

    all_slots = jnp.arange(slot_order.shape[0], dtype=jnp.int32)
    all_req, unused_index, unused_cached = locate(all_slots, cache_pages, slot_order, new_pages)
    holds = (all_req.reshape(-1, local_slots) == my_index).any(axis=1)
    valid = holds[:, None, None]

    outs = []
    for h in range(halves):
        q_start = (query_start + h * sub).astype(jnp.int32)
        part_o, part_st = slot_attention(sreq, perm, kstart, q_start, gathered[h], pages_out, sub)
        hi = lax.reduce_precision(part_st, exponent_bits=8, mantissa_bits=7)
        rest = part_st - hi
        mid = lax.reduce_precision(rest, exponent_bits=8, mantissa_bits=7)
        lo = rest - mid
        sent = jnp.concatenate([part_o] + [t.astype(jnp.bfloat16) for t in (hi, mid, lo)], axis=1)
        got = lax.all_to_all(sent, "req", 0, 0, tiled=True)
        got_o = got[:, :HD].reshape(requests, HD, GROUP, sub)
        got_bits = got[:, HD:].reshape(requests, 3, 2, GROUP, sub).astype(jnp.float32)
        got_st = (got_bits[:, 0] + got_bits[:, 1]) + got_bits[:, 2]

        m_parts = jnp.where(valid, got_st[:, 0], NEG_BIG)
        l_parts = jnp.where(valid, got_st[:, 1], 0.0)
        top = jnp.max(m_parts, axis=0)
        w = l_parts * jnp.exp(m_parts - top[None])
        den = jnp.sum(w, axis=0)
        o_parts = jnp.where(valid[..., None], got_o.astype(jnp.float32), 0.0)
        num = jnp.sum(o_parts * w[:, None, :, :], axis=0)
        attention_t = (num / den[None]).astype(jnp.bfloat16)
        attention_flat = jnp.transpose(attention_t, (2, 1, 0)).reshape(sub, GROUP * HD)

        head_terms = jnp.dot(attention_flat, out_full, preferred_element_type=jnp.float32)
        outs.append(head_terms.astype(jnp.bfloat16))
    first_out = lax.psum_scatter(outs[0], "tp", scatter_dimension=1, tiled=True)
    partial_t = outs[1]
    cols = partial_t.shape[1] // n_tp
    partial_t = jnp.moveaxis(partial_t.reshape(partial_t.shape[0], n_tp, cols), 1, 0)
    got_t = lax.all_to_all(partial_t, "tp", 0, 0, tiled=True)
    second_out = jnp.sum(got_t.astype(jnp.float32), axis=0).astype(jnp.bfloat16)
    attention_out = jnp.concatenate([first_out, second_out], axis=0)
    return (attention_out, pages_out)


def solution(mesh):
    return jax.shard_map(
        body,
        mesh=mesh,
        in_specs=(P("req", "tp"), P("req", "tp"), P("tp", "req"), P("req", None, "tp"), P(), P()),
        out_specs=(P("req", "tp"), P("req", None, "tp")),
        check_vma=False,
    )
```

```python
import math

import jax
import jax.numpy as jnp
from jax import lax
from jax.experimental import pallas as pl
from jax.experimental.pallas import tpu as pltpu
from jax.sharding import PartitionSpec as P

HD = 64
GROUP = 4
SPAN = 512


THETA = 1000000.0
NEG_BIG = -1e30


def rotary(values, positions):
    head_width = values.shape[-1]
    half_width = head_width // 2
    inv_freq = jnp.power(THETA, -(jnp.arange(half_width, dtype=jnp.float32) * 2.0 / head_width))
    angles = positions.astype(jnp.float32)[..., None] * inv_freq
    cosines = jnp.cos(angles)
    sines = jnp.sin(angles)
    lower_half = values[..., :half_width]
    upper_half = values[..., half_width:]
    return jnp.concatenate(
        [lower_half * cosines - upper_half * sines, upper_half * cosines + lower_half * sines],
        axis=-1,
    )


def locate(slot_ids, cache_pages, slot_order, new_pages):
    requests = cache_pages.shape[0]
    slot_count = slot_order.shape[0]
    counts = cache_pages + new_pages
    page_ends = jnp.cumsum(counts)
    starts = page_ends - counts
    ranking = jnp.sum(
        jnp.where(
            slot_order[None, :] == slot_ids[:, None],
            jnp.arange(slot_count, dtype=jnp.int32)[None, :],
            0,
        ),
        axis=1,
    )
    holder = jnp.sum((starts[None, :] <= ranking[:, None]).astype(jnp.int32), axis=1) - 1
    onehot = jnp.arange(requests, dtype=jnp.int32)[None, :] == holder[:, None]
    first_page = jnp.sum(jnp.where(onehot, starts[None, :], 0), axis=1)
    cached = jnp.sum(jnp.where(onehot, cache_pages[None, :], 0), axis=1)
    return (holder, ranking - first_page, cached)


def write_pages(kv_pages, fresh, slot_req, page_index, cached, new_pages):
    page_rows = kv_pages.shape[1]
    lane_width = kv_pages.shape[2]
    fresh_pages = fresh.reshape(-1, page_rows, lane_width)
    pick = slot_req * new_pages + jnp.clip(page_index - cached, 0, new_pages - 1)
    return jnp.where((page_index >= cached)[:, None, None], fresh_pages[pick], kv_pages)


def slot_attention(sreq, perm, kstart, qstart, packed, pages, sub):
    reqs, _, width = packed.shape
    slots, page_rows, _ = pages.shape
    assert width == GROUP * sub and sub & (sub - 1) == 0

    def kernel(sreq_ref, perm_ref, kstart_ref, qstart_ref, q_ref, page_ref, o_ref, st_ref, m_sc, l_sc, acc_sc):
        i = pl.program_id(0)
        n = pl.num_programs(0)
        req = sreq_ref[i]
        prev = sreq_ref[jnp.maximum(i - 1, 0)]
        nxt = sreq_ref[jnp.minimum(i + 1, n - 1)]
        first = jnp.logical_or(i == 0, prev != req)
        last = jnp.logical_or(i == n - 1, nxt != req)

        @pl.when(first)
        def _():
            m_sc[...] = jnp.full(m_sc.shape, NEG_BIG, jnp.float32)
            l_sc[...] = jnp.zeros(l_sc.shape, jnp.float32)
            acc_sc[...] = jnp.zeros(acc_sc.shape, jnp.float32)

        kst = kstart_ref[i]
        qst = qstart_ref[req]
        page = page_ref[perm_ref[i]]
        keys = page[:, :HD]
        vals = page[:, HD:]
        q = q_ref[req]

        def update(masked):
            s = jnp.dot(keys, q, preferred_element_type=jnp.float32)
            if masked:
                key_pos = lax.broadcasted_iota(jnp.int32, (page_rows, width), 0) + kst
                token = jnp.bitwise_and(lax.broadcasted_iota(jnp.int32, (page_rows, width), 1), sub - 1)
                vis = key_pos <= token + qst
                s = jnp.where(vis, s, NEG_BIG)
            m_prev = m_sc[...]
            m_next = jnp.maximum(m_prev, jnp.max(s, axis=0, keepdims=True))
            alpha = jnp.exp(m_prev - m_next)
            p = jnp.exp(s - m_next)
            if masked:
                p = jnp.where(vis, p, 0.0)
            l_sc[...] = alpha * l_sc[...] + jnp.sum(p, axis=0, keepdims=True)
            m_sc[...] = m_next
            pv = lax.dot_general(
                vals, p.astype(jnp.bfloat16), (((0,), (0,)), ((), ())),
                preferred_element_type=jnp.float32,
            )
            acc_sc[...] = acc_sc[...] * alpha + pv

        partial = kst + (page_rows - 1) > qst

        @pl.when(partial)
        def _():
            update(True)

        @pl.when(jnp.logical_not(partial))
        def _():
            update(False)

        @pl.when(last)
        def _():
            l_all = l_sc[...]
            safe = jnp.where(l_all > 0.0, l_all, 1.0)
            o_ref[req] = (acc_sc[...] / safe).astype(o_ref.dtype)
            st_ref[req, 0:1, :] = m_sc[...]
            st_ref[req, 1:2, :] = l_all

    grid_spec = pltpu.PrefetchScalarGridSpec(
        num_scalar_prefetch=4,
        grid=(slots,),
        in_specs=[
            pl.BlockSpec((reqs, HD, width), lambda i, sr, pm, ks, qs: (0, 0, 0)),
            pl.BlockSpec((slots, page_rows, 2 * HD), lambda i, sr, pm, ks, qs: (0, 0, 0)),
        ],
        out_specs=[
            pl.BlockSpec((reqs, HD, width), lambda i, sr, pm, ks, qs: (0, 0, 0)),
            pl.BlockSpec((reqs, 2, width), lambda i, sr, pm, ks, qs: (0, 0, 0)),
        ],
        scratch_shapes=[
            pltpu.VMEM((1, width), jnp.float32),
            pltpu.VMEM((1, width), jnp.float32),
            pltpu.VMEM((HD, width), jnp.float32),
        ],
    )
    return pl.pallas_call(
        kernel,
        grid_spec=grid_spec,
        out_shape=[
            jax.ShapeDtypeStruct((reqs, HD, width), jnp.bfloat16),
            jax.ShapeDtypeStruct((reqs, 2, width), jnp.float32),
        ],
        compiler_params=pltpu.CompilerParams(
            dimension_semantics=("arbitrary",), vmem_limit_bytes=48 * 1024 * 1024
        ),
    )(sreq, perm, kstart, qstart, packed, pages)


def body(hidden, qkv_weight, out_weight, kv_pages, cache_pages, slot_order):
    n_tp = lax.axis_size("tp")
    whole = lax.all_gather(hidden, "tp", axis=1, tiled=True)
    tok_rows = whole.shape[0]
    n_req = lax.axis_size("req")
    lanes = out_weight.shape[1]
    qkv_rows = qkv_weight.size // lanes
    both = jnp.concatenate([qkv_weight.reshape(qkv_rows, lanes), out_weight], axis=0)
    both = lax.all_to_all(jnp.broadcast_to(both[None], (n_req,) + both.shape), "req", 0, 0, tiled=True)
    qkv_full = both[:, :qkv_rows].reshape(n_req * qkv_weight.shape[0], qkv_weight.shape[1])
    out_full = jnp.moveaxis(both[:, qkv_rows:], 0, 1).reshape(out_weight.shape[0], n_req * lanes)
    projected = jnp.dot(whole, qkv_full, preferred_element_type=jnp.float32)
    local_slots = kv_pages.shape[0]
    page_rows = kv_pages.shape[1]
    lane_width = kv_pages.shape[2]
    kv_heads = lane_width // (2 * HD)
    assert kv_heads == 1 and tok_rows == SPAN
    new_pages = SPAN // page_rows
    requests = cache_pages.shape[0]
    my_index = lax.axis_index("req")
    query_start = cache_pages * page_rows
    home_start = lax.dynamic_slice_in_dim(query_start, my_index, 1, 0)
    projected = projected.reshape(SPAN, GROUP + 2, HD)
    positions = (home_start + jnp.arange(SPAN, dtype=jnp.int32))[:, None]
    rotated = rotary(projected[:, : GROUP + 1, :], positions)
    scale = jnp.concatenate(
        [jnp.full((GROUP, 1), 1.0 / math.sqrt(HD), jnp.float32), jnp.ones((1, 1), jnp.float32)], axis=0
    )
    rotated = (rotated * scale).astype(jnp.bfloat16)
    value_new = projected[:, GROUP + 1 :, :].astype(jnp.bfloat16)
    fresh = jnp.concatenate([rotated[:, GROUP:, :], value_new], axis=1)
    halves = 2
    sub = SPAN // halves
    width = GROUP * sub
    gathered = []
    for h in range(halves):
        piece = jnp.transpose(rotated[h * sub:(h + 1) * sub, :GROUP, :], (2, 1, 0)).reshape(HD, width)
        if h == 0:
            piece = jnp.concatenate([piece, fresh.reshape(-1, width)], axis=0)
        gathered.append(lax.all_gather(piece[None], "req", axis=0, tiled=True))
    fresh_all = gathered[0][:, HD:, :].reshape(requests, SPAN, 2 * HD)

    my_slots = my_index * local_slots + jnp.arange(local_slots, dtype=jnp.int32)
    slot_req, page_index, cached = locate(my_slots, cache_pages, slot_order, new_pages)
    pages_out = write_pages(kv_pages, fresh_all, slot_req, page_index, cached, new_pages)

    perm = jnp.argsort(slot_req, stable=True).astype(jnp.int32)
    sreq = slot_req[perm].astype(jnp.int32)
    kstart = (page_index[perm] * page_rows).astype(jnp.int32)

    all_slots = jnp.arange(slot_order.shape[0], dtype=jnp.int32)
    all_req, unused_index, unused_cached = locate(all_slots, cache_pages, slot_order, new_pages)
    holds = (all_req.reshape(-1, local_slots) == my_index).any(axis=1)
    valid = holds[:, None, None]

    outs = []
    for h in range(halves):
        q_start = (query_start + h * sub).astype(jnp.int32)
        part_o, part_st = slot_attention(sreq, perm, kstart, q_start, gathered[h], pages_out, sub)
        hi = lax.reduce_precision(part_st, exponent_bits=8, mantissa_bits=7)
        rest = part_st - hi
        mid = lax.reduce_precision(rest, exponent_bits=8, mantissa_bits=7)
        lo = rest - mid
        sent = jnp.concatenate([part_o] + [t.astype(jnp.bfloat16) for t in (hi, mid, lo)], axis=1)
        got = lax.all_to_all(sent, "req", 0, 0, tiled=True)
        got_o = got[:, :HD].reshape(requests, HD, GROUP, sub)
        got_bits = got[:, HD:].reshape(requests, 3, 2, GROUP, sub).astype(jnp.float32)
        got_st = (got_bits[:, 0] + got_bits[:, 1]) + got_bits[:, 2]

        m_parts = jnp.where(valid, got_st[:, 0], NEG_BIG)
        l_parts = jnp.where(valid, got_st[:, 1], 0.0)
        top = jnp.max(m_parts, axis=0)
        w = l_parts * jnp.exp(m_parts - top[None])
        den = jnp.sum(w, axis=0)
        o_parts = jnp.where(valid[..., None], got_o.astype(jnp.float32), 0.0)
        num = jnp.sum(o_parts * w[:, None, :, :], axis=0)
        attention_t = (num / den[None]).astype(jnp.bfloat16)
        attention_flat = jnp.transpose(attention_t, (2, 1, 0)).reshape(sub, GROUP * HD)

        head_terms = jnp.dot(attention_flat, out_full, preferred_element_type=jnp.float32)
        outs.append(head_terms.astype(jnp.bfloat16))
    partial_t = jnp.concatenate(outs, axis=0)
    cols = partial_t.shape[1] // n_tp
    partial_t = jnp.moveaxis(partial_t.reshape(partial_t.shape[0], n_tp, cols), 1, 0)
    got_t = lax.all_to_all(partial_t, "tp", 0, 0, tiled=True)
    attention_out = jnp.sum(got_t.astype(jnp.float32), axis=0).astype(jnp.bfloat16)
    return (attention_out, pages_out)


def solution(mesh):
    return jax.shard_map(
        body,
        mesh=mesh,
        in_specs=(P("req", "tp"), P("req", "tp"), P("tp", "req"), P("req", None, "tp"), P(), P()),
        out_specs=(P("req", "tp"), P("req", None, "tp")),
        check_vma=False,
    )
```

```python
import math

import jax
import jax.numpy as jnp
from jax import lax
from jax.experimental import pallas as pl
from jax.experimental.pallas import tpu as pltpu
from jax.sharding import PartitionSpec as P

HD = 64
GROUP = 4
SPAN = 512


THETA = 1000000.0
NEG_BIG = -1e30


def rotary(values, positions):
    head_width = values.shape[-1]
    half_width = head_width // 2
    inv_freq = jnp.power(THETA, -(jnp.arange(half_width, dtype=jnp.float32) * 2.0 / head_width))
    angles = positions.astype(jnp.float32)[..., None] * inv_freq
    cosines = jnp.cos(angles)
    sines = jnp.sin(angles)
    lower_half = values[..., :half_width]
    upper_half = values[..., half_width:]
    return jnp.concatenate(
        [lower_half * cosines - upper_half * sines, upper_half * cosines + lower_half * sines],
        axis=-1,
    )


def locate(slot_ids, cache_pages, slot_order, new_pages):
    requests = cache_pages.shape[0]
    slot_count = slot_order.shape[0]
    counts = cache_pages + new_pages
    page_ends = jnp.cumsum(counts)
    starts = page_ends - counts
    ranking = jnp.sum(
        jnp.where(
            slot_order[None, :] == slot_ids[:, None],
            jnp.arange(slot_count, dtype=jnp.int32)[None, :],
            0,
        ),
        axis=1,
    )
    holder = jnp.sum((starts[None, :] <= ranking[:, None]).astype(jnp.int32), axis=1) - 1
    onehot = jnp.arange(requests, dtype=jnp.int32)[None, :] == holder[:, None]
    first_page = jnp.sum(jnp.where(onehot, starts[None, :], 0), axis=1)
    cached = jnp.sum(jnp.where(onehot, cache_pages[None, :], 0), axis=1)
    return (holder, ranking - first_page, cached)


def write_pages(kv_pages, fresh, slot_req, page_index, cached, new_pages):
    page_rows = kv_pages.shape[1]
    lane_width = kv_pages.shape[2]
    fresh_pages = fresh.reshape(-1, page_rows, lane_width)
    pick = slot_req * new_pages + jnp.clip(page_index - cached, 0, new_pages - 1)
    return jnp.where((page_index >= cached)[:, None, None], fresh_pages[pick], kv_pages)


def slot_attention(sreq, perm, kstart, qstart, packed, pages, sub):
    reqs, _, width = packed.shape
    slots, page_rows, _ = pages.shape
    assert width == GROUP * sub and sub & (sub - 1) == 0

    assert slots % 2 == 0

    def kernel(sreq_ref, perm_ref, kstart_ref, qstart_ref, q_ref, page_ref, o_ref, st_ref, m_sc, l_sc, acc_sc):
        j = pl.program_id(0)
        a = 2 * j
        b = a + 1
        req_a = sreq_ref[a]
        req_b = sreq_ref[b]
        first_a = jnp.logical_or(a == 0, sreq_ref[jnp.maximum(a - 1, 0)] != req_a)
        last_b = jnp.logical_or(b == slots - 1, sreq_ref[jnp.minimum(b + 1, slots - 1)] != req_b)
        same = req_a == req_b
        kst_a = kstart_ref[a]
        kst_b = kstart_ref[b]
        page_a = page_ref[perm_ref[a]]
        page_b = page_ref[perm_ref[b]]

        def init():
            m_sc[...] = jnp.full(m_sc.shape, NEG_BIG, jnp.float32)
            l_sc[...] = jnp.zeros(l_sc.shape, jnp.float32)
            acc_sc[...] = jnp.zeros(acc_sc.shape, jnp.float32)

        def finish(req):
            l_all = l_sc[...]
            safe = jnp.where(l_all > 0.0, l_all, 1.0)
            o_ref[req] = (acc_sc[...] / safe).astype(o_ref.dtype)
            st_ref[req, 0:1, :] = m_sc[...]
            st_ref[req, 1:2, :] = l_all

        def update(items, req, masked):
            q = q_ref[req]
            qst = qstart_ref[req]
            if masked:
                token = jnp.bitwise_and(lax.broadcasted_iota(jnp.int32, (page_rows, width), 1), sub - 1) + qst
                row = lax.broadcasted_iota(jnp.int32, (page_rows, width), 0)
            scores = []
            for page, kst in items:
                sc = jnp.dot(page[:, :HD], q, preferred_element_type=jnp.float32)
                vis = None
                if masked:
                    vis = row + kst <= token
                    sc = jnp.where(vis, sc, NEG_BIG)
                scores.append((sc, vis))
            m_prev = m_sc[...]
            m_cur = jnp.max(scores[0][0], axis=0, keepdims=True)
            for sc, vis in scores[1:]:
                m_cur = jnp.maximum(m_cur, jnp.max(sc, axis=0, keepdims=True))
            m_next = jnp.maximum(m_prev, m_cur)
            alpha = jnp.exp(m_prev - m_next)
            l_add = None
            pv = None
            for (sc, vis), (page, kst) in zip(scores, items):
                p = jnp.exp(sc - m_next)
                if masked:
                    p = jnp.where(vis, p, 0.0)
                part_l = jnp.sum(p, axis=0, keepdims=True)
                part_pv = lax.dot_general(
                    page[:, HD:], p.astype(jnp.bfloat16), (((0,), (0,)), ((), ())),
                    preferred_element_type=jnp.float32,
                )
                l_add = part_l if l_add is None else l_add + part_l
                pv = part_pv if pv is None else pv + part_pv
            l_sc[...] = alpha * l_sc[...] + l_add
            m_sc[...] = m_next
            acc_sc[...] = acc_sc[...] * alpha + pv

        partial_a = kst_a + (page_rows - 1) > qstart_ref[req_a]
        partial_b = kst_b + (page_rows - 1) > qstart_ref[req_b]
        pair = [(page_a, kst_a), (page_b, kst_b)]

        @pl.when(first_a)
        def _():
            init()

        @pl.when(jnp.logical_and(same, jnp.logical_or(partial_a, partial_b)))
        def _():
            update(pair, req_a, True)

        @pl.when(jnp.logical_and(same, jnp.logical_not(jnp.logical_or(partial_a, partial_b))))
        def _():
            update(pair, req_a, False)

        @pl.when(jnp.logical_not(same))
        def _():
            update(pair[:1], req_a, True)
            finish(req_a)
            init()
            update(pair[1:], req_b, True)

        @pl.when(last_b)
        def _():
            finish(req_b)

    grid_spec = pltpu.PrefetchScalarGridSpec(
        num_scalar_prefetch=4,
        grid=(slots // 2,),
        in_specs=[
            pl.BlockSpec((reqs, HD, width), lambda i, sr, pm, ks, qs: (0, 0, 0)),
            pl.BlockSpec((slots, page_rows, 2 * HD), lambda i, sr, pm, ks, qs: (0, 0, 0)),
        ],
        out_specs=[
            pl.BlockSpec((reqs, HD, width), lambda i, sr, pm, ks, qs: (0, 0, 0)),
            pl.BlockSpec((reqs, 2, width), lambda i, sr, pm, ks, qs: (0, 0, 0)),
        ],
        scratch_shapes=[
            pltpu.VMEM((1, width), jnp.float32),
            pltpu.VMEM((1, width), jnp.float32),
            pltpu.VMEM((HD, width), jnp.float32),
        ],
    )
    return pl.pallas_call(
        kernel,
        grid_spec=grid_spec,
        out_shape=[
            jax.ShapeDtypeStruct((reqs, HD, width), jnp.bfloat16),
            jax.ShapeDtypeStruct((reqs, 2, width), jnp.float32),
        ],
        compiler_params=pltpu.CompilerParams(
            dimension_semantics=("arbitrary",), vmem_limit_bytes=48 * 1024 * 1024
        ),
    )(sreq, perm, kstart, qstart, packed, pages)


def body(hidden, qkv_weight, out_weight, kv_pages, cache_pages, slot_order):
    n_tp = lax.axis_size("tp")
    whole = lax.all_gather(hidden, "tp", axis=1, tiled=True)
    tok_rows = whole.shape[0]
    n_req = lax.axis_size("req")
    lanes = out_weight.shape[1]
    qkv_rows = qkv_weight.size // lanes
    both = jnp.concatenate([qkv_weight.reshape(qkv_rows, lanes), out_weight], axis=0)
    both = lax.all_to_all(jnp.broadcast_to(both[None], (n_req,) + both.shape), "req", 0, 0, tiled=True)
    qkv_full = both[:, :qkv_rows].reshape(n_req * qkv_weight.shape[0], qkv_weight.shape[1])
    out_full = jnp.moveaxis(both[:, qkv_rows:], 0, 1).reshape(out_weight.shape[0], n_req * lanes)
    projected = jnp.dot(whole, qkv_full, preferred_element_type=jnp.float32)
    local_slots = kv_pages.shape[0]
    page_rows = kv_pages.shape[1]
    lane_width = kv_pages.shape[2]
    kv_heads = lane_width // (2 * HD)
    assert kv_heads == 1 and tok_rows == SPAN
    new_pages = SPAN // page_rows
    requests = cache_pages.shape[0]
    my_index = lax.axis_index("req")
    query_start = cache_pages * page_rows
    home_start = lax.dynamic_slice_in_dim(query_start, my_index, 1, 0)
    projected = projected.reshape(SPAN, GROUP + 2, HD)
    positions = (home_start + jnp.arange(SPAN, dtype=jnp.int32))[:, None]
    rotated = rotary(projected[:, : GROUP + 1, :], positions)
    scale = jnp.concatenate(
        [jnp.full((GROUP, 1), 1.0 / math.sqrt(HD), jnp.float32), jnp.ones((1, 1), jnp.float32)], axis=0
    )
    rotated = (rotated * scale).astype(jnp.bfloat16)
    value_new = projected[:, GROUP + 1 :, :].astype(jnp.bfloat16)
    fresh = jnp.concatenate([rotated[:, GROUP:, :], value_new], axis=1)
    halves = 2
    sub = SPAN // halves
    width = GROUP * sub
    gathered = []
    for h in range(halves):
        piece = jnp.transpose(rotated[h * sub:(h + 1) * sub, :GROUP, :], (2, 1, 0)).reshape(HD, width)
        if h == 0:
            piece = jnp.concatenate([piece, fresh.reshape(-1, width)], axis=0)
        gathered.append(lax.all_gather(piece[None], "req", axis=0, tiled=True))
    fresh_all = gathered[0][:, HD:, :].reshape(requests, SPAN, 2 * HD)

    my_slots = my_index * local_slots + jnp.arange(local_slots, dtype=jnp.int32)
    slot_req, page_index, cached = locate(my_slots, cache_pages, slot_order, new_pages)
    pages_out = write_pages(kv_pages, fresh_all, slot_req, page_index, cached, new_pages)

    perm = jnp.argsort(slot_req, stable=True).astype(jnp.int32)
    sreq = slot_req[perm].astype(jnp.int32)
    kstart = (page_index[perm] * page_rows).astype(jnp.int32)

    all_slots = jnp.arange(slot_order.shape[0], dtype=jnp.int32)
    all_req, unused_index, unused_cached = locate(all_slots, cache_pages, slot_order, new_pages)
    holds = (all_req.reshape(-1, local_slots) == my_index).any(axis=1)
    valid = holds[:, None, None]

    outs = []
    for h in range(halves):
        q_start = (query_start + h * sub).astype(jnp.int32)
        part_o, part_st = slot_attention(sreq, perm, kstart, q_start, gathered[h], pages_out, sub)
        hi = lax.reduce_precision(part_st, exponent_bits=8, mantissa_bits=7)
        rest = part_st - hi
        mid = lax.reduce_precision(rest, exponent_bits=8, mantissa_bits=7)
        lo = rest - mid
        sent = jnp.concatenate([part_o] + [t.astype(jnp.bfloat16) for t in (hi, mid, lo)], axis=1)
        got = lax.all_to_all(sent, "req", 0, 0, tiled=True)
        got_o = got[:, :HD].reshape(requests, HD, GROUP, sub)
        got_bits = got[:, HD:].reshape(requests, 3, 2, GROUP, sub).astype(jnp.float32)
        got_st = (got_bits[:, 0] + got_bits[:, 1]) + got_bits[:, 2]

        m_parts = jnp.where(valid, got_st[:, 0], NEG_BIG)
        l_parts = jnp.where(valid, got_st[:, 1], 0.0)
        top = jnp.max(m_parts, axis=0)
        w = l_parts * jnp.exp(m_parts - top[None])
        den = jnp.sum(w, axis=0)
        o_parts = jnp.where(valid[..., None], got_o.astype(jnp.float32), 0.0)
        num = jnp.sum(o_parts * w[:, None, :, :], axis=0)
        attention_t = (num / den[None]).astype(jnp.bfloat16)
        attention_flat = jnp.transpose(attention_t, (2, 1, 0)).reshape(sub, GROUP * HD)

        head_terms = jnp.dot(attention_flat, out_full, preferred_element_type=jnp.float32)
        outs.append(head_terms.astype(jnp.bfloat16))
    partial_t = jnp.concatenate(outs, axis=0)
    cols = partial_t.shape[1] // n_tp
    partial_t = jnp.moveaxis(partial_t.reshape(partial_t.shape[0], n_tp, cols), 1, 0)
    got_t = lax.all_to_all(partial_t, "tp", 0, 0, tiled=True)
    attention_out = jnp.sum(got_t.astype(jnp.float32), axis=0).astype(jnp.bfloat16)
    return (attention_out, pages_out)


def solution(mesh):
    return jax.shard_map(
        body,
        mesh=mesh,
        in_specs=(P("req", "tp"), P("req", "tp"), P("tp", "req"), P("req", None, "tp"), P(), P()),
        out_specs=(P("req", "tp"), P("req", None, "tp")),
        check_vma=False,
    )
```

```python
import math

import jax
import jax.numpy as jnp
from jax import lax
from jax.experimental import pallas as pl
from jax.experimental.pallas import tpu as pltpu
from jax.sharding import PartitionSpec as P

HD = 64
GROUP = 4
SPAN = 512


THETA = 1000000.0
NEG_BIG = -1e30


def rotary(values, positions):
    head_width = values.shape[-1]
    half_width = head_width // 2
    inv_freq = jnp.power(THETA, -(jnp.arange(half_width, dtype=jnp.float32) * 2.0 / head_width))
    angles = positions.astype(jnp.float32)[..., None] * inv_freq
    cosines = jnp.cos(angles)
    sines = jnp.sin(angles)
    lower_half = values[..., :half_width]
    upper_half = values[..., half_width:]
    return jnp.concatenate(
        [lower_half * cosines - upper_half * sines, upper_half * cosines + lower_half * sines],
        axis=-1,
    )


def locate(slot_ids, cache_pages, slot_order, new_pages):
    requests = cache_pages.shape[0]
    slot_count = slot_order.shape[0]
    counts = cache_pages + new_pages
    page_ends = jnp.cumsum(counts)
    starts = page_ends - counts
    ranking = jnp.sum(
        jnp.where(
            slot_order[None, :] == slot_ids[:, None],
            jnp.arange(slot_count, dtype=jnp.int32)[None, :],
            0,
        ),
        axis=1,
    )
    holder = jnp.sum((starts[None, :] <= ranking[:, None]).astype(jnp.int32), axis=1) - 1
    onehot = jnp.arange(requests, dtype=jnp.int32)[None, :] == holder[:, None]
    first_page = jnp.sum(jnp.where(onehot, starts[None, :], 0), axis=1)
    cached = jnp.sum(jnp.where(onehot, cache_pages[None, :], 0), axis=1)
    return (holder, ranking - first_page, cached)


def write_pages(kv_pages, fresh, slot_req, page_index, cached, new_pages):
    page_rows = kv_pages.shape[1]
    lane_width = kv_pages.shape[2]
    fresh_pages = fresh.reshape(-1, page_rows, lane_width)
    pick = slot_req * new_pages + jnp.clip(page_index - cached, 0, new_pages - 1)
    return jnp.where((page_index >= cached)[:, None, None], fresh_pages[pick], kv_pages)


def slot_attention(sreq, perm, kstart, qstart, packed, pages, sub):
    reqs, _, width = packed.shape
    slots, page_rows, _ = pages.shape
    assert width == GROUP * sub and sub & (sub - 1) == 0

    assert slots % 2 == 0

    def kernel(sreq_ref, perm_ref, kstart_ref, qstart_ref, q_ref, page_ref, o_ref, st_ref, m_sc, l_sc, acc_sc):
        j = pl.program_id(0)
        a = 2 * j
        b = a + 1
        req_a = sreq_ref[a]
        req_b = sreq_ref[b]
        first_a = jnp.logical_or(a == 0, sreq_ref[jnp.maximum(a - 1, 0)] != req_a)
        last_b = jnp.logical_or(b == slots - 1, sreq_ref[jnp.minimum(b + 1, slots - 1)] != req_b)
        same = req_a == req_b
        kst_a = kstart_ref[a]
        kst_b = kstart_ref[b]
        page_a = page_ref[perm_ref[a]]
        page_b = page_ref[perm_ref[b]]

        def init():
            m_sc[...] = jnp.full(m_sc.shape, NEG_BIG, jnp.float32)
            l_sc[...] = jnp.zeros(l_sc.shape, jnp.float32)
            acc_sc[...] = jnp.zeros(acc_sc.shape, jnp.float32)

        def finish(req):
            l_all = l_sc[...]
            safe = jnp.where(l_all > 0.0, l_all, 1.0)
            o_ref[req] = (acc_sc[...] / safe).astype(o_ref.dtype)
            st_ref[req, 0:1, :] = m_sc[...]
            st_ref[req, 1:2, :] = l_all

        def update(items, req, masked):
            q = q_ref[req]
            qst = qstart_ref[req]
            if masked:
                token = jnp.bitwise_and(lax.broadcasted_iota(jnp.int32, (page_rows, width), 1), sub - 1) + qst
                row = lax.broadcasted_iota(jnp.int32, (page_rows, width), 0)
            scores = []
            for page, kst in items:
                sc = jnp.dot(page[:, :HD], q, preferred_element_type=jnp.float32)
                vis = None
                if masked:
                    vis = row + kst <= token
                    sc = jnp.where(vis, sc, NEG_BIG)
                scores.append((sc, vis))
            m_prev = m_sc[...]
            m_cur = jnp.max(scores[0][0], axis=0, keepdims=True)
            for sc, vis in scores[1:]:
                m_cur = jnp.maximum(m_cur, jnp.max(sc, axis=0, keepdims=True))
            m_next = jnp.maximum(m_prev, m_cur)
            alpha = jnp.exp(m_prev - m_next)
            l_add = None
            pv = None
            for (sc, vis), (page, kst) in zip(scores, items):
                p = jnp.exp(sc - m_next)
                if masked:
                    p = jnp.where(vis, p, 0.0)
                part_l = jnp.sum(p, axis=0, keepdims=True)
                part_pv = lax.dot_general(
                    page[:, HD:], p.astype(jnp.bfloat16), (((0,), (0,)), ((), ())),
                    preferred_element_type=jnp.float32,
                )
                l_add = part_l if l_add is None else l_add + part_l
                pv = part_pv if pv is None else pv + part_pv
            l_sc[...] = alpha * l_sc[...] + l_add
            m_sc[...] = m_next
            acc_sc[...] = acc_sc[...] * alpha + pv

        partial_a = kst_a + (page_rows - 1) > qstart_ref[req_a]
        partial_b = kst_b + (page_rows - 1) > qstart_ref[req_b]
        pair = [(page_a, kst_a), (page_b, kst_b)]

        @pl.when(first_a)
        def _():
            init()

        @pl.when(jnp.logical_and(same, jnp.logical_or(partial_a, partial_b)))
        def _():
            update(pair, req_a, True)

        @pl.when(jnp.logical_and(same, jnp.logical_not(jnp.logical_or(partial_a, partial_b))))
        def _():
            update(pair, req_a, False)

        @pl.when(jnp.logical_not(same))
        def _():
            update(pair[:1], req_a, True)
            finish(req_a)
            init()
            update(pair[1:], req_b, True)

        @pl.when(last_b)
        def _():
            finish(req_b)

    grid_spec = pltpu.PrefetchScalarGridSpec(
        num_scalar_prefetch=4,
        grid=(slots // 2,),
        in_specs=[
            pl.BlockSpec((reqs, HD, width), lambda i, sr, pm, ks, qs: (0, 0, 0)),
            pl.BlockSpec((slots, page_rows, 2 * HD), lambda i, sr, pm, ks, qs: (0, 0, 0)),
        ],
        out_specs=[
            pl.BlockSpec((reqs, HD, width), lambda i, sr, pm, ks, qs: (0, 0, 0)),
            pl.BlockSpec((reqs, 2, width), lambda i, sr, pm, ks, qs: (0, 0, 0)),
        ],
        scratch_shapes=[
            pltpu.VMEM((1, width), jnp.float32),
            pltpu.VMEM((1, width), jnp.float32),
            pltpu.VMEM((HD, width), jnp.float32),
        ],
    )
    return pl.pallas_call(
        kernel,
        grid_spec=grid_spec,
        out_shape=[
            jax.ShapeDtypeStruct((reqs, HD, width), jnp.bfloat16),
            jax.ShapeDtypeStruct((reqs, 2, width), jnp.float32),
        ],
        compiler_params=pltpu.CompilerParams(
            dimension_semantics=("arbitrary",), vmem_limit_bytes=48 * 1024 * 1024
        ),
    )(sreq, perm, kstart, qstart, packed, pages)


def body(hidden, qkv_weight, out_weight, kv_pages, cache_pages, slot_order):
    n_tp = lax.axis_size("tp")
    whole = lax.all_gather(hidden, "tp", axis=1, tiled=True)
    tok_rows = whole.shape[0]
    n_req = lax.axis_size("req")
    lanes = out_weight.shape[1]
    qkv_rows = qkv_weight.size // lanes
    both = jnp.concatenate([qkv_weight.reshape(qkv_rows, lanes), out_weight], axis=0)
    both = lax.all_to_all(jnp.broadcast_to(both[None], (n_req,) + both.shape), "req", 0, 0, tiled=True)
    qkv_full = both[:, :qkv_rows].reshape(n_req * qkv_weight.shape[0], qkv_weight.shape[1])
    out_full = jnp.moveaxis(both[:, qkv_rows:], 0, 1).reshape(out_weight.shape[0], n_req * lanes)
    projected = jnp.dot(whole, qkv_full, preferred_element_type=jnp.float32)
    local_slots = kv_pages.shape[0]
    page_rows = kv_pages.shape[1]
    lane_width = kv_pages.shape[2]
    kv_heads = lane_width // (2 * HD)
    assert kv_heads == 1 and tok_rows == SPAN
    new_pages = SPAN // page_rows
    requests = cache_pages.shape[0]
    my_index = lax.axis_index("req")
    query_start = cache_pages * page_rows
    home_start = lax.dynamic_slice_in_dim(query_start, my_index, 1, 0)
    projected = projected.reshape(SPAN, GROUP + 2, HD)
    positions = (home_start + jnp.arange(SPAN, dtype=jnp.int32))[:, None]
    rotated = rotary(projected[:, : GROUP + 1, :], positions)
    scale = jnp.concatenate(
        [jnp.full((GROUP, 1), 1.0 / math.sqrt(HD), jnp.float32), jnp.ones((1, 1), jnp.float32)], axis=0
    )
    rotated = (rotated * scale).astype(jnp.bfloat16)
    value_new = projected[:, GROUP + 1 :, :].astype(jnp.bfloat16)
    fresh = jnp.concatenate([rotated[:, GROUP:, :], value_new], axis=1)
    halves = 2
    sub = SPAN // halves
    width = GROUP * sub
    gathered = []
    for h in range(halves):
        piece = jnp.transpose(rotated[h * sub:(h + 1) * sub, :GROUP, :], (2, 1, 0)).reshape(HD, width)
        if h == 0:
            piece = jnp.concatenate([piece, fresh.reshape(-1, width)], axis=0)
        if h == 0:
            gathered.append(lax.all_gather(piece[None], "req", axis=0, tiled=True))
        else:
            copies = jnp.broadcast_to(piece[None], (n_req,) + piece.shape)
            gathered.append(lax.all_to_all(copies, "req", 0, 0, tiled=True))
    fresh_all = gathered[0][:, HD:, :].reshape(requests, SPAN, 2 * HD)

    my_slots = my_index * local_slots + jnp.arange(local_slots, dtype=jnp.int32)
    slot_req, page_index, cached = locate(my_slots, cache_pages, slot_order, new_pages)
    pages_out = write_pages(kv_pages, fresh_all, slot_req, page_index, cached, new_pages)

    perm = jnp.argsort(slot_req, stable=True).astype(jnp.int32)
    sreq = slot_req[perm].astype(jnp.int32)
    kstart = (page_index[perm] * page_rows).astype(jnp.int32)

    all_slots = jnp.arange(slot_order.shape[0], dtype=jnp.int32)
    all_req, unused_index, unused_cached = locate(all_slots, cache_pages, slot_order, new_pages)
    holds = (all_req.reshape(-1, local_slots) == my_index).any(axis=1)
    valid = holds[:, None, None]

    outs = []
    for h in range(halves):
        q_start = (query_start + h * sub).astype(jnp.int32)
        part_o, part_st = slot_attention(sreq, perm, kstart, q_start, gathered[h], pages_out, sub)
        hi = lax.reduce_precision(part_st, exponent_bits=8, mantissa_bits=7)
        rest = part_st - hi
        mid = lax.reduce_precision(rest, exponent_bits=8, mantissa_bits=7)
        lo = rest - mid
        sent = jnp.concatenate([part_o] + [t.astype(jnp.bfloat16) for t in (hi, mid, lo)], axis=1)
        got = lax.all_to_all(sent, "req", 0, 0, tiled=True)
        got_o = got[:, :HD].reshape(requests, HD, GROUP, sub)
        got_bits = got[:, HD:].reshape(requests, 3, 2, GROUP, sub).astype(jnp.float32)
        got_st = (got_bits[:, 0] + got_bits[:, 1]) + got_bits[:, 2]

        m_parts = jnp.where(valid, got_st[:, 0], NEG_BIG)
        l_parts = jnp.where(valid, got_st[:, 1], 0.0)
        top = jnp.max(m_parts, axis=0)
        w = l_parts * jnp.exp(m_parts - top[None])
        den = jnp.sum(w, axis=0)
        o_parts = jnp.where(valid[..., None], got_o.astype(jnp.float32), 0.0)
        num = jnp.sum(o_parts * w[:, None, :, :], axis=0)
        attention_t = (num / den[None]).astype(jnp.bfloat16)
        attention_flat = jnp.transpose(attention_t, (2, 1, 0)).reshape(sub, GROUP * HD)

        head_terms = jnp.dot(attention_flat, out_full, preferred_element_type=jnp.float32)
        outs.append(head_terms.astype(jnp.bfloat16))
    partial_t = jnp.concatenate(outs, axis=0)
    cols = partial_t.shape[1] // n_tp
    partial_t = jnp.moveaxis(partial_t.reshape(partial_t.shape[0], n_tp, cols), 1, 0)
    got_t = lax.all_to_all(partial_t, "tp", 0, 0, tiled=True)
    attention_out = jnp.sum(got_t.astype(jnp.float32), axis=0).astype(jnp.bfloat16)
    return (attention_out, pages_out)


def solution(mesh):
    return jax.shard_map(
        body,
        mesh=mesh,
        in_specs=(P("req", "tp"), P("req", "tp"), P("tp", "req"), P("req", None, "tp"), P(), P()),
        out_specs=(P("req", "tp"), P("req", None, "tp")),
        check_vma=False,
    )
```

```python
import math

import jax
import jax.numpy as jnp
from jax import lax
from jax.experimental import pallas as pl
from jax.experimental.pallas import tpu as pltpu
from jax.sharding import PartitionSpec as P

HD = 64
GROUP = 4
SPAN = 512


THETA = 1000000.0
NEG_BIG = -1e30


def rotary(values, positions):
    head_width = values.shape[-1]
    half_width = head_width // 2
    inv_freq = jnp.power(THETA, -(jnp.arange(half_width, dtype=jnp.float32) * 2.0 / head_width))
    angles = positions.astype(jnp.float32)[..., None] * inv_freq
    cosines = jnp.cos(angles)
    sines = jnp.sin(angles)
    lower_half = values[..., :half_width]
    upper_half = values[..., half_width:]
    return jnp.concatenate(
        [lower_half * cosines - upper_half * sines, upper_half * cosines + lower_half * sines],
        axis=-1,
    )


def locate(slot_ids, cache_pages, slot_order, new_pages):
    requests = cache_pages.shape[0]
    slot_count = slot_order.shape[0]
    counts = cache_pages + new_pages
    page_ends = jnp.cumsum(counts)
    starts = page_ends - counts
    ranking = jnp.sum(
        jnp.where(
            slot_order[None, :] == slot_ids[:, None],
            jnp.arange(slot_count, dtype=jnp.int32)[None, :],
            0,
        ),
        axis=1,
    )
    holder = jnp.sum((starts[None, :] <= ranking[:, None]).astype(jnp.int32), axis=1) - 1
    onehot = jnp.arange(requests, dtype=jnp.int32)[None, :] == holder[:, None]
    first_page = jnp.sum(jnp.where(onehot, starts[None, :], 0), axis=1)
    cached = jnp.sum(jnp.where(onehot, cache_pages[None, :], 0), axis=1)
    return (holder, ranking - first_page, cached)


def write_pages(kv_pages, fresh, slot_req, page_index, cached, new_pages):
    page_rows = kv_pages.shape[1]
    lane_width = kv_pages.shape[2]
    fresh_pages = fresh.reshape(-1, page_rows, lane_width)
    pick = slot_req * new_pages + jnp.clip(page_index - cached, 0, new_pages - 1)
    return jnp.where((page_index >= cached)[:, None, None], fresh_pages[pick], kv_pages)


def slot_attention(sreq, perm, kstart, qstart, packed, pages, sub):
    reqs, _, width = packed.shape
    slots, page_rows, _ = pages.shape
    assert width == GROUP * sub and sub & (sub - 1) == 0

    assert slots % 4 == 0

    def kernel(sreq_ref, perm_ref, kstart_ref, qstart_ref, q_ref, page_ref, o_ref, st_ref, m_sc, l_sc, acc_sc):
        j = pl.program_id(0)

        def init():
            m_sc[...] = jnp.full(m_sc.shape, NEG_BIG, jnp.float32)
            l_sc[...] = jnp.zeros(l_sc.shape, jnp.float32)
            acc_sc[...] = jnp.zeros(acc_sc.shape, jnp.float32)

        def finish(req):
            l_all = l_sc[...]
            safe = jnp.where(l_all > 0.0, l_all, 1.0)
            o_ref[req] = (acc_sc[...] / safe).astype(o_ref.dtype)
            st_ref[req, 0:1, :] = m_sc[...]
            st_ref[req, 1:2, :] = l_all

        def update(items, req, masked):
            q = q_ref[req]
            qst = qstart_ref[req]
            if masked:
                token = jnp.bitwise_and(lax.broadcasted_iota(jnp.int32, (page_rows, width), 1), sub - 1) + qst
                row = lax.broadcasted_iota(jnp.int32, (page_rows, width), 0)
            scores = []
            for page, kst in items:
                sc = jnp.dot(page[:, :HD], q, preferred_element_type=jnp.float32)
                vis = None
                if masked:
                    vis = row + kst <= token
                    sc = jnp.where(vis, sc, NEG_BIG)
                scores.append((sc, vis))
            m_prev = m_sc[...]
            m_cur = jnp.max(scores[0][0], axis=0, keepdims=True)
            for sc, vis in scores[1:]:
                m_cur = jnp.maximum(m_cur, jnp.max(sc, axis=0, keepdims=True))
            m_next = jnp.maximum(m_prev, m_cur)
            alpha = jnp.exp(m_prev - m_next)
            l_add = None
            pv = None
            for (sc, vis), (page, kst) in zip(scores, items):
                p = jnp.exp(sc - m_next)
                if masked:
                    p = jnp.where(vis, p, 0.0)
                part_l = jnp.sum(p, axis=0, keepdims=True)
                part_pv = lax.dot_general(
                    page[:, HD:], p.astype(jnp.bfloat16), (((0,), (0,)), ((), ())),
                    preferred_element_type=jnp.float32,
                )
                l_add = part_l if l_add is None else l_add + part_l
                pv = part_pv if pv is None else pv + part_pv
            l_sc[...] = alpha * l_sc[...] + l_add
            m_sc[...] = m_next
            acc_sc[...] = acc_sc[...] * alpha + pv

        def item(k):
            return (page_ref[perm_ref[k]], kstart_ref[k])

        def partial_of(k):
            return kstart_ref[k] + (page_rows - 1) > qstart_ref[sreq_ref[k]]

        def is_first(k):
            return jnp.logical_or(k == 0, sreq_ref[jnp.maximum(k - 1, 0)] != sreq_ref[k])

        def is_last(k):
            return jnp.logical_or(k == slots - 1, sreq_ref[jnp.minimum(k + 1, slots - 1)] != sreq_ref[k])

        def pair_step(a):
            b = a + 1
            req_a = sreq_ref[a]
            req_b = sreq_ref[b]
            same = req_a == req_b
            pair = [item(a), item(b)]
            masked = jnp.logical_or(partial_of(a), partial_of(b))

            @pl.when(is_first(a))
            def _():
                init()

            @pl.when(jnp.logical_and(same, masked))
            def _():
                update(pair, req_a, True)

            @pl.when(jnp.logical_and(same, jnp.logical_not(masked)))
            def _():
                update(pair, req_a, False)

            @pl.when(jnp.logical_not(same))
            def _():
                update(pair[:1], req_a, True)
                finish(req_a)
                init()
                update(pair[1:], req_b, True)

            @pl.when(is_last(b))
            def _():
                finish(req_b)

        a = 4 * j
        req = sreq_ref[a]
        whole = req == sreq_ref[a + 3]
        quad_masked = partial_of(a)
        for k in range(1, 4):
            quad_masked = jnp.logical_or(quad_masked, partial_of(a + k))

        @pl.when(whole)
        def _():
            quad = [item(a + k) for k in range(4)]

            @pl.when(is_first(a))
            def _():
                init()

            @pl.when(quad_masked)
            def _():
                update(quad, req, True)

            @pl.when(jnp.logical_not(quad_masked))
            def _():
                update(quad, req, False)

            @pl.when(is_last(a + 3))
            def _():
                finish(req)

        @pl.when(jnp.logical_not(whole))
        def _():
            pair_step(a)
            pair_step(a + 2)

    grid_spec = pltpu.PrefetchScalarGridSpec(
        num_scalar_prefetch=4,
        grid=(slots // 4,),
        in_specs=[
            pl.BlockSpec((reqs, HD, width), lambda i, sr, pm, ks, qs: (0, 0, 0)),
            pl.BlockSpec((slots, page_rows, 2 * HD), lambda i, sr, pm, ks, qs: (0, 0, 0)),
        ],
        out_specs=[
            pl.BlockSpec((reqs, HD, width), lambda i, sr, pm, ks, qs: (0, 0, 0)),
            pl.BlockSpec((reqs, 2, width), lambda i, sr, pm, ks, qs: (0, 0, 0)),
        ],
        scratch_shapes=[
            pltpu.VMEM((1, width), jnp.float32),
            pltpu.VMEM((1, width), jnp.float32),
            pltpu.VMEM((HD, width), jnp.float32),
        ],
    )
    return pl.pallas_call(
        kernel,
        grid_spec=grid_spec,
        out_shape=[
            jax.ShapeDtypeStruct((reqs, HD, width), jnp.bfloat16),
            jax.ShapeDtypeStruct((reqs, 2, width), jnp.float32),
        ],
        compiler_params=pltpu.CompilerParams(
            dimension_semantics=("arbitrary",), vmem_limit_bytes=48 * 1024 * 1024
        ),
    )(sreq, perm, kstart, qstart, packed, pages)


def body(hidden, qkv_weight, out_weight, kv_pages, cache_pages, slot_order):
    n_tp = lax.axis_size("tp")
    whole = lax.all_gather(hidden, "tp", axis=1, tiled=True)
    tok_rows = whole.shape[0]
    n_req = lax.axis_size("req")
    lanes = out_weight.shape[1]
    qkv_rows = qkv_weight.size // lanes
    both = jnp.concatenate([qkv_weight.reshape(qkv_rows, lanes), out_weight], axis=0)
    both = lax.all_to_all(jnp.broadcast_to(both[None], (n_req,) + both.shape), "req", 0, 0, tiled=True)
    qkv_full = both[:, :qkv_rows].reshape(n_req * qkv_weight.shape[0], qkv_weight.shape[1])
    out_full = jnp.moveaxis(both[:, qkv_rows:], 0, 1).reshape(out_weight.shape[0], n_req * lanes)
    projected = jnp.dot(whole, qkv_full, preferred_element_type=jnp.float32)
    local_slots = kv_pages.shape[0]
    page_rows = kv_pages.shape[1]
    lane_width = kv_pages.shape[2]
    kv_heads = lane_width // (2 * HD)
    assert kv_heads == 1 and tok_rows == SPAN
    new_pages = SPAN // page_rows
    requests = cache_pages.shape[0]
    my_index = lax.axis_index("req")
    query_start = cache_pages * page_rows
    home_start = lax.dynamic_slice_in_dim(query_start, my_index, 1, 0)
    projected = projected.reshape(SPAN, GROUP + 2, HD)
    positions = (home_start + jnp.arange(SPAN, dtype=jnp.int32))[:, None]
    rotated = rotary(projected[:, : GROUP + 1, :], positions)
    scale = jnp.concatenate(
        [jnp.full((GROUP, 1), 1.0 / math.sqrt(HD), jnp.float32), jnp.ones((1, 1), jnp.float32)], axis=0
    )
    rotated = (rotated * scale).astype(jnp.bfloat16)
    value_new = projected[:, GROUP + 1 :, :].astype(jnp.bfloat16)
    fresh = jnp.concatenate([rotated[:, GROUP:, :], value_new], axis=1)
    halves = 2
    sub = SPAN // halves
    width = GROUP * sub
    gathered = []
    for h in range(halves):
        piece = jnp.transpose(rotated[h * sub:(h + 1) * sub, :GROUP, :], (2, 1, 0)).reshape(HD, width)
        if h == 0:
            piece = jnp.concatenate([piece, fresh.reshape(-1, width)], axis=0)
        gathered.append(lax.all_gather(piece[None], "req", axis=0, tiled=True))
    fresh_all = gathered[0][:, HD:, :].reshape(requests, SPAN, 2 * HD)

    my_slots = my_index * local_slots + jnp.arange(local_slots, dtype=jnp.int32)
    slot_req, page_index, cached = locate(my_slots, cache_pages, slot_order, new_pages)
    pages_out = write_pages(kv_pages, fresh_all, slot_req, page_index, cached, new_pages)

    perm = jnp.argsort(slot_req, stable=True).astype(jnp.int32)
    sreq = slot_req[perm].astype(jnp.int32)
    kstart = (page_index[perm] * page_rows).astype(jnp.int32)

    all_slots = jnp.arange(slot_order.shape[0], dtype=jnp.int32)
    all_req, unused_index, unused_cached = locate(all_slots, cache_pages, slot_order, new_pages)
    holds = (all_req.reshape(-1, local_slots) == my_index).any(axis=1)
    valid = holds[:, None, None]

    outs = []
    for h in range(halves):
        q_start = (query_start + h * sub).astype(jnp.int32)
        part_o, part_st = slot_attention(sreq, perm, kstart, q_start, gathered[h], pages_out, sub)
        hi = lax.reduce_precision(part_st, exponent_bits=8, mantissa_bits=7)
        rest = part_st - hi
        mid = lax.reduce_precision(rest, exponent_bits=8, mantissa_bits=7)
        lo = rest - mid
        sent = jnp.concatenate([part_o] + [t.astype(jnp.bfloat16) for t in (hi, mid, lo)], axis=1)
        got = lax.all_to_all(sent, "req", 0, 0, tiled=True)
        got_o = got[:, :HD].reshape(requests, HD, GROUP, sub)
        got_bits = got[:, HD:].reshape(requests, 3, 2, GROUP, sub).astype(jnp.float32)
        got_st = (got_bits[:, 0] + got_bits[:, 1]) + got_bits[:, 2]

        m_parts = jnp.where(valid, got_st[:, 0], NEG_BIG)
        l_parts = jnp.where(valid, got_st[:, 1], 0.0)
        top = jnp.max(m_parts, axis=0)
        w = l_parts * jnp.exp(m_parts - top[None])
        den = jnp.sum(w, axis=0)
        o_parts = jnp.where(valid[..., None], got_o.astype(jnp.float32), 0.0)
        num = jnp.sum(o_parts * w[:, None, :, :], axis=0)
        attention_t = (num / den[None]).astype(jnp.bfloat16)
        attention_flat = jnp.transpose(attention_t, (2, 1, 0)).reshape(sub, GROUP * HD)

        head_terms = jnp.dot(attention_flat, out_full, preferred_element_type=jnp.float32)
        outs.append(head_terms.astype(jnp.bfloat16))
    partial_t = jnp.concatenate(outs, axis=0)
    cols = partial_t.shape[1] // n_tp
    partial_t = jnp.moveaxis(partial_t.reshape(partial_t.shape[0], n_tp, cols), 1, 0)
    got_t = lax.all_to_all(partial_t, "tp", 0, 0, tiled=True)
    attention_out = jnp.sum(got_t.astype(jnp.float32), axis=0).astype(jnp.bfloat16)
    return (attention_out, pages_out)


def solution(mesh):
    return jax.shard_map(
        body,
        mesh=mesh,
        in_specs=(P("req", "tp"), P("req", "tp"), P("tp", "req"), P("req", None, "tp"), P(), P()),
        out_specs=(P("req", "tp"), P("req", None, "tp")),
        check_vma=False,
    )
```

```python
import math

import jax
import jax.numpy as jnp
from jax import lax
from jax.experimental import pallas as pl
from jax.experimental.pallas import tpu as pltpu
from jax.sharding import PartitionSpec as P

HD = 64
GROUP = 4
SPAN = 512


THETA = 1000000.0
NEG_BIG = -1e30


def rotary(values, positions):
    head_width = values.shape[-1]
    half_width = head_width // 2
    inv_freq = jnp.power(THETA, -(jnp.arange(half_width, dtype=jnp.float32) * 2.0 / head_width))
    angles = positions.astype(jnp.float32)[..., None] * inv_freq
    cosines = jnp.cos(angles)
    sines = jnp.sin(angles)
    lower_half = values[..., :half_width]
    upper_half = values[..., half_width:]
    return jnp.concatenate(
        [lower_half * cosines - upper_half * sines, upper_half * cosines + lower_half * sines],
        axis=-1,
    )


def locate(slot_ids, cache_pages, slot_order, new_pages):
    requests = cache_pages.shape[0]
    slot_count = slot_order.shape[0]
    counts = cache_pages + new_pages
    page_ends = jnp.cumsum(counts)
    starts = page_ends - counts
    ranking = jnp.sum(
        jnp.where(
            slot_order[None, :] == slot_ids[:, None],
            jnp.arange(slot_count, dtype=jnp.int32)[None, :],
            0,
        ),
        axis=1,
    )
    holder = jnp.sum((starts[None, :] <= ranking[:, None]).astype(jnp.int32), axis=1) - 1
    onehot = jnp.arange(requests, dtype=jnp.int32)[None, :] == holder[:, None]
    first_page = jnp.sum(jnp.where(onehot, starts[None, :], 0), axis=1)
    cached = jnp.sum(jnp.where(onehot, cache_pages[None, :], 0), axis=1)
    return (holder, ranking - first_page, cached)


def write_pages(kv_pages, fresh, slot_req, page_index, cached, new_pages):
    page_rows = kv_pages.shape[1]
    lane_width = kv_pages.shape[2]
    fresh_pages = fresh.reshape(-1, page_rows, lane_width)
    pick = slot_req * new_pages + jnp.clip(page_index - cached, 0, new_pages - 1)
    return jnp.where((page_index >= cached)[:, None, None], fresh_pages[pick], kv_pages)


def slot_attention(sreq, perm, kstart, qstart, packed, pages, sub, row_block=0):
    reqs, _, width = packed.shape
    slots, page_rows, _ = pages.shape
    assert width == GROUP * sub and sub & (sub - 1) == 0

    assert slots % 2 == 0

    def kernel(sreq_ref, perm_ref, kstart_ref, qstart_ref, q_ref, page_ref, o_ref, st_ref, m_sc, l_sc, acc_sc):
        j = pl.program_id(0)
        a = 2 * j
        b = a + 1
        req_a = sreq_ref[a]
        req_b = sreq_ref[b]
        first_a = jnp.logical_or(a == 0, sreq_ref[jnp.maximum(a - 1, 0)] != req_a)
        last_b = jnp.logical_or(b == slots - 1, sreq_ref[jnp.minimum(b + 1, slots - 1)] != req_b)
        same = req_a == req_b
        kst_a = kstart_ref[a]
        kst_b = kstart_ref[b]
        page_a = page_ref[perm_ref[a]]
        page_b = page_ref[perm_ref[b]]

        def init():
            m_sc[...] = jnp.full(m_sc.shape, NEG_BIG, jnp.float32)
            l_sc[...] = jnp.zeros(l_sc.shape, jnp.float32)
            acc_sc[...] = jnp.zeros(acc_sc.shape, jnp.float32)

        def finish(req):
            l_all = l_sc[...]
            safe = jnp.where(l_all > 0.0, l_all, 1.0)
            o_ref[req] = (acc_sc[...] / safe).astype(o_ref.dtype)
            st_ref[req, 0:1, :] = m_sc[...]
            st_ref[req, 1:2, :] = l_all

        def update(items, req, masked):
            q = q_ref[req]
            qst = qstart_ref[req]
            if masked:
                token = jnp.bitwise_and(lax.broadcasted_iota(jnp.int32, (page_rows, width), 1), sub - 1) + qst
                row = lax.broadcasted_iota(jnp.int32, (page_rows, width), 0)
            scores = []
            for page, kst in items:
                sc = jnp.dot(page[:, :HD], q, preferred_element_type=jnp.float32)
                vis = None
                if masked:
                    vis = row + kst <= token
                    sc = jnp.where(vis, sc, NEG_BIG)
                scores.append((sc, vis))
            m_prev = m_sc[...]
            m_cur = jnp.max(scores[0][0], axis=0, keepdims=True)
            for sc, vis in scores[1:]:
                m_cur = jnp.maximum(m_cur, jnp.max(sc, axis=0, keepdims=True))
            m_next = jnp.maximum(m_prev, m_cur)
            alpha = jnp.exp(m_prev - m_next)
            l_add = None
            pv = None
            for (sc, vis), (page, kst) in zip(scores, items):
                p = jnp.exp(sc - m_next)
                if masked:
                    p = jnp.where(vis, p, 0.0)
                part_l = jnp.sum(p, axis=0, keepdims=True)
                part_pv = lax.dot_general(
                    page[:, HD:], p.astype(jnp.bfloat16), (((0,), (0,)), ((), ())),
                    preferred_element_type=jnp.float32,
                )
                l_add = part_l if l_add is None else l_add + part_l
                pv = part_pv if pv is None else pv + part_pv
            l_sc[...] = alpha * l_sc[...] + l_add
            m_sc[...] = m_next
            acc_sc[...] = acc_sc[...] * alpha + pv

        partial_a = kst_a + (page_rows - 1) > qstart_ref[req_a]
        partial_b = kst_b + (page_rows - 1) > qstart_ref[req_b]
        pair = [(page_a, kst_a), (page_b, kst_b)]

        @pl.when(first_a)
        def _():
            init()

        @pl.when(jnp.logical_and(same, jnp.logical_or(partial_a, partial_b)))
        def _():
            update(pair, req_a, True)

        @pl.when(jnp.logical_and(same, jnp.logical_not(jnp.logical_or(partial_a, partial_b))))
        def _():
            update(pair, req_a, False)

        @pl.when(jnp.logical_not(same))
        def _():
            update(pair[:1], req_a, True)
            finish(req_a)
            init()
            update(pair[1:], req_b, True)

        @pl.when(last_b)
        def _():
            finish(req_b)

    grid_spec = pltpu.PrefetchScalarGridSpec(
        num_scalar_prefetch=4,
        grid=(slots // 2,),
        in_specs=[
            pl.BlockSpec((reqs, HD, width), lambda i, sr, pm, ks, qs: (0, row_block, 0)),
            pl.BlockSpec((slots, page_rows, 2 * HD), lambda i, sr, pm, ks, qs: (0, 0, 0)),
        ],
        out_specs=[
            pl.BlockSpec((reqs, HD, width), lambda i, sr, pm, ks, qs: (0, 0, 0)),
            pl.BlockSpec((reqs, 2, width), lambda i, sr, pm, ks, qs: (0, 0, 0)),
        ],
        scratch_shapes=[
            pltpu.VMEM((1, width), jnp.float32),
            pltpu.VMEM((1, width), jnp.float32),
            pltpu.VMEM((HD, width), jnp.float32),
        ],
    )
    return pl.pallas_call(
        kernel,
        grid_spec=grid_spec,
        out_shape=[
            jax.ShapeDtypeStruct((reqs, HD, width), jnp.bfloat16),
            jax.ShapeDtypeStruct((reqs, 2, width), jnp.float32),
        ],
        compiler_params=pltpu.CompilerParams(
            dimension_semantics=("arbitrary",), vmem_limit_bytes=48 * 1024 * 1024
        ),
    )(sreq, perm, kstart, qstart, packed, pages)


def body(hidden, qkv_weight, out_weight, kv_pages, cache_pages, slot_order):
    n_tp = lax.axis_size("tp")
    whole = lax.all_gather(hidden, "tp", axis=1, tiled=True)
    tok_rows = whole.shape[0]
    n_req = lax.axis_size("req")
    lanes = out_weight.shape[1]
    qkv_rows = qkv_weight.size // lanes
    both = jnp.concatenate([qkv_weight.reshape(qkv_rows, lanes), out_weight], axis=0)
    both = lax.all_to_all(jnp.broadcast_to(both[None], (n_req,) + both.shape), "req", 0, 0, tiled=True)
    qkv_full = both[:, :qkv_rows].reshape(n_req * qkv_weight.shape[0], qkv_weight.shape[1])
    out_full = jnp.moveaxis(both[:, qkv_rows:], 0, 1).reshape(out_weight.shape[0], n_req * lanes)
    projected = jnp.dot(whole, qkv_full, preferred_element_type=jnp.float32)
    local_slots = kv_pages.shape[0]
    page_rows = kv_pages.shape[1]
    lane_width = kv_pages.shape[2]
    kv_heads = lane_width // (2 * HD)
    assert kv_heads == 1 and tok_rows == SPAN
    new_pages = SPAN // page_rows
    requests = cache_pages.shape[0]
    my_index = lax.axis_index("req")
    query_start = cache_pages * page_rows
    home_start = lax.dynamic_slice_in_dim(query_start, my_index, 1, 0)
    projected = projected.reshape(SPAN, GROUP + 2, HD)
    positions = (home_start + jnp.arange(SPAN, dtype=jnp.int32))[:, None]
    rotated = rotary(projected[:, : GROUP + 1, :], positions)
    scale = jnp.concatenate(
        [jnp.full((GROUP, 1), 1.0 / math.sqrt(HD), jnp.float32), jnp.ones((1, 1), jnp.float32)], axis=0
    )
    rotated = (rotated * scale).astype(jnp.bfloat16)
    value_new = projected[:, GROUP + 1 :, :].astype(jnp.bfloat16)
    fresh = jnp.concatenate([rotated[:, GROUP:, :], value_new], axis=1)
    halves = 2
    sub = SPAN // halves
    width = GROUP * sub
    pieces = []
    for h in range(halves):
        pieces.append(jnp.transpose(rotated[h * sub:(h + 1) * sub, :GROUP, :], (2, 1, 0)).reshape(HD, width))
        if h == 0:
            pieces.append(fresh.reshape(-1, width))
    packed_all = lax.all_gather(jnp.concatenate(pieces, axis=0)[None], "req", axis=0, tiled=True)
    fresh_all = packed_all[:, HD:2 * HD, :].reshape(requests, SPAN, 2 * HD)

    my_slots = my_index * local_slots + jnp.arange(local_slots, dtype=jnp.int32)
    slot_req, page_index, cached = locate(my_slots, cache_pages, slot_order, new_pages)
    pages_out = write_pages(kv_pages, fresh_all, slot_req, page_index, cached, new_pages)

    perm = jnp.argsort(slot_req, stable=True).astype(jnp.int32)
    sreq = slot_req[perm].astype(jnp.int32)
    kstart = (page_index[perm] * page_rows).astype(jnp.int32)

    all_slots = jnp.arange(slot_order.shape[0], dtype=jnp.int32)
    all_req, unused_index, unused_cached = locate(all_slots, cache_pages, slot_order, new_pages)
    holds = (all_req.reshape(-1, local_slots) == my_index).any(axis=1)
    valid = holds[:, None, None]

    outs = []
    for h in range(halves):
        q_start = (query_start + h * sub).astype(jnp.int32)
        part_o, part_st = slot_attention(
            sreq, perm, kstart, q_start, packed_all, pages_out, sub, row_block=0 if h == 0 else h + 1
        )
        hi = lax.reduce_precision(part_st, exponent_bits=8, mantissa_bits=7)
        rest = part_st - hi
        mid = lax.reduce_precision(rest, exponent_bits=8, mantissa_bits=7)
        lo = rest - mid
        sent = jnp.concatenate([part_o] + [t.astype(jnp.bfloat16) for t in (hi, mid, lo)], axis=1)
        got = lax.all_to_all(sent, "req", 0, 0, tiled=True)
        got_o = got[:, :HD].reshape(requests, HD, GROUP, sub)
        got_bits = got[:, HD:].reshape(requests, 3, 2, GROUP, sub).astype(jnp.float32)
        got_st = (got_bits[:, 0] + got_bits[:, 1]) + got_bits[:, 2]

        m_parts = jnp.where(valid, got_st[:, 0], NEG_BIG)
        l_parts = jnp.where(valid, got_st[:, 1], 0.0)
        top = jnp.max(m_parts, axis=0)
        w = l_parts * jnp.exp(m_parts - top[None])
        den = jnp.sum(w, axis=0)
        o_parts = jnp.where(valid[..., None], got_o.astype(jnp.float32), 0.0)
        num = jnp.sum(o_parts * w[:, None, :, :], axis=0)
        attention_t = (num / den[None]).astype(jnp.bfloat16)
        attention_flat = jnp.transpose(attention_t, (2, 1, 0)).reshape(sub, GROUP * HD)

        head_terms = jnp.dot(attention_flat, out_full, preferred_element_type=jnp.float32)
        outs.append(head_terms.astype(jnp.bfloat16))
    partial_t = jnp.concatenate(outs, axis=0)
    cols = partial_t.shape[1] // n_tp
    partial_t = jnp.moveaxis(partial_t.reshape(partial_t.shape[0], n_tp, cols), 1, 0)
    got_t = lax.all_to_all(partial_t, "tp", 0, 0, tiled=True)
    attention_out = jnp.sum(got_t.astype(jnp.float32), axis=0).astype(jnp.bfloat16)
    return (attention_out, pages_out)


def solution(mesh):
    return jax.shard_map(
        body,
        mesh=mesh,
        in_specs=(P("req", "tp"), P("req", "tp"), P("tp", "req"), P("req", None, "tp"), P(), P()),
        out_specs=(P("req", "tp"), P("req", None, "tp")),
        check_vma=False,
    )
```

```python
import math

import jax
import jax.numpy as jnp
from jax import lax
from jax.experimental import pallas as pl
from jax.experimental.pallas import tpu as pltpu
from jax.sharding import PartitionSpec as P

HD = 64
GROUP = 4
SPAN = 512


THETA = 1000000.0
NEG_BIG = -1e30


def rotary(values, positions):
    head_width = values.shape[-1]
    half_width = head_width // 2
    inv_freq = jnp.power(THETA, -(jnp.arange(half_width, dtype=jnp.float32) * 2.0 / head_width))
    angles = positions.astype(jnp.float32)[..., None] * inv_freq
    cosines = jnp.cos(angles)
    sines = jnp.sin(angles)
    lower_half = values[..., :half_width]
    upper_half = values[..., half_width:]
    return jnp.concatenate(
        [lower_half * cosines - upper_half * sines, upper_half * cosines + lower_half * sines],
        axis=-1,
    )


def locate(slot_ids, cache_pages, slot_order, new_pages):
    requests = cache_pages.shape[0]
    slot_count = slot_order.shape[0]
    counts = cache_pages + new_pages
    page_ends = jnp.cumsum(counts)
    starts = page_ends - counts
    ranking = jnp.sum(
        jnp.where(
            slot_order[None, :] == slot_ids[:, None],
            jnp.arange(slot_count, dtype=jnp.int32)[None, :],
            0,
        ),
        axis=1,
    )
    holder = jnp.sum((starts[None, :] <= ranking[:, None]).astype(jnp.int32), axis=1) - 1
    onehot = jnp.arange(requests, dtype=jnp.int32)[None, :] == holder[:, None]
    first_page = jnp.sum(jnp.where(onehot, starts[None, :], 0), axis=1)
    cached = jnp.sum(jnp.where(onehot, cache_pages[None, :], 0), axis=1)
    return (holder, ranking - first_page, cached)


def write_pages(kv_pages, fresh, slot_req, page_index, cached, new_pages):
    page_rows = kv_pages.shape[1]
    lane_width = kv_pages.shape[2]
    fresh_pages = fresh.reshape(-1, page_rows, lane_width)
    pick = slot_req * new_pages + jnp.clip(page_index - cached, 0, new_pages - 1)
    return jnp.where((page_index >= cached)[:, None, None], fresh_pages[pick], kv_pages)


def slot_attention(sreq, perm, kstart, qstart, packed, pages, sub):
    reqs, _, width = packed.shape
    slots, page_rows, _ = pages.shape
    assert width == GROUP * sub and sub & (sub - 1) == 0

    assert slots % 2 == 0

    def kernel(sreq_ref, perm_ref, kstart_ref, qstart_ref, q_ref, page_ref, o_ref, st_ref, m_sc, l_sc, acc_sc):
        j = pl.program_id(0)
        a = 2 * j
        b = a + 1
        req_a = sreq_ref[a]
        req_b = sreq_ref[b]
        first_a = jnp.logical_or(a == 0, sreq_ref[jnp.maximum(a - 1, 0)] != req_a)
        last_b = jnp.logical_or(b == slots - 1, sreq_ref[jnp.minimum(b + 1, slots - 1)] != req_b)
        same = req_a == req_b
        kst_a = kstart_ref[a]
        kst_b = kstart_ref[b]
        page_a = page_ref[perm_ref[a]]
        page_b = page_ref[perm_ref[b]]

        def init():
            m_sc[...] = jnp.full(m_sc.shape, NEG_BIG, jnp.float32)
            l_sc[...] = jnp.zeros(l_sc.shape, jnp.float32)
            acc_sc[...] = jnp.zeros(acc_sc.shape, jnp.float32)

        def finish(req):
            l_all = l_sc[...]
            safe = jnp.where(l_all > 0.0, l_all, 1.0)
            o_ref[req] = (acc_sc[...] / safe).astype(o_ref.dtype)
            st_ref[req, 0:1, :] = m_sc[...]
            st_ref[req, 1:2, :] = l_all

        def update(items, req, masked):
            q = q_ref[req]
            qst = qstart_ref[req]
            if masked:
                token = jnp.bitwise_and(lax.broadcasted_iota(jnp.int32, (page_rows, width), 1), sub - 1) + qst
                row = lax.broadcasted_iota(jnp.int32, (page_rows, width), 0)
            scores = []
            for page, kst in items:
                sc = jnp.dot(page[:, :HD], q, preferred_element_type=jnp.float32)
                vis = None
                if masked:
                    vis = row + kst <= token
                    sc = jnp.where(vis, sc, NEG_BIG)
                scores.append((sc, vis))
            m_prev = m_sc[...]
            m_cur = jnp.max(scores[0][0], axis=0, keepdims=True)
            for sc, vis in scores[1:]:
                m_cur = jnp.maximum(m_cur, jnp.max(sc, axis=0, keepdims=True))
            m_next = jnp.maximum(m_prev, m_cur)
            alpha = jnp.exp(m_prev - m_next)
            l_add = None
            pv = None
            for (sc, vis), (page, kst) in zip(scores, items):
                p = jnp.exp(sc - m_next)
                if masked:
                    p = jnp.where(vis, p, 0.0)
                part_l = jnp.sum(p, axis=0, keepdims=True)
                part_pv = lax.dot_general(
                    page[:, HD:], p.astype(jnp.bfloat16), (((0,), (0,)), ((), ())),
                    preferred_element_type=jnp.float32,
                )
                l_add = part_l if l_add is None else l_add + part_l
                pv = part_pv if pv is None else pv + part_pv
            l_sc[...] = alpha * l_sc[...] + l_add
            m_sc[...] = m_next
            acc_sc[...] = acc_sc[...] * alpha + pv

        partial_a = kst_a + (page_rows - 1) > qstart_ref[req_a]
        partial_b = kst_b + (page_rows - 1) > qstart_ref[req_b]
        pair = [(page_a, kst_a), (page_b, kst_b)]

        @pl.when(first_a)
        def _():
            init()

        @pl.when(jnp.logical_and(same, jnp.logical_or(partial_a, partial_b)))
        def _():
            update(pair, req_a, True)

        @pl.when(jnp.logical_and(same, jnp.logical_not(jnp.logical_or(partial_a, partial_b))))
        def _():
            update(pair, req_a, False)

        @pl.when(jnp.logical_not(same))
        def _():
            update(pair[:1], req_a, True)
            finish(req_a)
            init()
            update(pair[1:], req_b, True)

        @pl.when(last_b)
        def _():
            finish(req_b)

    grid_spec = pltpu.PrefetchScalarGridSpec(
        num_scalar_prefetch=4,
        grid=(slots // 2,),
        in_specs=[
            pl.BlockSpec((reqs, HD, width), lambda i, sr, pm, ks, qs: (0, 0, 0)),
            pl.BlockSpec((slots, page_rows, 2 * HD), lambda i, sr, pm, ks, qs: (0, 0, 0)),
        ],
        out_specs=[
            pl.BlockSpec((reqs, HD, width), lambda i, sr, pm, ks, qs: (0, 0, 0)),
            pl.BlockSpec((reqs, 2, width), lambda i, sr, pm, ks, qs: (0, 0, 0)),
        ],
        scratch_shapes=[
            pltpu.VMEM((1, width), jnp.float32),
            pltpu.VMEM((1, width), jnp.float32),
            pltpu.VMEM((HD, width), jnp.float32),
        ],
    )
    return pl.pallas_call(
        kernel,
        grid_spec=grid_spec,
        out_shape=[
            jax.ShapeDtypeStruct((reqs, HD, width), jnp.bfloat16),
            jax.ShapeDtypeStruct((reqs, 2, width), jnp.float32),
        ],
        compiler_params=pltpu.CompilerParams(
            dimension_semantics=("arbitrary",), vmem_limit_bytes=48 * 1024 * 1024
        ),
    )(sreq, perm, kstart, qstart, packed, pages)


def body(hidden, qkv_weight, out_weight, kv_pages, cache_pages, slot_order):
    n_tp = lax.axis_size("tp")
    whole = lax.all_gather(hidden, "tp", axis=1, tiled=True)
    tok_rows = whole.shape[0]
    n_req = lax.axis_size("req")
    lanes = out_weight.shape[1]
    qkv_rows = qkv_weight.size // lanes
    both = jnp.concatenate([qkv_weight.reshape(qkv_rows, lanes), out_weight], axis=0)
    both = lax.all_to_all(jnp.broadcast_to(both[None], (n_req,) + both.shape), "req", 0, 0, tiled=True)
    qkv_full = both[:, :qkv_rows].reshape(n_req * qkv_weight.shape[0], qkv_weight.shape[1])
    out_full = jnp.moveaxis(both[:, qkv_rows:], 0, 1).reshape(out_weight.shape[0], n_req * lanes)
    projected = jnp.dot(whole, qkv_full, preferred_element_type=jnp.float32)
    local_slots = kv_pages.shape[0]
    page_rows = kv_pages.shape[1]
    lane_width = kv_pages.shape[2]
    kv_heads = lane_width // (2 * HD)
    assert kv_heads == 1 and tok_rows == SPAN
    new_pages = SPAN // page_rows
    requests = cache_pages.shape[0]
    my_index = lax.axis_index("req")
    query_start = cache_pages * page_rows
    home_start = lax.dynamic_slice_in_dim(query_start, my_index, 1, 0)
    projected = projected.reshape(SPAN, GROUP + 2, HD)
    positions = (home_start + jnp.arange(SPAN, dtype=jnp.int32))[:, None]
    rotated = rotary(projected[:, : GROUP + 1, :], positions)
    scale = jnp.concatenate(
        [jnp.full((GROUP, 1), 1.0 / math.sqrt(HD), jnp.float32), jnp.ones((1, 1), jnp.float32)], axis=0
    )
    rotated = (rotated * scale).astype(jnp.bfloat16)
    value_new = projected[:, GROUP + 1 :, :].astype(jnp.bfloat16)
    fresh = jnp.concatenate([rotated[:, GROUP:, :], value_new], axis=1)
    halves = 2
    sub = SPAN // halves
    width = GROUP * sub
    gathered = []
    for h in range(halves):
        piece = jnp.transpose(rotated[h * sub:(h + 1) * sub, :GROUP, :], (2, 1, 0)).reshape(HD, width)
        if h == 0:
            piece = jnp.concatenate([piece, fresh.reshape(-1, width)], axis=0)
        gathered.append(lax.all_gather(piece[None], "req", axis=0, tiled=True))
    fresh_all = gathered[0][:, HD:, :].reshape(requests, SPAN, 2 * HD)

    my_slots = my_index * local_slots + jnp.arange(local_slots, dtype=jnp.int32)
    slot_req, page_index, cached = locate(my_slots, cache_pages, slot_order, new_pages)
    pages_out = write_pages(kv_pages, fresh_all, slot_req, page_index, cached, new_pages)

    perm = jnp.argsort(slot_req, stable=True).astype(jnp.int32)
    sreq = slot_req[perm].astype(jnp.int32)
    kstart = (page_index[perm] * page_rows).astype(jnp.int32)

    all_slots = jnp.arange(slot_order.shape[0], dtype=jnp.int32)
    all_req, unused_index, unused_cached = locate(all_slots, cache_pages, slot_order, new_pages)
    holds = (all_req.reshape(-1, local_slots) == my_index).any(axis=1)
    valid = holds[:, None, None]

    outs = []
    for h in range(halves):
        q_start = (query_start + h * sub).astype(jnp.int32)
        part_o, part_st = slot_attention(sreq, perm, kstart, q_start, gathered[h], pages_out, sub)
        hi = lax.reduce_precision(part_st, exponent_bits=8, mantissa_bits=7)
        rest = part_st - hi
        mid = lax.reduce_precision(rest, exponent_bits=8, mantissa_bits=7)
        lo = rest - mid
        sent = jnp.concatenate([part_o] + [t.astype(jnp.bfloat16) for t in (hi, mid, lo)], axis=1)
        got = lax.all_to_all(sent, "req", 0, 0, tiled=True)
        got_o = got[:, :HD]
        got_bits = got[:, HD:].reshape(requests, 3, 2, width).astype(jnp.float32)
        got_st = (got_bits[:, 0] + got_bits[:, 1]) + got_bits[:, 2]

        valid_row = holds[:, None]
        m_parts = jnp.where(valid_row, got_st[:, 0], NEG_BIG)
        l_parts = jnp.where(valid_row, got_st[:, 1], 0.0)
        top = jnp.max(m_parts, axis=0)
        w = l_parts * jnp.exp(m_parts - top[None])
        den = jnp.sum(w, axis=0)
        o_parts = jnp.where(valid, got_o.astype(jnp.float32), 0.0)
        num = jnp.sum(o_parts * w[:, None, :], axis=0)
        attention_t = (num / den[None]).astype(jnp.bfloat16).reshape(HD, GROUP, sub)
        attention_flat = jnp.transpose(attention_t, (2, 1, 0)).reshape(sub, GROUP * HD)

        head_terms = jnp.dot(attention_flat, out_full, preferred_element_type=jnp.float32)
        outs.append(head_terms.astype(jnp.bfloat16))
    partial_t = jnp.concatenate(outs, axis=0)
    cols = partial_t.shape[1] // n_tp
    partial_t = jnp.moveaxis(partial_t.reshape(partial_t.shape[0], n_tp, cols), 1, 0)
    got_t = lax.all_to_all(partial_t, "tp", 0, 0, tiled=True)
    attention_out = jnp.sum(got_t.astype(jnp.float32), axis=0).astype(jnp.bfloat16)
    return (attention_out, pages_out)


def solution(mesh):
    return jax.shard_map(
        body,
        mesh=mesh,
        in_specs=(P("req", "tp"), P("req", "tp"), P("tp", "req"), P("req", None, "tp"), P(), P()),
        out_specs=(P("req", "tp"), P("req", None, "tp")),
        check_vma=False,
    )
```
